256 devices in a mesh: frame: 8 (over x, core), pixel: 32 (over y, z).
Axes of the slice: x: 4, y: 4, z: 8, core: 2. Of those that a mesh axis runs over, the one named last changes fastest.
Arguments:
- frames: bfloat16 [1024, 131072], P('frame', 'pixel'), may hold values from -6 to 6
- dead_time: float32 [131072], P('pixel'), may hold values from 0.002 to 0.02
- band_width: int32 [131072], P('pixel'), may hold values from 0 to 8
- cycle_label: int32 [131072], P('pixel'), may hold values from 0 to 1, as said below
- valid: int32 [131072], P('pixel'), may hold values from 0 to 1
Outputs:
- two_time: float32 [1024, 2, 1024], P(('frame', 'pixel'))
The draws below stay inside these ranges and needn't reach their ends.
Inputs may be any that keep to these rules, and one draw needn't show every extreme that they name: `cycle_label`: every cycle holds at least one pixel with valid 1.
All inputs are finite; a program needn't handle non-finite values.
Results may differ from the reference program's by a relative error of at most 0.004.
Values may be sent and summed in bfloat16 or wider, within the bound.
A program may use at most 64 MiB of HBM per device.

```python
import math
import jax
import jax.numpy as jnp
from jax import lax

NFRAMES = 1024
CYCLES = 2
BAND = 8
NPIX = 131072


def draw_cycle_label(key, part):
    first = jax.random.randint(jax.random.fold_in(key, 11), (NPIX,), 0, CYCLES)
    second = jax.random.randint(jax.random.fold_in(key, 12), (NPIX,), 0, CYCLES)
    labels = jnp.minimum(first, second)
    position = jnp.arange(NPIX, dtype=jnp.int32)
    return jnp.where(position < CYCLES, position, labels).astype(jnp.int32)


def draw_valid(key, part):
    drawn = jax.random.randint(jax.random.fold_in(key, 21), (NPIX,), 0, 8)
    position = jnp.arange(NPIX, dtype=jnp.int32)
    return jnp.where((drawn < 7) | (position < CYCLES), 1, 0).astype(jnp.int32)


def set_ends(entries, stream_key, low, high):
    extent = entries.shape
    index_at = [jax.random.randint(jax.random.fold_in(stream_key, axis), (), 0, extent[axis]) for axis in range(len(extent))]
    entries = entries.at[tuple(index_at)].set(low)
    longest = extent.index(max(extent))
    index_at[longest] = (index_at[longest] + 1) % extent[longest]
    return entries.at[tuple(index_at)].set(high)


def with_spikes(values, stream_key, source, target, blocks, factor):
    owner, partner = [(jnp.arange(values.shape[axis_at]) // (values.shape[axis_at] // blocks)).reshape([-1 if axis == axis_at else 1 for axis in range(values.ndim)]) for axis_at in (source, target)]
    chosen = jax.random.permutation(stream_key, blocks)[partner]
    strong = (owner == chosen) | (owner == (partner + blocks // 2) % blocks)
    return jnp.where(strong, factor * values, values)


def level_of(key, shape, split, smallest, top_value):
    def one(dim, blocks):
        heights = jax.random.uniform(jax.random.fold_in(jax.random.fold_in(key, 6), dim), (blocks,), jnp.float32, smallest / len(split), top_value / len(split))
        return jnp.repeat(jnp.exp(heights), shape[dim] // blocks).reshape((-1,) + (1,) * (len(shape) - dim - 1))

    level = one(*split[0])
    for cut in split[1:]:
        level = level * one(*cut)
    return level


def noise_with(key, shape, scale, most, split, heavy, held_as=jnp.bfloat16):
    result = scale * jax.random.normal(key, shape, jnp.float32)
    if split:
        result = result * level_of(key, shape, split, -0.22, 0.18)
    return jnp.clip(with_spikes(result, jax.random.fold_in(key, 3), *heavy), -most, most).astype(held_as)


def setup_inputs(seed: int = 0) -> dict:
    splits = jax.random.split(jax.random.key(seed), 6)
    return {
        "frames": noise_with(splits[0], (NFRAMES, NPIX), 1.0, 6.0, ((0, 8), (1, 32)), (1, 0, 32, 2.75)),
        "dead_time": jnp.clip(jnp.exp(math.log(0.02) - 2.30258502 * jax.random.uniform(splits[1], (NPIX,), jnp.float32) ** level_of(splits[1], (NPIX,), ((0, 32),), -0.2, 0.2)), 0.002, 0.02),
        "band_width": set_ends(jax.random.randint(splits[2], (NPIX,), 0, BAND + 1), jax.random.fold_in(splits[2], 1), 0, BAND).astype(jnp.int32),
        "cycle_label": draw_cycle_label(jax.random.fold_in(splits[5], 71), 0),
        "valid": draw_valid(jax.random.fold_in(splits[5], 71), 0),
    }


def smooth_block(frame_block, dead_block, width_block):
    count_rate = 4.0 + frame_block.astype(jnp.float32)
    corrected = count_rate / (1.0 - dead_block[None, :] * count_rate)
    running = jnp.concatenate([jnp.zeros((1, corrected.shape[1]), jnp.float32), jnp.cumsum(corrected, axis=0)], axis=0)
    frame_idx = jnp.arange(NFRAMES, dtype=jnp.int32)[:, None]
    upper_end = jnp.minimum(frame_idx + width_block[None, :], NFRAMES - 1)
    lower_end = jnp.maximum(frame_idx - width_block[None, :], 0)
    total = jnp.take_along_axis(running, upper_end + 1, axis=0) - jnp.take_along_axis(running, lower_end, axis=0)
    return (total / (upper_end - lower_end + 1).astype(jnp.float32)).astype(jnp.bfloat16)


def reference(frames, dead_time, band_width, cycle_label, valid):
    npix_all = frames.shape[1]
    block = math.gcd(npix_all, 4096)
    nblocks = npix_all // block
    cycle_ids = jnp.arange(CYCLES, dtype=jnp.int32)[:, None]

    def step(index, carry):
        gram, cycle_sum, counts = carry
        begin = (index * block).astype(jnp.int32)
        frame_block = lax.dynamic_slice_in_dim(frames, begin, block, 1)
        dead_block = lax.dynamic_slice_in_dim(dead_time, begin, block, 0)
        width_block = lax.dynamic_slice_in_dim(band_width, begin, block, 0)
        label_block = lax.dynamic_slice_in_dim(cycle_label, begin, block, 0)
        valid_block = lax.dynamic_slice_in_dim(valid, begin, block, 0)
        smoothed = smooth_block(frame_block, dead_block, width_block)
        member = ((label_block[None, :] == cycle_ids) & (valid_block[None, :] == 1)).astype(jnp.bfloat16)
        counts = counts + jnp.sum(member.astype(jnp.float32), axis=1)
        cycle_sum = cycle_sum + lax.dot_general(smoothed, member, (((1,), (1,)), ((), ())), preferred_element_type=jnp.float32)
        weighted = (smoothed[:, None, :] * member[None, :, :]).reshape(NFRAMES * CYCLES, block)
        product = lax.dot_general(weighted, smoothed, (((1,), (1,)), ((), ())), preferred_element_type=jnp.float32)
        gram = gram + product.reshape(NFRAMES, CYCLES, NFRAMES)
        return gram, cycle_sum, counts

    start = (jnp.zeros((NFRAMES, CYCLES, NFRAMES), jnp.float32), jnp.zeros((NFRAMES, CYCLES), jnp.float32), jnp.zeros((CYCLES,), jnp.float32))
    gram, cycle_sum, counts = lax.fori_loop(0, nblocks, step, start)
    mean = cycle_sum / counts[None, :]
    return gram / counts[None, :, None] - mean[:, :, None] * jnp.transpose(mean)[None, :, :]
```

```python
import functools

import jax
import jax.numpy as jnp
from jax import lax
from jax.experimental import pallas as pl
from jax.experimental.pallas import tpu as pltpu
from jax.sharding import PartitionSpec as P

MESH = pl.DeviceIdType.MESH
CYCLES = 2
BAND = 8
CORES = 2
NX = 4
NY = 4
NZ = 8
LANES = 128
GROUP = 32
NFRAMES = 1024
NDEV_FRAME = NX * CORES
OWN_FRAMES = NFRAMES // NDEV_FRAME
NPIX_GROUP = 4096
OWN_PIX = NPIX_GROUP // NDEV_FRAME
CHUNKS = OWN_PIX // LANES
CHIP_PIX = CORES * OWN_PIX
CLASS_ROWS = NFRAMES // 4
SUB_ROWS = CLASS_ROWS // 4
PAD = BAND
TILE = 256


def remote(src, dst, send_sem, recv_sem, device):
    return pltpu.make_async_remote_copy(
        src_ref=src,
        dst_ref=dst,
        send_sem=send_sem,
        recv_sem=recv_sem,
        device_id=device,
        device_id_type=MESH,
    )


def kernel(
    frames, dead_hbm, band_hbm, label_hbm, valid_hbm,
    out,
    dead, band, label, valid, arrived, rate, smooth, outgoing,
    lhs, gsend, grecv, gown, hsend, hrecv, hown, tsend, trecv,
    stat1, stat2, stat3, statg2, statg3, spread, spread_t,
    fsend, frecv,
    par_sem, own_sem, a2a_send, a2a_recv, sib_send, sib_recv,
    s1_send, s1_recv, s2_send, s2_recv, s3_send, s3_recv,
    g_send, g_recv, h_send, h_recv, t_send, t_recv, f_send, f_recv,
):
    f = lax.axis_index("frame")
    p = lax.axis_index("pixel")
    x, c = f // CORES, f % CORES
    y, z = p // NZ, p % NZ
    a1 = c * x + (1 - c) * y
    a2 = c * y + (1 - c) * x

    def first_peer(a):
        return ((c * a + (1 - c) * x) * CORES + c, (c * y + (1 - c) * a) * NZ + z)

    def second_peer(a):
        return ((c * x + (1 - c) * a) * CORES + c, (c * a + (1 - c) * y) * NZ + z)

    def z_peer(other):
        return (f, y * NZ + other)

    def frame_peer(other):
        return (other, p)

    sibling = (x * CORES + (1 - c), p)

    barrier = pltpu.get_barrier_semaphore()
    for k in range(1, NDEV_FRAME):
        pl.semaphore_signal(barrier, inc=1, device_id=frame_peer((f + k) % NDEV_FRAME), device_id_type=MESH)
    for k in range(1, NY):
        pl.semaphore_signal(barrier, inc=1, device_id=(f, ((y + k) % NY) * NZ + z), device_id_type=MESH)
    for k in range(1, NZ):
        pl.semaphore_signal(barrier, inc=1, device_id=z_peer((z + k) % NZ), device_id_type=MESH)
    pl.semaphore_wait(barrier, NDEV_FRAME - 1 + NY - 1 + NZ - 1)

    def piece(owner, chunk):
        return frames.at[:, pl.ds(pl.multiple_of(owner * OWN_PIX + chunk * LANES, LANES), LANES)]

    def a2a_copy(k, chunk):
        to = (f + k) % NDEV_FRAME
        return remote(
            piece(to, chunk), arrived.at[chunk, f], a2a_send.at[chunk, k], a2a_recv.at[chunk, f], frame_peer(to)
        )

    def own_copy(chunk):
        return pltpu.make_async_copy(piece(f, chunk), arrived.at[chunk, f], own_sem.at[chunk])

    for chunk in range(CHUNKS):
        for k in range(1, NDEV_FRAME):
            a2a_copy(k, chunk).start()
        own_copy(chunk).start()
    params = [
        pltpu.make_async_copy(src, dst, par_sem.at[n])
        for n, (src, dst) in enumerate(
            ((dead_hbm, dead), (band_hbm, band), (label_hbm, label), (valid_hbm, valid))
        )
    ]
    for copy in params:
        copy.start()
    rate[0:PAD, :] = jnp.zeros((PAD, LANES), jnp.float32)
    rate[PAD + NFRAMES : PAD + NFRAMES + PAD, :] = jnp.zeros((PAD, LANES), jnp.float32)
    for copy in params:
        copy.wait()

    def sib_copy(chunk):
        return remote(
            outgoing.at[chunk],
            smooth.at[:, pl.ds(OWN_PIX + chunk * LANES, LANES)],
            sib_send.at[chunk],
            sib_recv.at[chunk],
            sibling,
        )

    for chunk in range(CHUNKS):
        own_copy(chunk).wait()
        for k in range(1, NDEV_FRAME):
            source = (f + k) % NDEV_FRAME
            remote(
                piece(source, chunk), arrived.at[chunk, source], a2a_send.at[chunk, k],
                a2a_recv.at[chunk, source], frame_peer(source),
            ).wait_recv()
        row = f * CHUNKS + chunk
        dead_row = dead[pl.ds(row, 1), :]
        width = band[pl.ds(row, 1), :]
        cycle = label[pl.ds(row, 1), :]
        used = valid[pl.ds(row, 1), :] == 1
        mine = jnp.where(used & (cycle == c), 1.0, 0.0)
        other = jnp.where(used & (cycle == 1 - c), 1.0, 0.0)
        within = [jnp.where(width >= k, 1.0, 0.0) for k in range(1, BAND + 1)]
        full = 1.0 / (2 * width + 1).astype(jnp.float32)

        def correct(block, _):
            for half in range(OWN_FRAMES // GROUP):
                count = 4.0 + arrived[chunk, block, half * GROUP : (half + 1) * GROUP, :].astype(jnp.float32)
                rate[pl.ds(pl.multiple_of(PAD + block * OWN_FRAMES + half * GROUP, 8), GROUP), :] = count / (
                    1.0 - dead_row * count
                )
            return 0

        lax.fori_loop(0, NDEV_FRAME, correct, 0)

        def window(start):
            total = rate[pl.ds(start + PAD, GROUP), :]
            for k in range(1, BAND + 1):
                total = total + within[k - 1] * (
                    rate[pl.ds(start + PAD - k, GROUP), :] + rate[pl.ds(start + PAD + k, GROUP), :]
                )
            return total

        def put(start, value):
            rows = pl.ds(start, GROUP)
            smooth[rows, chunk * LANES : (chunk + 1) * LANES] = (value * mine).astype(jnp.bfloat16)
            outgoing[chunk, rows, :] = (value * other).astype(jnp.bfloat16)

        def inside(block, _):
            start = pl.multiple_of(block * GROUP, GROUP)
            put(start, window(start) * full)
            return 0

        for start in (0, NFRAMES - GROUP):
            frame = start + lax.broadcasted_iota(jnp.int32, (GROUP, LANES), 0)
            span = jnp.minimum(frame + width, NFRAMES - 1) - jnp.maximum(frame - width, 0) + 1
            put(start, window(start) / span.astype(jnp.float32))
        lax.fori_loop(1, NFRAMES // GROUP - 1, inside, 0)
        sib_copy(chunk).start()

    chip_label = label[pl.ds(pl.multiple_of(x * (CHIP_PIX // LANES), 8), CHIP_PIX // LANES), :]
    chip_valid = valid[pl.ds(pl.multiple_of(x * (CHIP_PIX // LANES), 8), CHIP_PIX // LANES), :]
    held = jnp.sum(jnp.where((chip_label == c) & (chip_valid == 1), 1.0, 0.0), axis=(0, 1), keepdims=True)

    for chunk in range(CHUNKS):
        sib_copy(chunk).wait_recv()

    contract_last = (((1,), (1,)), ((), ()))
    sums = lax.dot_general(
        jnp.ones((8, CHIP_PIX), jnp.bfloat16), smooth[...], contract_last, preferred_element_type=jnp.float32
    )[0:1, :]
    stat1[a1, 0:1, :] = sums
    stat1[a1, 1:2, :] = jnp.broadcast_to(held, (1, NFRAMES))

    def stat1_copy(k):
        to = (a1 + k) % 4
        return remote(stat1.at[a1], stat1.at[a1], s1_send.at[k], s1_recv.at[a1], first_peer(to))

    for k in range(1, 4):
        stat1_copy(k).start()

    def group_start(a, g):
        second, core = g // CORES, g % CORES
        row_x = c * a + (1 - c) * second
        row_y = c * second + (1 - c) * a
        return pl.multiple_of((row_x * 8 + core * 4 + row_y) * GROUP, GROUP)

    def g_copy(k, sub):
        to = (a1 + k) % 4
        rows = pl.ds(pl.multiple_of(sub * SUB_ROWS, SUB_ROWS), SUB_ROWS)
        return remote(
            gsend.at[to, rows, :], grecv.at[a1, rows, :], g_send.at[k, sub], g_recv.at[a1, sub], first_peer(to)
        )

    ones = jnp.ones((CHIP_PIX, LANES), jnp.bfloat16)
    for k in (1, 2, 3, 0):
        to = (a1 + k) % 4
        for g in range(8):
            lhs[g * GROUP : (g + 1) * GROUP, :] = smooth[pl.ds(group_start(to, g), GROUP), :]
        column = jnp.dot(lhs[...], ones, preferred_element_type=jnp.float32) / jnp.maximum(held, 1.0)

        def tile(n, _):
            cols = pl.ds(pl.multiple_of(n * TILE, TILE), TILE)
            product = lax.dot_general(
                lhs[...], smooth[cols, :], contract_last, preferred_element_type=jnp.float32
            )
            gown[:, cols] = product
            return 0

        lax.fori_loop(0, NFRAMES // TILE, tile, 0)
        for n in range(NFRAMES // LANES):
            cols = slice(n * LANES, (n + 1) * LANES)
            centred = gown[:, cols] - column * sums[:, cols]
            if k:
                gsend[to, :, cols] = centred.astype(jnp.bfloat16)
            else:
                gown[:, cols] = centred
        if k:
            for j in (1, 2, 3, 0):
                g_copy(k, (a2 + j) % 4).start()

    for k in range(1, 4):
        source = (a1 + k) % 4
        remote(stat1.at[source], stat1.at[source], s1_send.at[k], s1_recv.at[source], first_peer(source)).wait_recv()
    statg2[...] = stat1[0] + stat1[1] + stat1[2] + stat1[3]

    def stat2_copy(k):
        return remote(statg2, stat2.at[a2], s2_send.at[k], s2_recv.at[a2], second_peer((a2 + k) % 4))

    for k in range(1, 4):
        stat2_copy(k).start()
    total = statg2[...]
    for k in range(1, 4):
        source = (a2 + k) % 4
        remote(statg2, stat2.at[source], s2_send.at[k], s2_recv.at[source], second_peer(source)).wait_recv()
        total = total + stat2[source]
    statg3[...] = total

    def stat3_copy(k):
        return remote(statg3, stat3.at[z], s3_send.at[k], s3_recv.at[z], z_peer((z + k) % NZ))

    for k in range(1, NZ):
        stat3_copy(k).start()
    for k in range(1, NZ):
        source = (z + k) % NZ
        remote(statg3, stat3.at[source], s3_send.at[k], s3_recv.at[source], z_peer(source)).wait_recv()
        total = total + stat3[source]
    counts = total[1:2, :]
    mean = total[0:1, :] / counts

    spread[...] = jnp.zeros_like(spread)
    for k in range(4):
        spread[k : k + 1, :] = stat1[k, 0:1, :] / jnp.maximum(stat1[k, 1:2, :], 1.0) - mean
    spread_t[...] = jnp.transpose(spread[...])
    for k in range(4):
        spread[k : k + 1, :] = spread[k : k + 1, :] * stat1[k, 1:2, :]
    for g in range(8):
        rows = pl.ds(g * GROUP, GROUP)
        gown[rows, :] += jnp.dot(
            spread_t[pl.ds(group_start(a1, g), GROUP), :], spread[...],
            preferred_element_type=jnp.float32, precision=lax.Precision.HIGHEST,
        )

    def h_copy(k):
        to = (a2 + k) % 4
        return remote(hsend.at[to], hrecv.at[a2], h_send.at[k], h_recv.at[a2], second_peer(to))

    for j in (1, 2, 3, 0):
        sub = (a2 + j) % 4
        rows = pl.ds(pl.multiple_of(sub * SUB_ROWS, SUB_ROWS), SUB_ROWS)
        for k in range(1, 4):
            source = (a1 + k) % 4
            remote(
                gsend.at[source, rows, :], grecv.at[source, rows, :], g_send.at[k, sub], g_recv.at[source, sub],
                first_peer(source),
            ).wait_recv()
        value = gown[rows, :]
        for k in range(1, 4):
            value = value + grecv[(a1 + k) % 4, rows, :].astype(jnp.float32)
        if j:
            hsend[sub] = value.astype(jnp.bfloat16)
            h_copy(j).start()
        else:
            hown[...] = value

    for k in range(1, 4):
        source = (a2 + k) % 4
        remote(hsend.at[source], hrecv.at[source], h_send.at[k], h_recv.at[source], second_peer(source)).wait_recv()
    value = hown[...]
    for k in range(1, 4):
        value = value + hrecv[(a2 + k) % 4].astype(jnp.float32)
    hown[...] = value
    own_rows = GROUP // NZ

    for other_z in range(NZ):
        rows = jnp.concatenate(
            [hown[core * GROUP + other_z * own_rows : core * GROUP + (other_z + 1) * own_rows, :] for core in range(CORES)],
            axis=0,
        )
        tsend[other_z] = rows.astype(jnp.bfloat16)

    def t_copy(k):
        to = (z + k) % NZ
        return remote(tsend.at[to], trecv.at[z], t_send.at[k], t_recv.at[z], z_peer(to))

    for k in range(1, NZ):
        t_copy(k).start()
    value = tsend[z].astype(jnp.float32)
    for k in range(1, NZ):
        source = (z + k) % NZ
        remote(tsend.at[source], trecv.at[source], t_send.at[k], t_recv.at[source], z_peer(source)).wait_recv()
        value = value + trecv[source].astype(jnp.float32)
    value = value / counts

    low, high = value[0:own_rows, :], value[own_rows : 2 * own_rows, :]
    fsend[...] = jnp.where(c == 0, high, low)
    last = remote(fsend, frecv, f_send, f_recv, sibling)
    last.start()
    out[c] = jnp.where(c == 0, low, high)
    last.wait_recv()
    out[1 - c] = frecv[...]

    for chunk in range(CHUNKS):
        for k in range(1, NDEV_FRAME):
            a2a_copy(k, chunk).wait_send()
        sib_copy(chunk).wait_send()
    for k in range(1, 4):
        stat1_copy(k).wait_send()
        stat2_copy(k).wait_send()
        h_copy(k).wait_send()
        for sub in range(4):
            g_copy(k, sub).wait_send()
    for k in range(1, NZ):
        stat3_copy(k).wait_send()
        t_copy(k).wait_send()
    last.wait_send()


def shards(frames, dead_time, band_width, cycle_label, valid):
    rows = NPIX_GROUP // LANES
    flat = [a.reshape(rows, LANES) for a in (dead_time, band_width, cycle_label, valid)]
    own_rows = GROUP // NZ
    dma = pltpu.SemaphoreType.DMA
    f32, bf16 = jnp.float32, jnp.bfloat16
    any_space = pl.BlockSpec(memory_space=pl.ANY)
    vmem = pltpu.VMEM
    out = pl.pallas_call(
        kernel,
        out_shape=jax.ShapeDtypeStruct((CYCLES, own_rows, NFRAMES), f32),
        in_specs=[any_space] * 5,
        out_specs=pl.BlockSpec(memory_space=pltpu.VMEM),
        scratch_shapes=[
            vmem((rows, LANES), f32),
            vmem((rows, LANES), jnp.int32),
            vmem((rows, LANES), jnp.int32),
            vmem((rows, LANES), jnp.int32),
            vmem((CHUNKS, NDEV_FRAME, OWN_FRAMES, LANES), bf16),
            vmem((PAD + NFRAMES + PAD, LANES), f32),
            vmem((NFRAMES, CHIP_PIX), bf16),
            vmem((CHUNKS, NFRAMES, LANES), bf16),
            vmem((CLASS_ROWS, CHIP_PIX), bf16),
            vmem((4, CLASS_ROWS, NFRAMES), bf16),
            vmem((4, CLASS_ROWS, NFRAMES), bf16),
            vmem((CLASS_ROWS, NFRAMES), f32),
            vmem((4, SUB_ROWS, NFRAMES), bf16),
            vmem((4, SUB_ROWS, NFRAMES), bf16),
            vmem((SUB_ROWS, NFRAMES), f32),
            vmem((NZ, CORES * own_rows, NFRAMES), bf16),
            vmem((NZ, CORES * own_rows, NFRAMES), bf16),
            vmem((4, 2, NFRAMES), f32),
            vmem((4, 2, NFRAMES), f32),
            vmem((NZ, 2, NFRAMES), f32),
            vmem((2, NFRAMES), f32),
            vmem((2, NFRAMES), f32),
            vmem((8, NFRAMES), f32),
            vmem((NFRAMES, 8), f32),
            vmem((own_rows, NFRAMES), f32),
            vmem((own_rows, NFRAMES), f32),
            dma((4,)),
            dma((CHUNKS,)),
            dma((CHUNKS, NDEV_FRAME)), dma((CHUNKS, NDEV_FRAME)),
            dma((CHUNKS,)), dma((CHUNKS,)),
            dma((4,)), dma((4,)),
            dma((4,)), dma((4,)),
            dma((NZ,)), dma((NZ,)),
            dma((4, 4)), dma((4, 4)),
            dma((4,)), dma((4,)),
            dma((NZ,)), dma((NZ,)),
            dma, dma,
        ],
        compiler_params=pltpu.CompilerParams(
            collective_id=0, has_side_effects=True, vmem_limit_bytes=48 * 2**20
        ),
    )(frames, *flat)
    return jnp.transpose(out, (1, 0, 2))


def solution(mesh):
    in_specs = (P("frame", "pixel"), P("pixel"), P("pixel"), P("pixel"), P("pixel"))
    out_specs = P(("frame", "pixel"), None, None)
    return jax.shard_map(shards, mesh=mesh, in_specs=in_specs, out_specs=out_specs, check_vma=False)
```

```python
import functools

import jax
import jax.numpy as jnp
from jax import lax
from jax.experimental import pallas as pl
from jax.experimental.pallas import tpu as pltpu
from jax.sharding import PartitionSpec as P

MESH = pl.DeviceIdType.MESH
CYCLES = 2
BAND = 8
CORES = 2
NX = 4
NY = 4
NZ = 8
LANES = 128
GROUP = 32
NFRAMES = 1024
NDEV_FRAME = NX * CORES
OWN_FRAMES = NFRAMES // NDEV_FRAME
NPIX_GROUP = 4096
OWN_PIX = NPIX_GROUP // NDEV_FRAME
CHUNKS = OWN_PIX // LANES
CHIP_PIX = CORES * OWN_PIX
CLASS_ROWS = NFRAMES // 4
SUB_ROWS = CLASS_ROWS // 4
PAD = BAND
TILE = 256


def remote(src, dst, send_sem, recv_sem, device):
    return pltpu.make_async_remote_copy(
        src_ref=src,
        dst_ref=dst,
        send_sem=send_sem,
        recv_sem=recv_sem,
        device_id=device,
        device_id_type=MESH,
    )


def kernel(
    frames, dead_hbm, band_hbm, label_hbm, valid_hbm,
    out,
    dead, band, label, valid, arrived, rate, smooth, outgoing,
    gram, sums_ref, sums_t, gsend, grecv, gown, hsend, hrecv, hown, tsend, trecv,
    stat1, stat2, stat3, statg2, statg3, spread, spread_t,
    fsend, frecv,
    par_sem, own_sem, a2a_send, a2a_recv, sib_send, sib_recv,
    s1_send, s1_recv, s2_send, s2_recv, s3_send, s3_recv,
    g_send, g_recv, h_send, h_recv, t_send, t_recv, f_send, f_recv,
):
    f = lax.axis_index("frame")
    p = lax.axis_index("pixel")
    x, c = f // CORES, f % CORES
    y, z = p // NZ, p % NZ
    a1 = c * x + (1 - c) * y
    a2 = c * y + (1 - c) * x

    def first_peer(a):
        return ((c * a + (1 - c) * x) * CORES + c, (c * y + (1 - c) * a) * NZ + z)

    def second_peer(a):
        return ((c * x + (1 - c) * a) * CORES + c, (c * a + (1 - c) * y) * NZ + z)

    def z_peer(other):
        return (f, y * NZ + other)

    def frame_peer(other):
        return (other, p)

    sibling = (x * CORES + (1 - c), p)

    pending = []

    def launch(copy):
        copy.start()
        pending.append(copy)

    def finish():
        for copy in pending:
            copy.wait_send()

    barrier = pltpu.get_barrier_semaphore()
    for k in range(1, NDEV_FRAME):
        pl.semaphore_signal(barrier, inc=1, device_id=frame_peer((f + k) % NDEV_FRAME), device_id_type=MESH)
    for k in range(1, NY):
        pl.semaphore_signal(barrier, inc=1, device_id=(f, ((y + k) % NY) * NZ + z), device_id_type=MESH)
    for k in range(1, NZ):
        pl.semaphore_signal(barrier, inc=1, device_id=z_peer((z + k) % NZ), device_id_type=MESH)
    pl.semaphore_wait(barrier, NDEV_FRAME - 1 + NY - 1 + NZ - 1)

    def piece(owner, chunk):
        return frames.at[:, pl.ds(pl.multiple_of(owner * OWN_PIX + chunk * LANES, LANES), LANES)]

    def a2a_copy(k, chunk):
        to = (f + k) % NDEV_FRAME
        return remote(
            piece(to, chunk), arrived.at[chunk, f], a2a_send.at[chunk, k], a2a_recv.at[chunk, f], frame_peer(to)
        )

    def own_copy(chunk):
        return pltpu.make_async_copy(piece(f, chunk), arrived.at[chunk, f], own_sem.at[chunk])

    for chunk in range(CHUNKS):
        for k in range(1, NDEV_FRAME):
            launch(a2a_copy(k, chunk))
        own_copy(chunk).start()
    params = [
        pltpu.make_async_copy(src, dst, par_sem.at[n])
        for n, (src, dst) in enumerate(
            ((dead_hbm, dead), (band_hbm, band), (label_hbm, label), (valid_hbm, valid))
        )
    ]
    for copy in params:
        copy.start()
    rate[0:PAD, :] = jnp.zeros((PAD, LANES), jnp.float32)
    rate[PAD + NFRAMES : PAD + NFRAMES + PAD, :] = jnp.zeros((PAD, LANES), jnp.float32)
    for copy in params:
        copy.wait()

    def sib_copy(chunk):
        return remote(
            outgoing.at[chunk],
            smooth.at[:, pl.ds((2 * chunk + 1) * LANES, LANES)],
            sib_send.at[chunk],
            sib_recv.at[chunk],
            sibling,
        )

    contract_last = (((1,), (1,)), ((), ()))

    def accumulate(chunk):
        lanes = slice(2 * chunk * LANES, 2 * (chunk + 1) * LANES)
        sib_copy(chunk).wait_recv()
        part = lax.dot_general(
            jnp.ones((8, 2 * LANES), jnp.bfloat16), smooth[:, lanes], contract_last, preferred_element_type=jnp.float32
        )
        sums_ref[...] = part if chunk == 0 else sums_ref[...] + part

        def columns(n, _):
            cols = pl.ds(pl.multiple_of(n * TILE, TILE), TILE)
            product = lax.dot_general(
                smooth[:, lanes], smooth[cols, lanes], contract_last, preferred_element_type=jnp.float32
            )
            if chunk == 0:
                gram[:, cols] = product
            else:
                gram[:, cols] += product
            return 0

        lax.fori_loop(0, NFRAMES // TILE, columns, 0)

    for chunk in range(CHUNKS):
        own_copy(chunk).wait()
        for k in range(1, NDEV_FRAME):
            source = (f + k) % NDEV_FRAME
            remote(
                piece(source, chunk), arrived.at[chunk, source], a2a_send.at[chunk, k],
                a2a_recv.at[chunk, source], frame_peer(source),
            ).wait_recv()
        row = f * CHUNKS + chunk
        dead_row = dead[pl.ds(row, 1), :]
        width = band[pl.ds(row, 1), :]
        cycle = label[pl.ds(row, 1), :]
        used = valid[pl.ds(row, 1), :] == 1
        mine = jnp.where(used & (cycle == c), 1.0, 0.0)
        other = jnp.where(used & (cycle == 1 - c), 1.0, 0.0)
        within = [jnp.where(width >= k, 1.0, 0.0) for k in range(1, BAND + 1)]
        full = 1.0 / (2 * width + 1).astype(jnp.float32)

        def correct(block, _):
            for half in range(OWN_FRAMES // GROUP):
                count = 4.0 + arrived[chunk, block, half * GROUP : (half + 1) * GROUP, :].astype(jnp.float32)
                rate[pl.ds(pl.multiple_of(PAD + block * OWN_FRAMES + half * GROUP, 8), GROUP), :] = count / (
                    1.0 - dead_row * count
                )
            return 0

        lax.fori_loop(0, NDEV_FRAME, correct, 0)

        def window(start):
            total = rate[pl.ds(start + PAD, GROUP), :]
            for k in range(1, BAND + 1):
                total = total + within[k - 1] * (
                    rate[pl.ds(start + PAD - k, GROUP), :] + rate[pl.ds(start + PAD + k, GROUP), :]
                )
            return total

        def put(start, value):
            rows = pl.ds(start, GROUP)
            smooth[rows, 2 * chunk * LANES : (2 * chunk + 1) * LANES] = (value * mine).astype(jnp.bfloat16)
            outgoing[chunk, rows, :] = (value * other).astype(jnp.bfloat16)

        def inside(block, _):
            start = pl.multiple_of(block * GROUP, GROUP)
            put(start, window(start) * full)
            return 0

        for start in (0, NFRAMES - GROUP):
            frame = start + lax.broadcasted_iota(jnp.int32, (GROUP, LANES), 0)
            span = jnp.minimum(frame + width, NFRAMES - 1) - jnp.maximum(frame - width, 0) + 1
            put(start, window(start) / span.astype(jnp.float32))
        lax.fori_loop(1, NFRAMES // GROUP - 1, inside, 0)
        launch(sib_copy(chunk))
        if chunk:
            accumulate(chunk - 1)

    chip_label = label[pl.ds(pl.multiple_of(x * (CHIP_PIX // LANES), 8), CHIP_PIX // LANES), :]
    chip_valid = valid[pl.ds(pl.multiple_of(x * (CHIP_PIX // LANES), 8), CHIP_PIX // LANES), :]
    held = jnp.sum(jnp.where((chip_label == c) & (chip_valid == 1), 1.0, 0.0), axis=(0, 1), keepdims=True)

    accumulate(CHUNKS - 1)
    sums = sums_ref[0:1, :]
    sums_t[...] = jnp.transpose(sums_ref[...] / jnp.maximum(held, 1.0))
    stat1[a1, 0:1, :] = sums
    stat1[a1, 1:2, :] = jnp.broadcast_to(held, (1, NFRAMES))

    def stat1_copy(k):
        to = (a1 + k) % 4
        return remote(stat1.at[a1], stat1.at[a1], s1_send.at[k], s1_recv.at[a1], first_peer(to))

    for k in range(1, 4):
        launch(stat1_copy(k))

    def group_start(a, g):
        second, core = g // CORES, g % CORES
        row_x = c * a + (1 - c) * second
        row_y = c * second + (1 - c) * a
        return pl.multiple_of((row_x * 8 + core * 4 + row_y) * GROUP, GROUP)

    def g_copy(k, sub):
        to = (a1 + k) % 4
        rows = pl.ds(pl.multiple_of(sub * SUB_ROWS, SUB_ROWS), SUB_ROWS)
        return remote(
            gsend.at[to, rows, :], grecv.at[a1, rows, :], g_send.at[k, sub], g_recv.at[a1, sub], first_peer(to)
        )

    for k in (1, 2, 3, 0):
        to = (a1 + k) % 4
        for g in range(8):
            start = group_start(to, g)
            column = jnp.broadcast_to(sums_t[pl.ds(start, GROUP), 0:1], (GROUP, LANES))
            rows = pl.ds(g * GROUP, GROUP)
            for n in range(NFRAMES // LANES):
                cols = slice(n * LANES, (n + 1) * LANES)
                centred = gram[pl.ds(start, GROUP), cols] - column * sums[:, cols]
                if k:
                    gsend[to, rows, cols] = centred.astype(jnp.bfloat16)
                else:
                    gown[rows, cols] = centred
        if k:
            for j in (1, 2, 3, 0):
                launch(g_copy(k, (a2 + j) % 4))

    for k in range(1, 4):
        source = (a1 + k) % 4
        remote(stat1.at[source], stat1.at[source], s1_send.at[k], s1_recv.at[source], first_peer(source)).wait_recv()
    statg2[...] = stat1[0] + stat1[1] + stat1[2] + stat1[3]
    stat2[a2] = statg2[...]

    def stat2_copy(k):
        return remote(statg2, stat2.at[a2], s2_send.at[k], s2_recv.at[a2], second_peer((a2 + k) % 4))

    for k in range(1, 4):
        launch(stat2_copy(k))
    def stat3_copy(k):
        return remote(statg3, stat3.at[z], s3_send.at[k], s3_recv.at[z], z_peer((z + k) % NZ))

    def between(stat, members):
        group = stat[0]
        for k in range(1, members):
            group = group + stat[k]
        mean = group[0:1, :] / jnp.maximum(group[1:2, :], 1.0)
        for k in range(members):
            spread[k : k + 1, :] = stat[k, 0:1, :] / jnp.maximum(stat[k, 1:2, :], 1.0) - mean
        spread_t[...] = jnp.transpose(spread[...])
        for k in range(members):
            spread[k : k + 1, :] = spread[k : k + 1, :] * stat[k, 1:2, :]
        return group

    def outer(rows):
        return jnp.dot(rows, spread[...], preferred_element_type=jnp.float32, precision=lax.Precision.HIGHEST)

    spread[...] = jnp.zeros_like(spread)
    between(stat1, 4)
    for g in range(8):
        gown[g * GROUP : (g + 1) * GROUP, :] += outer(spread_t[pl.ds(group_start(a1, g), GROUP), :])

    def h_copy(k):
        to = (a2 + k) % 4
        return remote(hsend.at[to], hrecv.at[a2], h_send.at[k], h_recv.at[a2], second_peer(to))

    for j in (1, 2, 3, 0):
        sub = (a2 + j) % 4
        rows = pl.ds(pl.multiple_of(sub * SUB_ROWS, SUB_ROWS), SUB_ROWS)
        for k in range(1, 4):
            source = (a1 + k) % 4
            remote(
                gsend.at[source, rows, :], grecv.at[source, rows, :], g_send.at[k, sub], g_recv.at[source, sub],
                first_peer(source),
            ).wait_recv()
        value = gown[rows, :]
        for k in range(1, 4):
            value = value + grecv[(a1 + k) % 4, rows, :].astype(jnp.float32)
        if j:
            hsend[sub] = value.astype(jnp.bfloat16)
            launch(h_copy(j))
        else:
            hown[...] = value

    for k in range(1, 4):
        source = (a2 + k) % 4
        remote(statg2, stat2.at[source], s2_send.at[k], s2_recv.at[source], second_peer(source)).wait_recv()
    statg3[...] = stat2[0] + stat2[1] + stat2[2] + stat2[3]
    stat3[z] = statg3[...]
    for k in range(1, NZ):
        launch(stat3_copy(k))
    between(stat2, 4)
    for core in range(CORES):
        hown[core * GROUP : (core + 1) * GROUP, :] += outer(
            spread_t[pl.ds(group_start(a1, a2 * CORES + core), GROUP), :]
        )
    for k in range(1, 4):
        source = (a2 + k) % 4
        remote(hsend.at[source], hrecv.at[source], h_send.at[k], h_recv.at[source], second_peer(source)).wait_recv()
    value = hown[...]
    for k in range(1, 4):
        value = value + hrecv[(a2 + k) % 4].astype(jnp.float32)
    hown[...] = value
    own_rows = GROUP // NZ

    for other_z in range(NZ):
        rows = jnp.concatenate(
            [hown[core * GROUP + other_z * own_rows : core * GROUP + (other_z + 1) * own_rows, :] for core in range(CORES)],
            axis=0,
        )
        tsend[other_z] = rows.astype(jnp.bfloat16)

    def t_copy(k):
        to = (z + k) % NZ
        return remote(tsend.at[to], trecv.at[z], t_send.at[k], t_recv.at[z], z_peer(to))

    for k in range(1, NZ):
        launch(t_copy(k))
    for k in range(1, NZ):
        source = (z + k) % NZ
        remote(statg3, stat3.at[source], s3_send.at[k], s3_recv.at[source], z_peer(source)).wait_recv()
    counts = between(stat3, NZ)[1:2, :]
    halves = [
        spread_t[pl.ds(pl.multiple_of(group_start(a1, a2 * CORES + core) + z // 2 * 8, 8), 8), :] for core in range(CORES)
    ]
    even = z % 2 == 0
    value = tsend[z].astype(jnp.float32) + outer(
        jnp.concatenate([jnp.where(even, half[0:own_rows], half[own_rows : 2 * own_rows]) for half in halves], axis=0)
    )
    for k in range(1, NZ):
        source = (z + k) % NZ
        remote(tsend.at[source], trecv.at[source], t_send.at[k], t_recv.at[source], z_peer(source)).wait_recv()
        value = value + trecv[source].astype(jnp.float32)
    value = value / counts

    low, high = value[0:own_rows, :], value[own_rows : 2 * own_rows, :]
    fsend[...] = jnp.where(c == 0, high, low)
    last = remote(fsend, frecv, f_send, f_recv, sibling)
    launch(last)
    out[c] = jnp.where(c == 0, low, high)
    last.wait_recv()
    out[1 - c] = frecv[...]

    finish()


def shards(frames, dead_time, band_width, cycle_label, valid):
    rows = NPIX_GROUP // LANES
    flat = [a.reshape(rows, LANES) for a in (dead_time, band_width, cycle_label, valid)]
    own_rows = GROUP // NZ
    dma = pltpu.SemaphoreType.DMA
    f32, bf16 = jnp.float32, jnp.bfloat16
    any_space = pl.BlockSpec(memory_space=pltpu.HBM)
    vmem = pltpu.VMEM
    out = pl.pallas_call(
        kernel,
        out_shape=jax.ShapeDtypeStruct((CYCLES, own_rows, NFRAMES), f32),
        in_specs=[any_space] * 5,
        out_specs=pl.BlockSpec(memory_space=pltpu.VMEM),
        scratch_shapes=[
            vmem((rows, LANES), f32),
            vmem((rows, LANES), jnp.int32),
            vmem((rows, LANES), jnp.int32),
            vmem((rows, LANES), jnp.int32),
            vmem((CHUNKS, NDEV_FRAME, OWN_FRAMES, LANES), bf16),
            vmem((PAD + NFRAMES + PAD, LANES), f32),
            vmem((NFRAMES, CHIP_PIX), bf16),
            vmem((CHUNKS, NFRAMES, LANES), bf16),
            vmem((NFRAMES, NFRAMES), f32),
            vmem((8, NFRAMES), f32),
            vmem((NFRAMES, 8), f32),
            vmem((4, CLASS_ROWS, NFRAMES), bf16),
            vmem((4, CLASS_ROWS, NFRAMES), bf16),
            vmem((CLASS_ROWS, NFRAMES), f32),
            vmem((4, SUB_ROWS, NFRAMES), bf16),
            vmem((4, SUB_ROWS, NFRAMES), bf16),
            vmem((SUB_ROWS, NFRAMES), f32),
            vmem((NZ, CORES * own_rows, NFRAMES), bf16),
            vmem((NZ, CORES * own_rows, NFRAMES), bf16),
            vmem((4, 2, NFRAMES), f32),
            vmem((4, 2, NFRAMES), f32),
            vmem((NZ, 2, NFRAMES), f32),
            vmem((2, NFRAMES), f32),
            vmem((2, NFRAMES), f32),
            vmem((8, NFRAMES), f32),
            vmem((NFRAMES, 8), f32),
            vmem((own_rows, NFRAMES), f32),
            vmem((own_rows, NFRAMES), f32),
            dma((4,)),
            dma((CHUNKS,)),
            dma((CHUNKS, NDEV_FRAME)), dma((CHUNKS, NDEV_FRAME)),
            dma((CHUNKS,)), dma((CHUNKS,)),
            dma((4,)), dma((4,)),
            dma((4,)), dma((4,)),
            dma((NZ,)), dma((NZ,)),
            dma((4, 4)), dma((4, 4)),
            dma((4,)), dma((4,)),
            dma((NZ,)), dma((NZ,)),
            dma, dma,
        ],
        compiler_params=pltpu.CompilerParams(
            collective_id=0, has_side_effects=True, vmem_limit_bytes=60 * 2**20
        ),
    )(frames, *flat)
    return jnp.transpose(out, (1, 0, 2))


def solution(mesh):
    in_specs = (P("frame", "pixel"), P("pixel"), P("pixel"), P("pixel"), P("pixel"))
    out_specs = P(("frame", "pixel"), None, None)
    return jax.shard_map(shards, mesh=mesh, in_specs=in_specs, out_specs=out_specs, check_vma=False)
```

```python
import functools

import jax
import jax.numpy as jnp
from jax import lax
from jax.experimental import pallas as pl
from jax.experimental.pallas import tpu as pltpu
from jax.sharding import PartitionSpec as P

MESH = pl.DeviceIdType.MESH
CYCLES = 2
BAND = 8
CORES = 2
NX = 4
NY = 4
NZ = 8
LANES = 128
GROUP = 32
NFRAMES = 1024
NDEV_FRAME = NX * CORES
OWN_FRAMES = NFRAMES // NDEV_FRAME
NPIX_GROUP = 4096
OWN_PIX = NPIX_GROUP // NDEV_FRAME
CHUNKS = OWN_PIX // LANES
CHIP_PIX = CORES * OWN_PIX
CLASS_ROWS = NFRAMES // 4
SUB_ROWS = CLASS_ROWS // 4
PAD = BAND
TILE = 512


def remote(src, dst, send_sem, recv_sem, device):
    return pltpu.make_async_remote_copy(
        src_ref=src,
        dst_ref=dst,
        send_sem=send_sem,
        recv_sem=recv_sem,
        device_id=device,
        device_id_type=MESH,
    )


def kernel(
    frames, dead_hbm, band_hbm, label_hbm, valid_hbm,
    out,
    dead, band, label, valid, arrived, rate, smooth, outgoing,
    gram, sums_ref, sums_t, gsend, grecv, gown, hsend, hrecv, hown, tsend, trecv,
    stat1, stat2, stat3, statg2, statg3, spread, spread_t,
    par_sem, own_sem, a2a_send, a2a_recv, sib_send, sib_recv,
    s1_send, s1_recv, s2_send, s2_recv, s3_send, s3_recv,
    g_send, g_recv, h_send, h_recv, t_send, t_recv,
):
    f = lax.axis_index("frame")
    p = lax.axis_index("pixel")
    x, c = f // CORES, f % CORES
    y, z = p // NZ, p % NZ
    a1 = c * x + (1 - c) * y
    a2 = c * y + (1 - c) * x

    def first_peer(a):
        return ((c * a + (1 - c) * x) * CORES + c, (c * y + (1 - c) * a) * NZ + z)

    def second_peer(a):
        return ((c * x + (1 - c) * a) * CORES + c, (c * a + (1 - c) * y) * NZ + z)

    def z_peer(other):
        return (f, y * NZ + other)

    def frame_peer(other):
        return (other, p)

    sibling = (x * CORES + (1 - c), p)

    pending = []

    def launch(copy):
        copy.start()
        pending.append(copy)

    def finish():
        for copy in pending:
            copy.wait_send()

    barrier = pltpu.get_barrier_semaphore()
    for k in range(1, NDEV_FRAME):
        pl.semaphore_signal(barrier, inc=1, device_id=frame_peer((f + k) % NDEV_FRAME), device_id_type=MESH)
    for k in range(1, NY):
        pl.semaphore_signal(barrier, inc=1, device_id=(f, ((y + k) % NY) * NZ + z), device_id_type=MESH)
    for k in range(1, NZ):
        for core in range(CORES):
            pl.semaphore_signal(
                barrier, inc=1, device_id=(x * CORES + core, y * NZ + (z + k) % NZ), device_id_type=MESH
            )
    pl.semaphore_wait(barrier, NDEV_FRAME - 1 + NY - 1 + CORES * (NZ - 1))

    def piece(owner, chunk):
        return frames.at[:, pl.ds(pl.multiple_of(owner * OWN_PIX + chunk * LANES, LANES), LANES)]

    def a2a_copy(k, chunk):
        to = (f + k) % NDEV_FRAME
        return remote(
            piece(to, chunk), arrived.at[chunk, f], a2a_send.at[chunk, k], a2a_recv.at[chunk, f], frame_peer(to)
        )

    def own_copy(chunk):
        return pltpu.make_async_copy(piece(f, chunk), arrived.at[chunk, f], own_sem.at[chunk])

    for chunk in range(CHUNKS):
        for k in range(1, NDEV_FRAME):
            launch(a2a_copy(k, chunk))
        own_copy(chunk).start()
    params = [
        pltpu.make_async_copy(src, dst, par_sem.at[n])
        for n, (src, dst) in enumerate(
            ((dead_hbm, dead), (band_hbm, band), (label_hbm, label), (valid_hbm, valid))
        )
    ]
    for copy in params:
        copy.start()
    rate[0:PAD, :] = jnp.zeros((PAD, LANES), jnp.float32)
    rate[PAD + NFRAMES : PAD + NFRAMES + PAD, :] = jnp.zeros((PAD, LANES), jnp.float32)
    for copy in params:
        copy.wait()

    def sib_copy(chunk):
        return remote(
            outgoing.at[chunk],
            smooth.at[:, pl.ds((2 * chunk + 1) * LANES, LANES)],
            sib_send.at[chunk],
            sib_recv.at[chunk],
            sibling,
        )

    contract_last = (((1,), (1,)), ((), ()))

    def accumulate(chunk):
        lanes = slice(2 * chunk * LANES, 2 * (chunk + 1) * LANES)
        sib_copy(chunk).wait_recv()
        part = lax.dot_general(
            jnp.ones((8, 2 * LANES), jnp.bfloat16), smooth[:, lanes], contract_last, preferred_element_type=jnp.float32
        )
        sums_ref[...] = part if chunk == 0 else sums_ref[...] + part

        for n in range(NFRAMES // TILE):
            cols = slice(n * TILE, (n + 1) * TILE)
            product = lax.dot_general(
                smooth[:, lanes], smooth[cols, lanes], contract_last, preferred_element_type=jnp.float32
            )
            gram[:, cols] = product if chunk == 0 else gram[:, cols] + product

    for chunk in range(CHUNKS):
        own_copy(chunk).wait()
        for k in range(1, NDEV_FRAME):
            source = (f + k) % NDEV_FRAME
            remote(
                piece(source, chunk), arrived.at[chunk, source], a2a_send.at[chunk, k],
                a2a_recv.at[chunk, source], frame_peer(source),
            ).wait_recv()
        row = f * CHUNKS + chunk
        dead_row = dead[pl.ds(row, 1), :]
        width = band[pl.ds(row, 1), :]
        cycle = label[pl.ds(row, 1), :]
        used = valid[pl.ds(row, 1), :] == 1
        mine = jnp.where(used & (cycle == c), 1.0, 0.0)
        other = jnp.where(used & (cycle == 1 - c), 1.0, 0.0)
        within = [jnp.where(width >= k, 1.0, 0.0) for k in range(1, BAND + 1)]
        full = 1.0 / (2 * width + 1).astype(jnp.float32)

        def correct(block, _):
            for half in range(OWN_FRAMES // GROUP):
                count = 4.0 + arrived[chunk, block, half * GROUP : (half + 1) * GROUP, :].astype(jnp.float32)
                rate[pl.ds(pl.multiple_of(PAD + block * OWN_FRAMES + half * GROUP, 8), GROUP), :] = count / (
                    1.0 - dead_row * count
                )
            return 0

        lax.fori_loop(0, NDEV_FRAME, correct, 0)

        def window(start):
            total = rate[pl.ds(start + PAD, GROUP), :]
            for k in range(1, BAND + 1):
                total = total + within[k - 1] * (
                    rate[pl.ds(start + PAD - k, GROUP), :] + rate[pl.ds(start + PAD + k, GROUP), :]
                )
            return total

        def put(start, value):
            rows = pl.ds(start, GROUP)
            smooth[rows, 2 * chunk * LANES : (2 * chunk + 1) * LANES] = (value * mine).astype(jnp.bfloat16)
            outgoing[chunk, rows, :] = (value * other).astype(jnp.bfloat16)

        def inside(block, _):
            start = pl.multiple_of(block * GROUP, GROUP)
            put(start, window(start) * full)
            return 0

        for start in (0, NFRAMES - GROUP):
            frame = start + lax.broadcasted_iota(jnp.int32, (GROUP, LANES), 0)
            span = jnp.minimum(frame + width, NFRAMES - 1) - jnp.maximum(frame - width, 0) + 1
            put(start, window(start) / span.astype(jnp.float32))
        lax.fori_loop(1, NFRAMES // GROUP - 1, inside, 0)
        launch(sib_copy(chunk))
        if chunk:
            accumulate(chunk - 1)

    chip_label = label[pl.ds(pl.multiple_of(x * (CHIP_PIX // LANES), 8), CHIP_PIX // LANES), :]
    chip_valid = valid[pl.ds(pl.multiple_of(x * (CHIP_PIX // LANES), 8), CHIP_PIX // LANES), :]
    held = jnp.sum(jnp.where((chip_label == c) & (chip_valid == 1), 1.0, 0.0), axis=(0, 1), keepdims=True)

    accumulate(CHUNKS - 1)
    sums = sums_ref[0:1, :]
    sums_t[...] = jnp.transpose(sums_ref[...] / jnp.maximum(held, 1.0))
    stat1[a1, 0:1, :] = sums
    stat1[a1, 1:2, :] = jnp.broadcast_to(held, (1, NFRAMES))

    def stat1_copy(k):
        to = (a1 + k) % 4
        return remote(stat1.at[a1], stat1.at[a1], s1_send.at[k], s1_recv.at[a1], first_peer(to))

    for k in range(1, 4):
        launch(stat1_copy(k))

    def group_start(a, g):
        second, core = g // CORES, g % CORES
        row_x = c * a + (1 - c) * second
        row_y = c * second + (1 - c) * a
        return pl.multiple_of((row_x * 8 + core * 4 + row_y) * GROUP, GROUP)

    def g_copy(k, sub):
        to = (a1 + k) % 4
        rows = pl.ds(pl.multiple_of(sub * SUB_ROWS, SUB_ROWS), SUB_ROWS)
        return remote(
            gsend.at[to, rows, :], grecv.at[a1, rows, :], g_send.at[k, sub], g_recv.at[a1, sub], first_peer(to)
        )

    for k in (1, 2, 3, 0):
        to = (a1 + k) % 4
        for g in range(8):
            start = group_start(to, g)
            column = jnp.broadcast_to(sums_t[pl.ds(start, GROUP), 0:1], (GROUP, LANES))
            rows = pl.ds(g * GROUP, GROUP)
            for n in range(NFRAMES // LANES):
                cols = slice(n * LANES, (n + 1) * LANES)
                centred = gram[pl.ds(start, GROUP), cols] - column * sums[:, cols]
                if k:
                    gsend[to, rows, cols] = centred.astype(jnp.bfloat16)
                else:
                    gown[rows, cols] = centred

    for j in (1, 2, 3, 0):
        for k in (2, 1, 3):
            launch(g_copy(k, (a2 + j) % 4))
    for k in range(1, 4):
        source = (a1 + k) % 4
        remote(stat1.at[source], stat1.at[source], s1_send.at[k], s1_recv.at[source], first_peer(source)).wait_recv()
    statg2[...] = stat1[0] + stat1[1] + stat1[2] + stat1[3]
    stat2[a2] = statg2[...]

    def stat2_copy(k):
        return remote(statg2, stat2.at[a2], s2_send.at[k], s2_recv.at[a2], second_peer((a2 + k) % 4))

    for k in range(1, 4):
        launch(stat2_copy(k))
    def stat3_copy(k):
        return remote(statg3, stat3.at[z], s3_send.at[k], s3_recv.at[z], z_peer((z + k) % NZ))

    def between(stat, group):
        mean = group[0:1, :] / jnp.maximum(group[1:2, :], 1.0)
        for k in range(4):
            spread[k : k + 1, :] = stat[k, 0:1, :] / jnp.maximum(stat[k, 1:2, :], 1.0) - mean
        spread_t[...] = jnp.transpose(spread[...])
        for k in range(4):
            spread[k : k + 1, :] = spread[k : k + 1, :] * stat[k, 1:2, :]

    def outer(rows):
        return jnp.dot(rows, spread[...], preferred_element_type=jnp.float32, precision=lax.Precision.HIGHEST)

    spread[...] = jnp.zeros_like(spread)
    between(stat1, statg2[...])
    for g in range(8):
        gown[g * GROUP : (g + 1) * GROUP, :] += outer(spread_t[pl.ds(group_start(a1, g), GROUP), :])

    def h_copy(k):
        to = (a2 + k) % 4
        return remote(hsend.at[to], hrecv.at[a2], h_send.at[k], h_recv.at[a2], second_peer(to))

    for j in (1, 2, 3, 0):
        sub = (a2 + j) % 4
        rows = pl.ds(pl.multiple_of(sub * SUB_ROWS, SUB_ROWS), SUB_ROWS)
        for k in range(1, 4):
            source = (a1 + k) % 4
            remote(
                gsend.at[source, rows, :], grecv.at[source, rows, :], g_send.at[k, sub], g_recv.at[source, sub],
                first_peer(source),
            ).wait_recv()
        if j == 3:
            for k in range(1, 4):
                source = (a2 + k) % 4
                remote(
                    statg2, stat2.at[source], s2_send.at[k], s2_recv.at[source], second_peer(source)
                ).wait_recv()
            statg3[...] = stat2[0] + stat2[1] + stat2[2] + stat2[3]
            for k in range(1, NZ):
                launch(stat3_copy(k))
        value = gown[rows, :]
        for k in range(1, 4):
            value = value + grecv[(a1 + k) % 4, rows, :].astype(jnp.float32)
        if j:
            hsend[sub] = value.astype(jnp.bfloat16)
            launch(h_copy(j))
        else:
            hown[...] = value

    everything = statg3[...]
    for k in range(1, NZ):
        source = (z + k) % NZ
        remote(statg3, stat3.at[source], s3_send.at[k], s3_recv.at[source], z_peer(source)).wait_recv()
        everything = everything + stat3[source]
    between(stat2, everything)
    for core in range(CORES):
        hown[core * GROUP : (core + 1) * GROUP, :] += outer(
            spread_t[pl.ds(group_start(a1, a2 * CORES + core), GROUP), :]
        )

    for k in range(1, 4):
        source = (a2 + k) % 4
        remote(hsend.at[source], hrecv.at[source], h_send.at[k], h_recv.at[source], second_peer(source)).wait_recv()
    value = hown[...]
    for k in range(1, 4):
        value = value + hrecv[(a2 + k) % 4].astype(jnp.float32)
    hown[...] = value / everything[1:2, :]
    own_rows = GROUP // NZ

    for other_z in range(NZ):
        for core in range(CORES):
            start = core * GROUP + other_z * own_rows
            tsend[other_z, core] = hown[start : start + own_rows, :].astype(jnp.bfloat16)

    def t_copy(k, flip):
        to, core = (z + k) % NZ, (c + flip) % CORES
        return remote(
            tsend.at[to, core], trecv.at[c, z], t_send.at[k, flip], t_recv.at[c, z],
            (x * CORES + core, y * NZ + to),
        )

    for k in range(NZ):
        for flip in range(CORES):
            if k or flip:
                launch(t_copy(k, flip))
    trecv[c, z] = tsend[z, c]
    for k in range(NZ):
        for flip in range(CORES):
            if k or flip:
                source, core = (z + k) % NZ, (c + flip) % CORES
                remote(
                    tsend.at[source, core], trecv.at[core, source], t_send.at[k, flip], t_recv.at[core, source],
                    (x * CORES + core, y * NZ + source),
                ).wait_recv()
    for core in range(CORES):
        value = trecv[core, 0].astype(jnp.float32)
        for k in range(1, NZ):
            value = value + trecv[core, k].astype(jnp.float32)
        out[core] = value

    finish()


def shards(frames, dead_time, band_width, cycle_label, valid):
    rows = NPIX_GROUP // LANES
    flat = [a.reshape(rows, LANES) for a in (dead_time, band_width, cycle_label, valid)]
    own_rows = GROUP // NZ
    dma = pltpu.SemaphoreType.DMA
    f32, bf16 = jnp.float32, jnp.bfloat16
    any_space = pl.BlockSpec(memory_space=pltpu.HBM)
    vmem = pltpu.VMEM
    out = pl.pallas_call(
        kernel,
        out_shape=jax.ShapeDtypeStruct((CYCLES, own_rows, NFRAMES), f32),
        in_specs=[any_space] * 5,
        out_specs=pl.BlockSpec(memory_space=pltpu.VMEM),
        scratch_shapes=[
            vmem((rows, LANES), f32),
            vmem((rows, LANES), jnp.int32),
            vmem((rows, LANES), jnp.int32),
            vmem((rows, LANES), jnp.int32),
            vmem((CHUNKS, NDEV_FRAME, OWN_FRAMES, LANES), bf16),
            vmem((PAD + NFRAMES + PAD, LANES), f32),
            vmem((NFRAMES, CHIP_PIX), bf16),
            vmem((CHUNKS, NFRAMES, LANES), bf16),
            vmem((NFRAMES, NFRAMES), f32),
            vmem((8, NFRAMES), f32),
            vmem((NFRAMES, 8), f32),
            vmem((4, CLASS_ROWS, NFRAMES), bf16),
            vmem((4, CLASS_ROWS, NFRAMES), bf16),
            vmem((CLASS_ROWS, NFRAMES), f32),
            vmem((4, SUB_ROWS, NFRAMES), bf16),
            vmem((4, SUB_ROWS, NFRAMES), bf16),
            vmem((SUB_ROWS, NFRAMES), f32),
            vmem((NZ, CORES, own_rows, NFRAMES), bf16),
            vmem((CORES, NZ, own_rows, NFRAMES), bf16),
            vmem((4, 2, NFRAMES), f32),
            vmem((4, 2, NFRAMES), f32),
            vmem((NZ, 2, NFRAMES), f32),
            vmem((2, NFRAMES), f32),
            vmem((2, NFRAMES), f32),
            vmem((8, NFRAMES), f32),
            vmem((NFRAMES, 8), f32),
            dma((4,)),
            dma((CHUNKS,)),
            dma((CHUNKS, NDEV_FRAME)), dma((CHUNKS, NDEV_FRAME)),
            dma((CHUNKS,)), dma((CHUNKS,)),
            dma((4,)), dma((4,)),
            dma((4,)), dma((4,)),
            dma((NZ,)), dma((NZ,)),
            dma((4, 4)), dma((4, 4)),
            dma((4,)), dma((4,)),
            dma((NZ, CORES)), dma((CORES, NZ)),
        ],
        compiler_params=pltpu.CompilerParams(
            collective_id=0, has_side_effects=True, vmem_limit_bytes=60 * 2**20
        ),
    )(frames, *flat)
    return jnp.transpose(out, (1, 0, 2))


def solution(mesh):
    in_specs = (P("frame", "pixel"), P("pixel"), P("pixel"), P("pixel"), P("pixel"))
    out_specs = P(("frame", "pixel"), None, None)
    return jax.shard_map(shards, mesh=mesh, in_specs=in_specs, out_specs=out_specs, check_vma=False)
```

```python
import functools

import jax
import jax.numpy as jnp
from jax import lax
from jax.experimental import pallas as pl
from jax.experimental.pallas import tpu as pltpu
from jax.sharding import PartitionSpec as P

MESH = pl.DeviceIdType.MESH
CYCLES = 2
BAND = 8
CORES = 2
NX = 4
NY = 4
NZ = 8
LANES = 128
GROUP = 32
NFRAMES = 1024
NDEV_FRAME = NX * CORES
OWN_FRAMES = NFRAMES // NDEV_FRAME
NPIX_GROUP = 4096
OWN_PIX = NPIX_GROUP // NDEV_FRAME
CHUNKS = OWN_PIX // LANES
CHIP_PIX = CORES * OWN_PIX
CLASS_ROWS = NFRAMES // 4
SUB_ROWS = CLASS_ROWS // 4
PAD = BAND
TILE = 512


def remote(src, dst, send_sem, recv_sem, device):
    return pltpu.make_async_remote_copy(
        src_ref=src,
        dst_ref=dst,
        send_sem=send_sem,
        recv_sem=recv_sem,
        device_id=device,
        device_id_type=MESH,
    )


def kernel(
    frames, dead_hbm, band_hbm, label_hbm, valid_hbm,
    out,
    dead, band, label, valid, arrived, rate, smooth, outgoing,
    gram, sums_ref, sums_t, gsend, grecv, gown, hsend, hrecv, hown, tsend, trecv,
    stat1, stat2, stat3, statg2, statg3, spread, spread_t,
    fsend, frecv,
    par_sem, own_sem, a2a_send, a2a_recv, sib_send, sib_recv,
    s1_send, s1_recv, s2_send, s2_recv, s3_send, s3_recv,
    g_send, g_recv, h_send, h_recv, t_send, t_recv, f_send, f_recv,
):
    f = lax.axis_index("frame")
    p = lax.axis_index("pixel")
    x, c = f // CORES, f % CORES
    y, z = p // NZ, p % NZ
    a1 = c * x + (1 - c) * y
    a2 = c * y + (1 - c) * x

    def first_peer(a):
        return ((c * a + (1 - c) * x) * CORES + c, (c * y + (1 - c) * a) * NZ + z)

    def second_peer(a):
        return ((c * x + (1 - c) * a) * CORES + c, (c * a + (1 - c) * y) * NZ + z)

    def z_peer(other):
        return (f, y * NZ + other)

    def frame_peer(other):
        return (other, p)

    sibling = (x * CORES + (1 - c), p)

    pending = []

    def launch(copy):
        copy.start()
        pending.append(copy)

    def finish():
        for copy in pending:
            copy.wait_send()

    barrier = pltpu.get_barrier_semaphore()
    for k in range(1, NDEV_FRAME):
        pl.semaphore_signal(barrier, inc=1, device_id=frame_peer((f + k) % NDEV_FRAME), device_id_type=MESH)
    for k in range(1, NY):
        pl.semaphore_signal(barrier, inc=1, device_id=(f, ((y + k) % NY) * NZ + z), device_id_type=MESH)
    for k in range(1, NZ):
        pl.semaphore_signal(barrier, inc=1, device_id=z_peer((z + k) % NZ), device_id_type=MESH)
    pl.semaphore_wait(barrier, NDEV_FRAME - 1 + NY - 1 + NZ - 1)

    def piece(owner, chunk):
        return frames.at[:, pl.ds(pl.multiple_of(owner * OWN_PIX + chunk * LANES, LANES), LANES)]

    def a2a_copy(k, chunk):
        to = (f + k) % NDEV_FRAME
        return remote(
            piece(to, chunk), arrived.at[chunk, f], a2a_send.at[chunk, k], a2a_recv.at[chunk, f], frame_peer(to)
        )

    def own_copy(chunk):
        return pltpu.make_async_copy(piece(f, chunk), arrived.at[chunk, f], own_sem.at[chunk])

    for chunk in range(CHUNKS):
        for k in range(1, NDEV_FRAME):
            launch(a2a_copy(k, chunk))
        own_copy(chunk).start()
    params = [
        pltpu.make_async_copy(src, dst, par_sem.at[n])
        for n, (src, dst) in enumerate(
            ((dead_hbm, dead), (band_hbm, band), (label_hbm, label), (valid_hbm, valid))
        )
    ]
    for copy in params:
        copy.start()
    rate[0:PAD, :] = jnp.zeros((PAD, LANES), jnp.float32)
    rate[PAD + NFRAMES : PAD + NFRAMES + PAD, :] = jnp.zeros((PAD, LANES), jnp.float32)
    for copy in params:
        copy.wait()

    def sib_copy(chunk):
        return remote(
            outgoing.at[chunk],
            smooth.at[:, pl.ds((2 * chunk + 1) * LANES, LANES)],
            sib_send.at[chunk],
            sib_recv.at[chunk],
            sibling,
        )

    contract_last = (((1,), (1,)), ((), ()))

    def accumulate(chunk):
        lanes = slice(2 * chunk * LANES, 2 * (chunk + 1) * LANES)
        sib_copy(chunk).wait_recv()
        part = lax.dot_general(
            jnp.ones((8, 2 * LANES), jnp.bfloat16), smooth[:, lanes], contract_last, preferred_element_type=jnp.float32
        )
        sums_ref[...] = part if chunk == 0 else sums_ref[...] + part

        for n in range(NFRAMES // TILE):
            cols = slice(n * TILE, (n + 1) * TILE)
            product = lax.dot_general(
                smooth[:, lanes], smooth[cols, lanes], contract_last, preferred_element_type=jnp.float32
            )
            gram[:, cols] = product if chunk == 0 else gram[:, cols] + product

    for chunk in range(CHUNKS):
        own_copy(chunk).wait()
        for k in range(1, NDEV_FRAME):
            source = (f + k) % NDEV_FRAME
            remote(
                piece(source, chunk), arrived.at[chunk, source], a2a_send.at[chunk, k],
                a2a_recv.at[chunk, source], frame_peer(source),
            ).wait_recv()
        row = f * CHUNKS + chunk
        dead_row = dead[pl.ds(row, 1), :]
        width = band[pl.ds(row, 1), :]
        cycle = label[pl.ds(row, 1), :]
        used = valid[pl.ds(row, 1), :] == 1
        mine = jnp.where(used & (cycle == c), 1.0, 0.0)
        other = jnp.where(used & (cycle == 1 - c), 1.0, 0.0)
        within = [jnp.where(width >= k, 1.0, 0.0) for k in range(1, BAND + 1)]
        full = 1.0 / (2 * width + 1).astype(jnp.float32)

        def correct(block, _):
            for half in range(OWN_FRAMES // GROUP):
                count = 4.0 + arrived[chunk, block, half * GROUP : (half + 1) * GROUP, :].astype(jnp.float32)
                rate[pl.ds(pl.multiple_of(PAD + block * OWN_FRAMES + half * GROUP, 8), GROUP), :] = count / (
                    1.0 - dead_row * count
                )
            return 0

        lax.fori_loop(0, NDEV_FRAME, correct, 0)

        def window(start):
            total = rate[pl.ds(start + PAD, GROUP), :]
            for k in range(1, BAND + 1):
                total = total + within[k - 1] * (
                    rate[pl.ds(start + PAD - k, GROUP), :] + rate[pl.ds(start + PAD + k, GROUP), :]
                )
            return total

        def put(start, value):
            rows = pl.ds(start, GROUP)
            smooth[rows, 2 * chunk * LANES : (2 * chunk + 1) * LANES] = (value * mine).astype(jnp.bfloat16)
            outgoing[chunk, rows, :] = (value * other).astype(jnp.bfloat16)

        def inside(block, _):
            start = pl.multiple_of(block * GROUP, GROUP)
            put(start, window(start) * full)
            return 0

        for start in (0, NFRAMES - GROUP):
            frame = start + lax.broadcasted_iota(jnp.int32, (GROUP, LANES), 0)
            span = jnp.minimum(frame + width, NFRAMES - 1) - jnp.maximum(frame - width, 0) + 1
            put(start, window(start) / span.astype(jnp.float32))
        lax.fori_loop(1, NFRAMES // GROUP - 1, inside, 0)
        launch(sib_copy(chunk))
        if chunk:
            accumulate(chunk - 1)

    chip_label = label[pl.ds(pl.multiple_of(x * (CHIP_PIX // LANES), 8), CHIP_PIX // LANES), :]
    chip_valid = valid[pl.ds(pl.multiple_of(x * (CHIP_PIX // LANES), 8), CHIP_PIX // LANES), :]
    held = jnp.sum(jnp.where((chip_label == c) & (chip_valid == 1), 1.0, 0.0), axis=(0, 1), keepdims=True)

    accumulate(CHUNKS - 1)
    sums = sums_ref[0:1, :]
    sums_t[...] = jnp.transpose(sums_ref[...] / jnp.maximum(held, 1.0))
    stat1[a1, 0:1, :] = sums
    stat1[a1, 1:2, :] = jnp.broadcast_to(held, (1, NFRAMES))

    def stat1_copy(k):
        to = (a1 + k) % 4
        return remote(stat1.at[a1], stat1.at[a1], s1_send.at[k], s1_recv.at[a1], first_peer(to))

    for k in range(1, 4):
        launch(stat1_copy(k))

    def group_start(a, g):
        second, core = g // CORES, g % CORES
        row_x = c * a + (1 - c) * second
        row_y = c * second + (1 - c) * a
        return pl.multiple_of((row_x * 8 + core * 4 + row_y) * GROUP, GROUP)

    def g_copy(k, sub):
        to = (a1 + k) % 4
        rows = pl.ds(pl.multiple_of(sub * SUB_ROWS, SUB_ROWS), SUB_ROWS)
        return remote(
            gsend.at[to, rows, :], grecv.at[a1, rows, :], g_send.at[k, sub], g_recv.at[a1, sub], first_peer(to)
        )

    for k in (1, 2, 3, 0):
        to = (a1 + k) % 4
        for g in range(8):
            start = group_start(to, g)
            column = jnp.broadcast_to(sums_t[pl.ds(start, GROUP), 0:1], (GROUP, LANES))
            rows = pl.ds(g * GROUP, GROUP)
            for n in range(NFRAMES // LANES):
                cols = slice(n * LANES, (n + 1) * LANES)
                centred = gram[pl.ds(start, GROUP), cols] - column * sums[:, cols]
                if k:
                    gsend[to, rows, cols] = centred.astype(jnp.bfloat16)
                else:
                    gown[rows, cols] = centred

    for j in (1, 2, 3, 0):
        for k in (2, 1, 3):
            launch(g_copy(k, (a2 + j) % 4))
    for k in range(1, 4):
        source = (a1 + k) % 4
        remote(stat1.at[source], stat1.at[source], s1_send.at[k], s1_recv.at[source], first_peer(source)).wait_recv()
    statg2[...] = stat1[0] + stat1[1] + stat1[2] + stat1[3]
    stat2[a2] = statg2[...]

    def stat2_copy(k):
        return remote(statg2, stat2.at[a2], s2_send.at[k], s2_recv.at[a2], second_peer((a2 + k) % 4))

    for k in range(1, 4):
        launch(stat2_copy(k))
    def stat3_copy(k):
        return remote(statg3, stat3.at[z], s3_send.at[k], s3_recv.at[z], z_peer((z + k) % NZ))

    def between(stat, members):
        group = stat[0]
        for k in range(1, members):
            group = group + stat[k]
        mean = group[0:1, :] / jnp.maximum(group[1:2, :], 1.0)
        for k in range(members):
            spread[k : k + 1, :] = stat[k, 0:1, :] / jnp.maximum(stat[k, 1:2, :], 1.0) - mean
        spread_t[...] = jnp.transpose(spread[...])
        for k in range(members):
            spread[k : k + 1, :] = spread[k : k + 1, :] * stat[k, 1:2, :]
        return group

    def outer(rows):
        return jnp.dot(rows, spread[...], preferred_element_type=jnp.float32, precision=lax.Precision.HIGHEST)

    spread[...] = jnp.zeros_like(spread)
    between(stat1, 4)
    for g in range(8):
        gown[g * GROUP : (g + 1) * GROUP, :] += outer(spread_t[pl.ds(group_start(a1, g), GROUP), :])

    def h_copy(k):
        to = (a2 + k) % 4
        return remote(hsend.at[to], hrecv.at[a2], h_send.at[k], h_recv.at[a2], second_peer(to))

    for j in (1, 2, 3, 0):
        sub = (a2 + j) % 4
        rows = pl.ds(pl.multiple_of(sub * SUB_ROWS, SUB_ROWS), SUB_ROWS)
        for k in range(1, 4):
            source = (a1 + k) % 4
            remote(
                gsend.at[source, rows, :], grecv.at[source, rows, :], g_send.at[k, sub], g_recv.at[source, sub],
                first_peer(source),
            ).wait_recv()
        value = gown[rows, :]
        for k in range(1, 4):
            value = value + grecv[(a1 + k) % 4, rows, :].astype(jnp.float32)
        if j:
            hsend[sub] = value.astype(jnp.bfloat16)
            launch(h_copy(j))
        else:
            hown[...] = value

    for k in range(1, 4):
        source = (a2 + k) % 4
        remote(statg2, stat2.at[source], s2_send.at[k], s2_recv.at[source], second_peer(source)).wait_recv()
    statg3[...] = stat2[0] + stat2[1] + stat2[2] + stat2[3]
    stat3[z] = statg3[...]
    for k in range(1, NZ):
        launch(stat3_copy(k))
    between(stat2, 4)
    for core in range(CORES):
        hown[core * GROUP : (core + 1) * GROUP, :] += outer(
            spread_t[pl.ds(group_start(a1, a2 * CORES + core), GROUP), :]
        )
    for k in range(1, 4):
        source = (a2 + k) % 4
        remote(hsend.at[source], hrecv.at[source], h_send.at[k], h_recv.at[source], second_peer(source)).wait_recv()
    value = hown[...]
    for k in range(1, 4):
        value = value + hrecv[(a2 + k) % 4].astype(jnp.float32)
    hown[...] = value
    own_rows = GROUP // NZ

    for other_z in range(NZ):
        rows = jnp.concatenate(
            [hown[core * GROUP + other_z * own_rows : core * GROUP + (other_z + 1) * own_rows, :] for core in range(CORES)],
            axis=0,
        )
        tsend[other_z] = rows.astype(jnp.bfloat16)

    def t_copy(k):
        to = (z + k) % NZ
        return remote(tsend.at[to], trecv.at[z], t_send.at[k], t_recv.at[z], z_peer(to))

    for k in range(1, NZ):
        launch(t_copy(k))
    for k in range(1, NZ):
        source = (z + k) % NZ
        remote(statg3, stat3.at[source], s3_send.at[k], s3_recv.at[source], z_peer(source)).wait_recv()
    counts = between(stat3, NZ)[1:2, :]
    halves = [
        spread_t[pl.ds(pl.multiple_of(group_start(a1, a2 * CORES + core) + z // 2 * 8, 8), 8), :] for core in range(CORES)
    ]
    even = z % 2 == 0
    value = tsend[z].astype(jnp.float32) + outer(
        jnp.concatenate([jnp.where(even, half[0:own_rows], half[own_rows : 2 * own_rows]) for half in halves], axis=0)
    )
    for k in range(1, NZ):
        source = (z + k) % NZ
        remote(tsend.at[source], trecv.at[source], t_send.at[k], t_recv.at[source], z_peer(source)).wait_recv()
        value = value + trecv[source].astype(jnp.float32)
    value = value / counts

    low, high = value[0:own_rows, :], value[own_rows : 2 * own_rows, :]
    fsend[...] = jnp.where(c == 0, high, low)
    last = remote(fsend, frecv, f_send, f_recv, sibling)
    launch(last)
    out[c] = jnp.where(c == 0, low, high)
    last.wait_recv()
    out[1 - c] = frecv[...]

    finish()


def shards(frames, dead_time, band_width, cycle_label, valid):
    rows = NPIX_GROUP // LANES
    flat = [a.reshape(rows, LANES) for a in (dead_time, band_width, cycle_label, valid)]
    own_rows = GROUP // NZ
    dma = pltpu.SemaphoreType.DMA
    f32, bf16 = jnp.float32, jnp.bfloat16
    any_space = pl.BlockSpec(memory_space=pltpu.HBM)
    vmem = pltpu.VMEM
    out = pl.pallas_call(
        kernel,
        out_shape=jax.ShapeDtypeStruct((CYCLES, own_rows, NFRAMES), f32),
        in_specs=[any_space] * 5,
        out_specs=pl.BlockSpec(memory_space=pltpu.VMEM),
        scratch_shapes=[
            vmem((rows, LANES), f32),
            vmem((rows, LANES), jnp.int32),
            vmem((rows, LANES), jnp.int32),
            vmem((rows, LANES), jnp.int32),
            vmem((CHUNKS, NDEV_FRAME, OWN_FRAMES, LANES), bf16),
            vmem((PAD + NFRAMES + PAD, LANES), f32),
            vmem((NFRAMES, CHIP_PIX), bf16),
            vmem((CHUNKS, NFRAMES, LANES), bf16),
            vmem((NFRAMES, NFRAMES), f32),
            vmem((8, NFRAMES), f32),
            vmem((NFRAMES, 8), f32),
            vmem((4, CLASS_ROWS, NFRAMES), bf16),
            vmem((4, CLASS_ROWS, NFRAMES), bf16),
            vmem((CLASS_ROWS, NFRAMES), f32),
            vmem((4, SUB_ROWS, NFRAMES), bf16),
            vmem((4, SUB_ROWS, NFRAMES), bf16),
            vmem((SUB_ROWS, NFRAMES), f32),
            vmem((NZ, CORES * own_rows, NFRAMES), bf16),
            vmem((NZ, CORES * own_rows, NFRAMES), bf16),
            vmem((4, 2, NFRAMES), f32),
            vmem((4, 2, NFRAMES), f32),
            vmem((NZ, 2, NFRAMES), f32),
            vmem((2, NFRAMES), f32),
            vmem((2, NFRAMES), f32),
            vmem((8, NFRAMES), f32),
            vmem((NFRAMES, 8), f32),
            vmem((own_rows, NFRAMES), f32),
            vmem((own_rows, NFRAMES), f32),
            dma((4,)),
            dma((CHUNKS,)),
            dma((CHUNKS, NDEV_FRAME)), dma((CHUNKS, NDEV_FRAME)),
            dma((CHUNKS,)), dma((CHUNKS,)),
            dma((4,)), dma((4,)),
            dma((4,)), dma((4,)),
            dma((NZ,)), dma((NZ,)),
            dma((4, 4)), dma((4, 4)),
            dma((4,)), dma((4,)),
            dma((NZ,)), dma((NZ,)),
            dma, dma,
        ],
        compiler_params=pltpu.CompilerParams(
            collective_id=0, has_side_effects=True, vmem_limit_bytes=60 * 2**20
        ),
    )(frames, *flat)
    return jnp.transpose(out, (1, 0, 2))


def solution(mesh):
    in_specs = (P("frame", "pixel"), P("pixel"), P("pixel"), P("pixel"), P("pixel"))
    out_specs = P(("frame", "pixel"), None, None)
    return jax.shard_map(shards, mesh=mesh, in_specs=in_specs, out_specs=out_specs, check_vma=False)
```

```python
import functools

import jax
import jax.numpy as jnp
from jax import lax
from jax.experimental import pallas as pl
from jax.experimental.pallas import tpu as pltpu
from jax.sharding import PartitionSpec as P

MESH = pl.DeviceIdType.MESH
CYCLES = 2
BAND = 8
CORES = 2
NX = 4
NY = 4
NZ = 8
LANES = 128
GROUP = 32
NFRAMES = 1024
NDEV_FRAME = NX * CORES
OWN_FRAMES = NFRAMES // NDEV_FRAME
NPIX_GROUP = 4096
OWN_PIX = NPIX_GROUP // NDEV_FRAME
CHUNKS = OWN_PIX // LANES
CHIP_PIX = CORES * OWN_PIX
CLASS_ROWS = NFRAMES // 4
SUB_ROWS = CLASS_ROWS // 4
PAD = BAND
TILE = 256
HELD = 640


def remote(src, dst, send_sem, recv_sem, device):
    return pltpu.make_async_remote_copy(
        src_ref=src,
        dst_ref=dst,
        send_sem=send_sem,
        recv_sem=recv_sem,
        device_id=device,
        device_id_type=MESH,
    )


def kernel(
    frames, dead_hbm, band_hbm, label_hbm, valid_hbm,
    out,
    dead, band, label, valid, arrived, rate, smooth, outgoing,
    gram, sums_ref, sums_t, gsend, grecv, gown, hsend, hrecv, hown, tsend, trecv,
    stat1, stat2, stat3, statg2, statg3, spread, spread_t,
    fsend, frecv, m1_out, m1_in, m2_out, m2_in, permuted, ordered,
    par_sem, own_sem, a2a_send, a2a_recv, sib_send, sib_recv,
    s1_send, s1_recv, s2_send, s2_recv, s3_send, s3_recv,
    g_send, g_recv, h_send, h_recv, t_send, t_recv, f_send, f_recv,
    m1_send, m1_recv, m2_send, m2_recv,
):
    f = lax.axis_index("frame")
    p = lax.axis_index("pixel")
    x, c = f // CORES, f % CORES
    y, z = p // NZ, p % NZ
    a1 = c * x + (1 - c) * y
    a2 = c * y + (1 - c) * x

    def peer(a, b):
        return ((c * a + (1 - c) * b) * CORES + c, (c * b + (1 - c) * a) * NZ + z)

    def first_peer(a):
        return peer(a, a2)

    def second_peer(b):
        return peer(a1, b)

    def z_peer(other):
        return (f, y * NZ + other)

    def frame_peer(other):
        return (other, p)

    sibling = (x * CORES + (1 - c), p)

    pending = []

    def launch(copy):
        copy.start()
        pending.append(copy)

    def finish():
        for copy in pending:
            copy.wait_send()

    barrier = pltpu.get_barrier_semaphore()
    for k in range(1, NDEV_FRAME):
        pl.semaphore_signal(barrier, inc=1, device_id=frame_peer((f + k) % NDEV_FRAME), device_id_type=MESH)
    for k in range(1, NY):
        pl.semaphore_signal(barrier, inc=1, device_id=(f, ((y + k) % NY) * NZ + z), device_id_type=MESH)
    for k in range(1, NZ):
        pl.semaphore_signal(barrier, inc=1, device_id=z_peer((z + k) % NZ), device_id_type=MESH)
    for k in range(1, 4):
        for n in range(1, 4):
            pl.semaphore_signal(barrier, inc=1, device_id=peer((a1 + k) % 4, (a2 + n) % 4), device_id_type=MESH)
    pl.semaphore_wait(barrier, NDEV_FRAME - 1 + NY - 1 + NZ - 1 + 9)

    def piece(owner, chunk):
        return frames.at[:, pl.ds(pl.multiple_of(owner * OWN_PIX + chunk * LANES, LANES), LANES)]

    def a2a_copy(k, chunk):
        to = (f + k) % NDEV_FRAME
        return remote(
            piece(to, chunk), arrived.at[chunk, f], a2a_send.at[chunk, k], a2a_recv.at[chunk, f], frame_peer(to)
        )

    def own_copy(chunk):
        return pltpu.make_async_copy(piece(f, chunk), arrived.at[chunk, f], own_sem.at[chunk])

    for chunk in range(CHUNKS):
        for k in range(1, NDEV_FRAME):
            launch(a2a_copy(k, chunk))
        own_copy(chunk).start()
    params = [
        pltpu.make_async_copy(src, dst, par_sem.at[n])
        for n, (src, dst) in enumerate(
            ((dead_hbm, dead), (band_hbm, band), (label_hbm, label), (valid_hbm, valid))
        )
    ]
    for copy in params:
        copy.start()
    rate[0:PAD, :] = jnp.zeros((PAD, LANES), jnp.float32)
    rate[PAD + NFRAMES : PAD + NFRAMES + PAD, :] = jnp.zeros((PAD, LANES), jnp.float32)
    for copy in params:
        copy.wait()

    def sib_copy(chunk):
        return remote(
            outgoing.at[chunk],
            smooth.at[:, pl.ds((2 * chunk + 1) * LANES, LANES)],
            sib_send.at[chunk],
            sib_recv.at[chunk],
            sibling,
        )

    contract_last = (((1,), (1,)), ((), ()))

    def accumulate(chunk):
        lanes = slice(2 * chunk * LANES, 2 * (chunk + 1) * LANES)
        sib_copy(chunk).wait_recv()
        part = lax.dot_general(
            jnp.ones((8, 2 * LANES), jnp.bfloat16), smooth[:, lanes], contract_last, preferred_element_type=jnp.float32
        )
        sums_ref[...] = part if chunk == 0 else sums_ref[...] + part

        for m in range(4):
            for n in (m, (m + 1) % 4, (m + 2) % 4):
                rows, cols = slice(m * TILE, (m + 1) * TILE), slice(n * TILE, (n + 1) * TILE)
                product = lax.dot_general(
                    smooth[rows, lanes], smooth[cols, lanes], contract_last, preferred_element_type=jnp.float32
                )
                gram[rows, cols] = product if chunk == 0 else gram[rows, cols] + product

    for chunk in range(CHUNKS):
        own_copy(chunk).wait()
        for k in range(1, NDEV_FRAME):
            source = (f + k) % NDEV_FRAME
            remote(
                piece(source, chunk), arrived.at[chunk, source], a2a_send.at[chunk, k],
                a2a_recv.at[chunk, source], frame_peer(source),
            ).wait_recv()
        row = f * CHUNKS + chunk
        dead_row = dead[pl.ds(row, 1), :]
        width = band[pl.ds(row, 1), :]
        cycle = label[pl.ds(row, 1), :]
        used = valid[pl.ds(row, 1), :] == 1
        mine = jnp.where(used & (cycle == c), 1.0, 0.0)
        other = jnp.where(used & (cycle == 1 - c), 1.0, 0.0)
        within = [jnp.where(width >= k, 1.0, 0.0) for k in range(1, BAND + 1)]
        full = 1.0 / (2 * width + 1).astype(jnp.float32)

        def correct(block, _):
            for half in range(OWN_FRAMES // GROUP):
                count = 4.0 + arrived[chunk, block, half * GROUP : (half + 1) * GROUP, :].astype(jnp.float32)
                rate[pl.ds(pl.multiple_of(PAD + block * OWN_FRAMES + half * GROUP, 8), GROUP), :] = count / (
                    1.0 - dead_row * count
                )
            return 0

        lax.fori_loop(0, NDEV_FRAME, correct, 0)

        def window(start):
            total = rate[pl.ds(start + PAD, GROUP), :]
            for k in range(1, BAND + 1):
                total = total + within[k - 1] * (
                    rate[pl.ds(start + PAD - k, GROUP), :] + rate[pl.ds(start + PAD + k, GROUP), :]
                )
            return total

        def put(block, value):
            row_x, core, row_y = block // 8, block // 4 % 2, block % 4
            along_x, along_y = row_x * 8 + row_y * 2 + core, row_y * 8 + row_x * 2 + core
            own_rows = pl.ds(pl.multiple_of((c * along_x + (1 - c) * along_y) * GROUP, GROUP), GROUP)
            sib_rows = pl.ds(pl.multiple_of((c * along_y + (1 - c) * along_x) * GROUP, GROUP), GROUP)
            smooth[own_rows, 2 * chunk * LANES : (2 * chunk + 1) * LANES] = (value * mine).astype(jnp.bfloat16)
            outgoing[chunk, sib_rows, :] = (value * other).astype(jnp.bfloat16)

        def inside(block, _):
            put(block, window(pl.multiple_of(block * GROUP, GROUP)) * full)
            return 0

        for start in (0, NFRAMES - GROUP):
            frame = start + lax.broadcasted_iota(jnp.int32, (GROUP, LANES), 0)
            span = jnp.minimum(frame + width, NFRAMES - 1) - jnp.maximum(frame - width, 0) + 1
            put(start // GROUP, window(start) / span.astype(jnp.float32))
        lax.fori_loop(1, NFRAMES // GROUP - 1, inside, 0)
        launch(sib_copy(chunk))
        if chunk:
            accumulate(chunk - 1)

    chip_label = label[pl.ds(pl.multiple_of(x * (CHIP_PIX // LANES), 8), CHIP_PIX // LANES), :]
    chip_valid = valid[pl.ds(pl.multiple_of(x * (CHIP_PIX // LANES), 8), CHIP_PIX // LANES), :]
    held = jnp.sum(jnp.where((chip_label == c) & (chip_valid == 1), 1.0, 0.0), axis=(0, 1), keepdims=True)

    accumulate(CHUNKS - 1)
    sums_t[...] = jnp.transpose(sums_ref[...] / jnp.maximum(held, 1.0))
    stat1[a1, 0:1, :] = sums_ref[0:1, :]
    stat1[a1, 1:2, :] = jnp.broadcast_to(held, (1, NFRAMES))

    def stat1_copy(k):
        to = (a1 + k) % 4
        return remote(stat1.at[a1], stat1.at[a1], s1_send.at[k], s1_recv.at[a1], first_peer(to))

    for k in range(1, 4):
        launch(stat1_copy(k))

    def lane(a, half):
        return pl.ds(pl.multiple_of(((a1 + a) % 4 * 2 + half) * LANES, LANES), LANES)

    def other_half(a, half):
        high = a // 2
        return (1 - half) * high + half * (1 - high)

    def g_copy(k, sub):
        to = (a1 + k) % 4
        rows = pl.ds(pl.multiple_of(sub * SUB_ROWS, SUB_ROWS), SUB_ROWS)
        return remote(
            gsend.at[to, rows, :], grecv.at[a1, rows, :], g_send.at[k, sub], g_recv.at[a1, sub], first_peer(to)
        )

    for k in (1, 2, 3, 0):
        to = (a1 + k) % 4
        for half in range(2):
            start = pl.multiple_of(to * CLASS_ROWS + half * LANES, LANES)
            column = jnp.broadcast_to(sums_t[pl.ds(start, LANES), 0:1], (LANES, LANES))
            rows = slice(half * LANES, (half + 1) * LANES)
            held_lanes = [lane(k, 0), lane(k, 1), lane(k + 1, 0), lane(k + 1, 1), lane(k + 2, other_half(to, half))]
            for n, cols in enumerate(held_lanes):
                centred = gram[pl.ds(start, LANES), cols] - column * sums_ref[0:1, cols]
                if k:
                    gsend[to, rows, n * LANES : (n + 1) * LANES] = centred.astype(jnp.bfloat16)
                else:
                    gown[rows, n * LANES : (n + 1) * LANES] = centred

    for j in (1, 2, 3, 0):
        for k in (2, 1, 3):
            launch(g_copy(k, (a2 + j) % 4))
    for k in range(1, 4):
        source = (a1 + k) % 4
        remote(stat1.at[source], stat1.at[source], s1_send.at[k], s1_recv.at[source], first_peer(source)).wait_recv()
    statg2[...] = stat1[0] + stat1[1] + stat1[2] + stat1[3]
    stat2[a2] = statg2[...]

    def stat2_copy(k):
        return remote(statg2, stat2.at[a2], s2_send.at[k], s2_recv.at[a2], second_peer((a2 + k) % 4))

    for k in range(1, 4):
        launch(stat2_copy(k))
    def stat3_copy(k):
        return remote(statg3, stat3.at[z], s3_send.at[k], s3_recv.at[z], z_peer((z + k) % NZ))

    def between(stat, members):
        group = stat[0]
        for k in range(1, members):
            group = group + stat[k]
        mean = group[0:1, :] / jnp.maximum(group[1:2, :], 1.0)
        for k in range(members):
            spread[k : k + 1, :] = stat[k, 0:1, :] / jnp.maximum(stat[k, 1:2, :], 1.0) - mean
        spread_t[...] = jnp.transpose(spread[...])
        for k in range(members):
            spread[k : k + 1, :] = spread[k : k + 1, :] * stat[k, 1:2, :]
        return group

    def outer(rows, cols):
        return jnp.dot(rows, spread[:, cols], preferred_element_type=jnp.float32, precision=lax.Precision.HIGHEST)

    spread[...] = jnp.zeros_like(spread)
    between(stat1, 4)
    own_start = pl.multiple_of(a1 * CLASS_ROWS, CLASS_ROWS)
    for n in range(4):
        gown[:, n * LANES : (n + 1) * LANES] += outer(spread_t[pl.ds(own_start, CLASS_ROWS), :], lane(n // 2, n % 2))
    for half in range(2):
        gown[half * LANES : (half + 1) * LANES, 4 * LANES :] += outer(
            spread_t[pl.ds(own_start + half * LANES, LANES), :], lane(2, other_half(a1, half))
        )

    def h_copy(k):
        to = (a2 + k) % 4
        return remote(hsend.at[to], hrecv.at[a2], h_send.at[k], h_recv.at[a2], second_peer(to))

    for j in (1, 2, 3, 0):
        sub = (a2 + j) % 4
        rows = pl.ds(pl.multiple_of(sub * SUB_ROWS, SUB_ROWS), SUB_ROWS)
        for k in range(1, 4):
            source = (a1 + k) % 4
            remote(
                gsend.at[source, rows, :], grecv.at[source, rows, :], g_send.at[k, sub], g_recv.at[source, sub],
                first_peer(source),
            ).wait_recv()
        value = gown[rows, :]
        for k in range(1, 4):
            value = value + grecv[(a1 + k) % 4, rows, :].astype(jnp.float32)
        gown[rows, :] = value
        if j:
            hsend[sub] = value.astype(jnp.bfloat16)
            launch(h_copy(j))

    def mirror_copy(n):
        return remote(
            m1_out.at[n], m1_in.at[a2], m1_send.at[n], m1_recv.at[a2], peer((a1 + 1) % 4, n)
        )

    def half_copy(n):
        return remote(
            m2_out.at[n], m2_in.at[a2], m2_send.at[n], m2_recv.at[a2], peer((a1 + 2) % 4, n)
        )

    mirror = jnp.transpose(gown[:, 2 * LANES : 4 * LANES]).astype(jnp.bfloat16)
    for n in range(4):
        m1_out[n] = mirror[n * SUB_ROWS : (n + 1) * SUB_ROWS, :]
        launch(mirror_copy(n))
    for half in range(2):
        mirror = jnp.transpose(gown[half * LANES : (half + 1) * LANES, 4 * LANES :]).astype(jnp.bfloat16)
        for n in range(2):
            m2_out[other_half(a1, half) * 2 + n] = mirror[n * SUB_ROWS : (n + 1) * SUB_ROWS, :]
    for n in range(4):
        launch(half_copy(n))

    for k in range(1, 4):
        source = (a2 + k) % 4
        remote(statg2, stat2.at[source], s2_send.at[k], s2_recv.at[source], second_peer(source)).wait_recv()
    statg3[...] = stat2[0] + stat2[1] + stat2[2] + stat2[3]
    stat3[z] = statg3[...]
    for k in range(1, NZ):
        launch(stat3_copy(k))
    between(stat2, 4)
    row_start = pl.multiple_of(a1 * CLASS_ROWS + a2 * SUB_ROWS, SUB_ROWS)
    hown[...] = outer(spread_t[pl.ds(row_start, SUB_ROWS), :], slice(None))
    for k in range(1, 4):
        source = (a2 + k) % 4
        remote(hsend.at[source], hrecv.at[source], h_send.at[k], h_recv.at[source], second_peer(source)).wait_recv()
    value = gown[pl.ds(pl.multiple_of(a2 * SUB_ROWS, SUB_ROWS), SUB_ROWS), :]
    for k in range(1, 4):
        value = value + hrecv[(a2 + k) % 4].astype(jnp.float32)
    own_half = other_half(a1, a2 // 2)
    for n, cols in enumerate((lane(0, 0), lane(0, 1), lane(1, 0), lane(1, 1), lane(2, own_half))):
        hown[:, cols] += value[:, n * LANES : (n + 1) * LANES]
    for n in range(4):
        remote(m1_out.at[n], m1_in.at[n], m1_send.at[n], m1_recv.at[n], peer((a1 + 3) % 4, n)).wait_recv()
    value = m1_in[0].astype(jnp.float32)
    for n in range(1, 4):
        value = value + m1_in[n].astype(jnp.float32)
    hown[:, lane(3, 0)] += value[:, 0:LANES]
    hown[:, lane(3, 1)] += value[:, LANES:]
    for n in range(4):
        remote(m2_out.at[n], m2_in.at[n], m2_send.at[n], m2_recv.at[n], peer((a1 + 2) % 4, n)).wait_recv()
    value = m2_in[0].astype(jnp.float32)
    for n in range(1, 4):
        value = value + m2_in[n].astype(jnp.float32)
    hown[:, lane(2, 1 - own_half)] += value
    own_rows = GROUP // NZ

    for other_z in range(NZ):
        rows = jnp.concatenate(
            [hown[core * GROUP + other_z * own_rows : core * GROUP + (other_z + 1) * own_rows, :] for core in range(CORES)],
            axis=0,
        )
        tsend[other_z] = rows.astype(jnp.bfloat16)

    def t_copy(k):
        to = (z + k) % NZ
        return remote(tsend.at[to], trecv.at[z], t_send.at[k], t_recv.at[z], z_peer(to))

    for k in range(1, NZ):
        launch(t_copy(k))
    for k in range(1, NZ):
        source = (z + k) % NZ
        remote(statg3, stat3.at[source], s3_send.at[k], s3_recv.at[source], z_peer(source)).wait_recv()
    counts = between(stat3, NZ)[1:2, :]
    halves = [
        spread_t[pl.ds(pl.multiple_of(row_start + core * GROUP + z // 2 * 8, 8), 8), :] for core in range(CORES)
    ]
    even = z % 2 == 0
    value = tsend[z].astype(jnp.float32) + outer(
        jnp.concatenate([jnp.where(even, half[0:own_rows], half[own_rows : 2 * own_rows]) for half in halves], axis=0),
        slice(None),
    )
    for k in range(1, NZ):
        source = (z + k) % NZ
        remote(tsend.at[source], trecv.at[source], t_send.at[k], t_recv.at[source], z_peer(source)).wait_recv()
        value = value + trecv[source].astype(jnp.float32)
    permuted[...] = value / counts
    place = lax.broadcasted_iota(jnp.int32, (CORES * own_rows, LANES), 1) // GROUP
    for row_x in range(4):
        for core in range(CORES):
            piece_of = None
            for row_y in range(4):
                first, second = c * row_x + (1 - c) * row_y, c * row_y + (1 - c) * row_x
                block = pl.ds(pl.multiple_of((first * 2 + second // 2) * LANES, LANES), LANES)
                shift = (row_y * GROUP + LANES - (second % 2 * 2 + core) * GROUP) % LANES
                moved = pltpu.roll(permuted[:, block], shift, 1)
                piece_of = moved if piece_of is None else jnp.where(place == row_y, moved, piece_of)
            block = (row_x * CORES + core) * LANES
            ordered[:, block : block + LANES] = piece_of
    value = ordered[...]

    low, high = value[0:own_rows, :], value[own_rows : 2 * own_rows, :]
    fsend[...] = jnp.where(c == 0, high, low)
    last = remote(fsend, frecv, f_send, f_recv, sibling)
    launch(last)
    out[c] = jnp.where(c == 0, low, high)
    last.wait_recv()
    out[1 - c] = frecv[...]

    finish()


def shards(frames, dead_time, band_width, cycle_label, valid):
    rows = NPIX_GROUP // LANES
    flat = [a.reshape(rows, LANES) for a in (dead_time, band_width, cycle_label, valid)]
    own_rows = GROUP // NZ
    dma = pltpu.SemaphoreType.DMA
    f32, bf16 = jnp.float32, jnp.bfloat16
    any_space = pl.BlockSpec(memory_space=pltpu.HBM)
    vmem = pltpu.VMEM
    out = pl.pallas_call(
        kernel,
        out_shape=jax.ShapeDtypeStruct((CYCLES, own_rows, NFRAMES), f32),
        in_specs=[any_space] * 5,
        out_specs=pl.BlockSpec(memory_space=pltpu.VMEM),
        scratch_shapes=[
            vmem((rows, LANES), f32),
            vmem((rows, LANES), jnp.int32),
            vmem((rows, LANES), jnp.int32),
            vmem((rows, LANES), jnp.int32),
            vmem((CHUNKS, NDEV_FRAME, OWN_FRAMES, LANES), bf16),
            vmem((PAD + NFRAMES + PAD, LANES), f32),
            vmem((NFRAMES, CHIP_PIX), bf16),
            vmem((CHUNKS, NFRAMES, LANES), bf16),
            vmem((NFRAMES, NFRAMES), f32),
            vmem((8, NFRAMES), f32),
            vmem((NFRAMES, 8), f32),
            vmem((4, CLASS_ROWS, HELD), bf16),
            vmem((4, CLASS_ROWS, HELD), bf16),
            vmem((CLASS_ROWS, HELD), f32),
            vmem((4, SUB_ROWS, HELD), bf16),
            vmem((4, SUB_ROWS, HELD), bf16),
            vmem((SUB_ROWS, NFRAMES), f32),
            vmem((NZ, CORES * own_rows, NFRAMES), bf16),
            vmem((NZ, CORES * own_rows, NFRAMES), bf16),
            vmem((4, 2, NFRAMES), f32),
            vmem((4, 2, NFRAMES), f32),
            vmem((NZ, 2, NFRAMES), f32),
            vmem((2, NFRAMES), f32),
            vmem((2, NFRAMES), f32),
            vmem((8, NFRAMES), f32),
            vmem((NFRAMES, 8), f32),
            vmem((own_rows, NFRAMES), f32),
            vmem((own_rows, NFRAMES), f32),
            vmem((4, SUB_ROWS, 2 * LANES), bf16), vmem((4, SUB_ROWS, 2 * LANES), bf16),
            vmem((4, SUB_ROWS, LANES), bf16), vmem((4, SUB_ROWS, LANES), bf16),
            vmem((CORES * own_rows, NFRAMES), f32),
            vmem((CORES * own_rows, NFRAMES), f32),
            dma((4,)),
            dma((CHUNKS,)),
            dma((CHUNKS, NDEV_FRAME)), dma((CHUNKS, NDEV_FRAME)),
            dma((CHUNKS,)), dma((CHUNKS,)),
            dma((4,)), dma((4,)),
            dma((4,)), dma((4,)),
            dma((NZ,)), dma((NZ,)),
            dma((4, 4)), dma((4, 4)),
            dma((4,)), dma((4,)),
            dma((NZ,)), dma((NZ,)),
            dma, dma,
            dma((4,)), dma((4,)),
            dma((4,)), dma((4,)),
        ],
        compiler_params=pltpu.CompilerParams(
            collective_id=0, has_side_effects=True, vmem_limit_bytes=60 * 2**20
        ),
    )(frames, *flat)
    return jnp.transpose(out, (1, 0, 2))


def solution(mesh):
    in_specs = (P("frame", "pixel"), P("pixel"), P("pixel"), P("pixel"), P("pixel"))
    out_specs = P(("frame", "pixel"), None, None)
    return jax.shard_map(shards, mesh=mesh, in_specs=in_specs, out_specs=out_specs, check_vma=False)
```

```python
import functools

import jax
import jax.numpy as jnp
from jax import lax
from jax.experimental import pallas as pl
from jax.experimental.pallas import tpu as pltpu
from jax.sharding import PartitionSpec as P

MESH = pl.DeviceIdType.MESH
CYCLES = 2
BAND = 8
CORES = 2
NX = 4
NY = 4
NZ = 8
LANES = 128
GROUP = 32
NFRAMES = 1024
NDEV_FRAME = NX * CORES
OWN_FRAMES = NFRAMES // NDEV_FRAME
NPIX_GROUP = 4096
OWN_PIX = NPIX_GROUP // NDEV_FRAME
CHUNKS = OWN_PIX // LANES
CHIP_PIX = CORES * OWN_PIX
CLASS_ROWS = NFRAMES // 4
SUB_ROWS = CLASS_ROWS // 4
PAD = BAND
TILE = 256
HELD = 640


def remote(src, dst, send_sem, recv_sem, device):
    return pltpu.make_async_remote_copy(
        src_ref=src,
        dst_ref=dst,
        send_sem=send_sem,
        recv_sem=recv_sem,
        device_id=device,
        device_id_type=MESH,
    )


def kernel(
    frames, dead_hbm, band_hbm, label_hbm, valid_hbm,
    out,
    dead, band, label, valid, arrived, rate, smooth, outgoing,
    gram, sums_ref, sums_t, gsend, grecv, gown, hsend, hrecv, hown, tsend, trecv, usend, urecv,
    stat1, stat2, stat3, statg2, statg3, spread, spread_t,
    fsend, frecv, m1_out, m1_in, m2_out, m2_in, permuted, ordered,
    par_sem, own_sem, a2a_send, a2a_recv, sib_send, sib_recv,
    s1_send, s1_recv, s2_send, s2_recv, s3_send, s3_recv,
    g_send, g_recv, h_send, h_recv, t_send, t_recv, f_send, f_recv,
    m1_send, m1_recv, m2_send, m2_recv,
):
    f = lax.axis_index("frame")
    p = lax.axis_index("pixel")
    x, c = f // CORES, f % CORES
    y, z = p // NZ, p % NZ
    a1 = c * x + (1 - c) * y
    a2 = c * y + (1 - c) * x

    def peer(a, b):
        return ((c * a + (1 - c) * b) * CORES + c, (c * b + (1 - c) * a) * NZ + z)

    def first_peer(a):
        return peer(a, a2)

    def second_peer(b):
        return peer(a1, b)

    def z_peer(other):
        return (f, y * NZ + other)

    def frame_peer(other):
        return (other, p)

    sibling = (x * CORES + (1 - c), p)

    pending = []

    def launch(copy):
        copy.start()
        pending.append(copy)

    def finish():
        for copy in pending:
            copy.wait_send()

    barrier = pltpu.get_barrier_semaphore()
    for k in range(1, NDEV_FRAME):
        pl.semaphore_signal(barrier, inc=1, device_id=frame_peer((f + k) % NDEV_FRAME), device_id_type=MESH)
    for k in range(1, NY):
        pl.semaphore_signal(barrier, inc=1, device_id=(f, ((y + k) % NY) * NZ + z), device_id_type=MESH)
    for k in range(1, NZ):
        pl.semaphore_signal(barrier, inc=1, device_id=z_peer((z + k) % NZ), device_id_type=MESH)
    for k in range(1, 4):
        for n in range(1, 4):
            pl.semaphore_signal(barrier, inc=1, device_id=peer((a1 + k) % 4, (a2 + n) % 4), device_id_type=MESH)
    pl.semaphore_wait(barrier, NDEV_FRAME - 1 + NY - 1 + NZ - 1 + 9)

    def piece(owner, chunk):
        return frames.at[:, pl.ds(pl.multiple_of(owner * OWN_PIX + chunk * LANES, LANES), LANES)]

    def a2a_copy(k, chunk):
        to = (f + k) % NDEV_FRAME
        return remote(
            piece(to, chunk), arrived.at[chunk, f], a2a_send.at[chunk, k], a2a_recv.at[chunk, f], frame_peer(to)
        )

    def own_copy(chunk):
        return pltpu.make_async_copy(piece(f, chunk), arrived.at[chunk, f], own_sem.at[chunk])

    for chunk in range(CHUNKS):
        for k in range(1, NDEV_FRAME):
            launch(a2a_copy(k, chunk))
        own_copy(chunk).start()
    params = [
        pltpu.make_async_copy(src, dst, par_sem.at[n])
        for n, (src, dst) in enumerate(
            ((dead_hbm, dead), (band_hbm, band), (label_hbm, label), (valid_hbm, valid))
        )
    ]
    for copy in params:
        copy.start()
    rate[0:PAD, :] = jnp.zeros((PAD, LANES), jnp.float32)
    rate[PAD + NFRAMES : PAD + NFRAMES + PAD, :] = jnp.zeros((PAD, LANES), jnp.float32)
    for copy in params:
        copy.wait()

    def sib_copy(chunk):
        return remote(
            outgoing.at[chunk],
            smooth.at[:, pl.ds((2 * chunk + 1) * LANES, LANES)],
            sib_send.at[chunk],
            sib_recv.at[chunk],
            sibling,
        )

    contract_last = (((1,), (1,)), ((), ()))

    def accumulate(chunk):
        lanes = slice(2 * chunk * LANES, 2 * (chunk + 1) * LANES)
        sib_copy(chunk).wait_recv()
        part = lax.dot_general(
            jnp.ones((8, 2 * LANES), jnp.bfloat16), smooth[:, lanes], contract_last, preferred_element_type=jnp.float32
        )
        sums_ref[...] = part if chunk == 0 else sums_ref[...] + part

        for m in range(4):
            for n in (m, (m + 1) % 4, (m + 2) % 4):
                rows, cols = slice(m * TILE, (m + 1) * TILE), slice(n * TILE, (n + 1) * TILE)
                product = lax.dot_general(
                    smooth[rows, lanes], smooth[cols, lanes], contract_last, preferred_element_type=jnp.float32
                )
                gram[rows, cols] = product if chunk == 0 else gram[rows, cols] + product

    for chunk in range(CHUNKS):
        own_copy(chunk).wait()
        for k in range(1, NDEV_FRAME):
            source = (f + k) % NDEV_FRAME
            remote(
                piece(source, chunk), arrived.at[chunk, source], a2a_send.at[chunk, k],
                a2a_recv.at[chunk, source], frame_peer(source),
            ).wait_recv()
        row = f * CHUNKS + chunk
        dead_row = dead[pl.ds(row, 1), :]
        width = band[pl.ds(row, 1), :]
        cycle = label[pl.ds(row, 1), :]
        used = valid[pl.ds(row, 1), :] == 1
        mine = jnp.where(used & (cycle == c), 1.0, 0.0)
        other = jnp.where(used & (cycle == 1 - c), 1.0, 0.0)
        within = [jnp.where(width >= k, 1.0, 0.0) for k in range(1, BAND + 1)]
        full = 1.0 / (2 * width + 1).astype(jnp.float32)

        def correct(block, _):
            for half in range(OWN_FRAMES // GROUP):
                count = 4.0 + arrived[chunk, block, half * GROUP : (half + 1) * GROUP, :].astype(jnp.float32)
                rate[pl.ds(pl.multiple_of(PAD + block * OWN_FRAMES + half * GROUP, 8), GROUP), :] = count / (
                    1.0 - dead_row * count
                )
            return 0

        lax.fori_loop(0, NDEV_FRAME, correct, 0)

        def window(start):
            total = rate[pl.ds(start + PAD, GROUP), :]
            for k in range(1, BAND + 1):
                total = total + within[k - 1] * (
                    rate[pl.ds(start + PAD - k, GROUP), :] + rate[pl.ds(start + PAD + k, GROUP), :]
                )
            return total

        def put(block, value):
            row_x, core, row_y = block // 8, block // 4 % 2, block % 4
            along_x, along_y = row_x * 8 + row_y * 2 + core, row_y * 8 + row_x * 2 + core
            own_rows = pl.ds(pl.multiple_of((c * along_x + (1 - c) * along_y) * GROUP, GROUP), GROUP)
            sib_rows = pl.ds(pl.multiple_of((c * along_y + (1 - c) * along_x) * GROUP, GROUP), GROUP)
            smooth[own_rows, 2 * chunk * LANES : (2 * chunk + 1) * LANES] = (value * mine).astype(jnp.bfloat16)
            outgoing[chunk, sib_rows, :] = (value * other).astype(jnp.bfloat16)

        def inside(block, _):
            put(block, window(pl.multiple_of(block * GROUP, GROUP)) * full)
            return 0

        for start in (0, NFRAMES - GROUP):
            frame = start + lax.broadcasted_iota(jnp.int32, (GROUP, LANES), 0)
            span = jnp.minimum(frame + width, NFRAMES - 1) - jnp.maximum(frame - width, 0) + 1
            put(start // GROUP, window(start) / span.astype(jnp.float32))
        lax.fori_loop(1, NFRAMES // GROUP - 1, inside, 0)
        launch(sib_copy(chunk))
        if chunk:
            accumulate(chunk - 1)

    chip_label = label[pl.ds(pl.multiple_of(x * (CHIP_PIX // LANES), 8), CHIP_PIX // LANES), :]
    chip_valid = valid[pl.ds(pl.multiple_of(x * (CHIP_PIX // LANES), 8), CHIP_PIX // LANES), :]
    held = jnp.sum(jnp.where((chip_label == c) & (chip_valid == 1), 1.0, 0.0), axis=(0, 1), keepdims=True)

    accumulate(CHUNKS - 1)
    sums_t[...] = jnp.transpose(sums_ref[...] / jnp.maximum(held, 1.0))
    stat1[a1, 0:1, :] = sums_ref[0:1, :]
    stat1[a1, 1:2, :] = jnp.broadcast_to(held, (1, NFRAMES))

    def stat1_copy(k):
        to = (a1 + k) % 4
        return remote(stat1.at[a1], stat1.at[a1], s1_send.at[k], s1_recv.at[a1], first_peer(to))

    for k in range(1, 4):
        launch(stat1_copy(k))

    def lane(a, half):
        return pl.ds(pl.multiple_of(((a1 + a) % 4 * 2 + half) * LANES, LANES), LANES)

    def other_half(a, half):
        high = a // 2
        return (1 - half) * high + half * (1 - high)

    def g_copy(k, sub):
        to = (a1 + k) % 4
        rows = pl.ds(pl.multiple_of(sub * SUB_ROWS, SUB_ROWS), SUB_ROWS)
        return remote(
            gsend.at[to, rows, :], grecv.at[a1, rows, :], g_send.at[k, sub], g_recv.at[a1, sub], first_peer(to)
        )

    for k in (1, 2, 3, 0):
        to = (a1 + k) % 4
        for half in range(2):
            start = pl.multiple_of(to * CLASS_ROWS + half * LANES, LANES)
            column = jnp.broadcast_to(sums_t[pl.ds(start, LANES), 0:1], (LANES, LANES))
            rows = slice(half * LANES, (half + 1) * LANES)
            held_lanes = [lane(k, 0), lane(k, 1), lane(k + 1, 0), lane(k + 1, 1), lane(k + 2, other_half(to, half))]
            for n, cols in enumerate(held_lanes):
                centred = gram[pl.ds(start, LANES), cols] - column * sums_ref[0:1, cols]
                if k:
                    gsend[to, rows, n * LANES : (n + 1) * LANES] = centred.astype(jnp.bfloat16)
                else:
                    gown[rows, n * LANES : (n + 1) * LANES] = centred

    own_side = a2 // 2
    subs = [(1 - own_side) * 2, (1 - own_side) * 2 + 1, a2 + 1 - a2 % 2 * 2, a2]
    for sub in subs:
        for k in (2, 1, 3):
            launch(g_copy(k, sub))
    for k in range(1, 4):
        source = (a1 + k) % 4
        remote(stat1.at[source], stat1.at[source], s1_send.at[k], s1_recv.at[source], first_peer(source)).wait_recv()
    statg2[...] = stat1[0] + stat1[1] + stat1[2] + stat1[3]
    stat2[a2] = statg2[...]

    def stat2_copy(k):
        return remote(statg2, stat2.at[a2], s2_send.at[k], s2_recv.at[a2], second_peer((a2 + k) % 4))

    for k in range(1, 4):
        launch(stat2_copy(k))
    def stat3_copy(k):
        return remote(statg3, stat3.at[z], s3_send.at[k], s3_recv.at[z], z_peer((z + k) % NZ))

    def between(stat, members):
        group = stat[0]
        for k in range(1, members):
            group = group + stat[k]
        mean = group[0:1, :] / jnp.maximum(group[1:2, :], 1.0)
        for k in range(members):
            spread[k : k + 1, :] = stat[k, 0:1, :] / jnp.maximum(stat[k, 1:2, :], 1.0) - mean
        spread_t[...] = jnp.transpose(spread[...])
        for k in range(members):
            spread[k : k + 1, :] = spread[k : k + 1, :] * stat[k, 1:2, :]
        return group

    def outer(rows, cols):
        return jnp.dot(rows, spread[:, cols], preferred_element_type=jnp.float32, precision=lax.Precision.HIGHEST)

    spread[...] = jnp.zeros_like(spread)
    between(stat1, 4)
    own_start = pl.multiple_of(a1 * CLASS_ROWS, CLASS_ROWS)
    for n in range(4):
        gown[:, n * LANES : (n + 1) * LANES] += outer(spread_t[pl.ds(own_start, CLASS_ROWS), :], lane(n // 2, n % 2))
    for half in range(2):
        gown[half * LANES : (half + 1) * LANES, 4 * LANES :] += outer(
            spread_t[pl.ds(own_start + half * LANES, LANES), :], lane(2, other_half(a1, half))
        )

    def h_copy(sub):
        return remote(hsend.at[sub], hrecv.at[a2], h_send.at[sub], h_recv.at[a2], second_peer(sub))

    def mirror(phase, half):
        rows = pl.ds(pl.multiple_of(half * LANES, LANES), LANES)
        turned = jnp.transpose(gown[rows, 2 * LANES : 4 * LANES]).astype(jnp.bfloat16)
        for n in range(4):
            m1_out[phase, n] = turned[n * SUB_ROWS : (n + 1) * SUB_ROWS, :]
            launch(
                remote(
                    m1_out.at[phase, n], m1_in.at[half, a2], m1_send.at[phase, n], m1_recv.at[half, a2],
                    peer((a1 + 1) % 4, n),
                )
            )
        turned = jnp.transpose(gown[rows, 4 * LANES :]).astype(jnp.bfloat16)
        for n in range(2):
            to = other_half(a1, half) * 2 + n
            m2_out[to] = turned[n * SUB_ROWS : (n + 1) * SUB_ROWS, :]
            launch(remote(m2_out.at[to], m2_in.at[a2], m2_send.at[to], m2_recv.at[a2], peer((a1 + 2) % 4, to)))

    for n, sub in enumerate(subs):
        rows = pl.ds(pl.multiple_of(sub * SUB_ROWS, SUB_ROWS), SUB_ROWS)
        for k in range(1, 4):
            source = (a1 + k) % 4
            remote(
                gsend.at[source, rows, :], grecv.at[source, rows, :], g_send.at[k, sub], g_recv.at[source, sub],
                first_peer(source),
            ).wait_recv()
        value = gown[rows, :]
        for k in range(1, 4):
            value = value + grecv[(a1 + k) % 4, rows, :].astype(jnp.float32)
        gown[rows, :] = value
        if n < 3:
            hsend[sub] = value.astype(jnp.bfloat16)
            launch(h_copy(sub))
        if n == 1:
            mirror(0, 1 - own_side)
        if n == 3:
            mirror(1, own_side)

    for k in range(1, 4):
        source = (a2 + k) % 4
        remote(statg2, stat2.at[source], s2_send.at[k], s2_recv.at[source], second_peer(source)).wait_recv()
    statg3[...] = stat2[0] + stat2[1] + stat2[2] + stat2[3]
    stat3[z] = statg3[...]
    for k in range(1, NZ):
        launch(stat3_copy(k))
    between(stat2, 4)
    row_start = pl.multiple_of(a1 * CLASS_ROWS + a2 * SUB_ROWS, SUB_ROWS)
    own_half = other_half(a1, own_side)
    order = [lane(0, 0), lane(0, 1), lane(1, 0), lane(1, 1), lane(2, own_half)]
    order += [lane(2, 1 - own_half), lane(3, 0), lane(3, 1)]
    for n, cols in enumerate(order):
        hown[:, n * LANES : (n + 1) * LANES] = outer(spread_t[pl.ds(row_start, SUB_ROWS), :], cols)
    own_rows = GROUP // NZ

    def along_z(part, lanes, buffer, landed, send_sem, recv_sem):
        for other_z in range(NZ):
            rows = [
                hown[core * GROUP + other_z * own_rows : core * GROUP + (other_z + 1) * own_rows, lanes]
                for core in range(CORES)
            ]
            buffer[other_z] = jnp.concatenate(rows, axis=0).astype(jnp.bfloat16)
        for k in range(1, NZ):
            to = (z + k) % NZ
            launch(
                remote(buffer.at[to], landed.at[z], send_sem.at[part, k], recv_sem.at[part, z], z_peer(to))
            )

    def from_z(part, buffer, landed, send_sem, recv_sem):
        value = buffer[z].astype(jnp.float32)
        for k in range(1, NZ):
            source = (z + k) % NZ
            remote(
                buffer.at[source], landed.at[source], send_sem.at[part, k], recv_sem.at[part, source], z_peer(source)
            ).wait_recv()
            value = value + landed[source].astype(jnp.float32)
        return value

    for k in range(1, 4):
        source = (a2 + k) % 4
        remote(
            hsend.at[source], hrecv.at[source], h_send.at[source], h_recv.at[source], second_peer(source)
        ).wait_recv()
    value = gown[pl.ds(pl.multiple_of(a2 * SUB_ROWS, SUB_ROWS), SUB_ROWS), :]
    for k in range(1, 4):
        value = value + hrecv[(a2 + k) % 4].astype(jnp.float32)
    hown[:, 0:HELD] += value
    along_z(0, slice(0, HELD), tsend, trecv, t_send, t_recv)

    for n in range(4):
        remote(m2_out.at[n], m2_in.at[n], m2_send.at[n], m2_recv.at[n], peer((a1 + 2) % 4, n)).wait_recv()
        hown[:, HELD : HELD + LANES] += m2_in[n].astype(jnp.float32)
    for half in range(2):
        for n in range(4):
            remote(
                m1_out.at[half, n], m1_in.at[half, n], m1_send.at[half, n], m1_recv.at[half, n], peer((a1 + 3) % 4, n)
            ).wait_recv()
            hown[:, HELD + (half + 1) * LANES : HELD + (half + 2) * LANES] += m1_in[half, n].astype(jnp.float32)
    along_z(1, slice(HELD, NFRAMES), usend, urecv, t_send, t_recv)

    for k in range(1, NZ):
        source = (z + k) % NZ
        remote(statg3, stat3.at[source], s3_send.at[k], s3_recv.at[source], z_peer(source)).wait_recv()
    counts = between(stat3, NZ)[1:2, :]
    halves = [
        spread_t[pl.ds(pl.multiple_of(row_start + core * GROUP + z // 2 * 8, 8), 8), :] for core in range(CORES)
    ]
    even = z % 2 == 0
    permuted[...] = outer(
        jnp.concatenate([jnp.where(even, half[0:own_rows], half[own_rows : 2 * own_rows]) for half in halves], axis=0),
        slice(None),
    )
    value = from_z(0, tsend, trecv, t_send, t_recv)
    for n in range(5):
        permuted[:, order[n]] += value[:, n * LANES : (n + 1) * LANES]
    value = from_z(1, usend, urecv, t_send, t_recv)
    for n in range(5, 8):
        permuted[:, order[n]] += value[:, (n - 5) * LANES : (n - 4) * LANES]
    permuted[...] = permuted[...] / counts
    place = lax.broadcasted_iota(jnp.int32, (CORES * own_rows, LANES), 1) // GROUP
    for row_x in range(4):
        for core in range(CORES):
            piece_of = None
            for row_y in range(4):
                first, second = c * row_x + (1 - c) * row_y, c * row_y + (1 - c) * row_x
                block = pl.ds(pl.multiple_of((first * 2 + second // 2) * LANES, LANES), LANES)
                shift = (row_y * GROUP + LANES - (second % 2 * 2 + core) * GROUP) % LANES
                moved = pltpu.roll(permuted[:, block], shift, 1)
                piece_of = moved if piece_of is None else jnp.where(place == row_y, moved, piece_of)
            block = (row_x * CORES + core) * LANES
            ordered[:, block : block + LANES] = piece_of
    value = ordered[...]

    low, high = value[0:own_rows, :], value[own_rows : 2 * own_rows, :]
    fsend[...] = jnp.where(c == 0, high, low)
    last = remote(fsend, frecv, f_send, f_recv, sibling)
    launch(last)
    out[c] = jnp.where(c == 0, low, high)
    last.wait_recv()
    out[1 - c] = frecv[...]

    finish()


def shards(frames, dead_time, band_width, cycle_label, valid):
    rows = NPIX_GROUP // LANES
    flat = [a.reshape(rows, LANES) for a in (dead_time, band_width, cycle_label, valid)]
    own_rows = GROUP // NZ
    dma = pltpu.SemaphoreType.DMA
    f32, bf16 = jnp.float32, jnp.bfloat16
    any_space = pl.BlockSpec(memory_space=pltpu.HBM)
    vmem = pltpu.VMEM
    out = pl.pallas_call(
        kernel,
        out_shape=jax.ShapeDtypeStruct((CYCLES, own_rows, NFRAMES), f32),
        in_specs=[any_space] * 5,
        out_specs=pl.BlockSpec(memory_space=pltpu.VMEM),
        scratch_shapes=[
            vmem((rows, LANES), f32),
            vmem((rows, LANES), jnp.int32),
            vmem((rows, LANES), jnp.int32),
            vmem((rows, LANES), jnp.int32),
            vmem((CHUNKS, NDEV_FRAME, OWN_FRAMES, LANES), bf16),
            vmem((PAD + NFRAMES + PAD, LANES), f32),
            vmem((NFRAMES, CHIP_PIX), bf16),
            vmem((CHUNKS, NFRAMES, LANES), bf16),
            vmem((NFRAMES, NFRAMES), f32),
            vmem((8, NFRAMES), f32),
            vmem((NFRAMES, 8), f32),
            vmem((4, CLASS_ROWS, HELD), bf16),
            vmem((4, CLASS_ROWS, HELD), bf16),
            vmem((CLASS_ROWS, HELD), f32),
            vmem((4, SUB_ROWS, HELD), bf16),
            vmem((4, SUB_ROWS, HELD), bf16),
            vmem((SUB_ROWS, NFRAMES), f32),
            vmem((NZ, CORES * own_rows, HELD), bf16),
            vmem((NZ, CORES * own_rows, HELD), bf16),
            vmem((NZ, CORES * own_rows, NFRAMES - HELD), bf16),
            vmem((NZ, CORES * own_rows, NFRAMES - HELD), bf16),
            vmem((4, 2, NFRAMES), f32),
            vmem((4, 2, NFRAMES), f32),
            vmem((NZ, 2, NFRAMES), f32),
            vmem((2, NFRAMES), f32),
            vmem((2, NFRAMES), f32),
            vmem((8, NFRAMES), f32),
            vmem((NFRAMES, 8), f32),
            vmem((own_rows, NFRAMES), f32),
            vmem((own_rows, NFRAMES), f32),
            vmem((2, 4, SUB_ROWS, LANES), bf16), vmem((2, 4, SUB_ROWS, LANES), bf16),
            vmem((4, SUB_ROWS, LANES), bf16), vmem((4, SUB_ROWS, LANES), bf16),
            vmem((CORES * own_rows, NFRAMES), f32),
            vmem((CORES * own_rows, NFRAMES), f32),
            dma((4,)),
            dma((CHUNKS,)),
            dma((CHUNKS, NDEV_FRAME)), dma((CHUNKS, NDEV_FRAME)),
            dma((CHUNKS,)), dma((CHUNKS,)),
            dma((4,)), dma((4,)),
            dma((4,)), dma((4,)),
            dma((NZ,)), dma((NZ,)),
            dma((4, 4)), dma((4, 4)),
            dma((4,)), dma((4,)),
            dma((2, NZ)), dma((2, NZ)),
            dma, dma,
            dma((2, 4)), dma((2, 4)),
            dma((4,)), dma((4,)),
        ],
        compiler_params=pltpu.CompilerParams(
            collective_id=0, has_side_effects=True, vmem_limit_bytes=60 * 2**20
        ),
    )(frames, *flat)
    return jnp.transpose(out, (1, 0, 2))


def solution(mesh):
    in_specs = (P("frame", "pixel"), P("pixel"), P("pixel"), P("pixel"), P("pixel"))
    out_specs = P(("frame", "pixel"), None, None)
    return jax.shard_map(shards, mesh=mesh, in_specs=in_specs, out_specs=out_specs, check_vma=False)
```

```python
import functools

import jax
import jax.numpy as jnp
from jax import lax
from jax.experimental import pallas as pl
from jax.experimental.pallas import tpu as pltpu
from jax.sharding import PartitionSpec as P

MESH = pl.DeviceIdType.MESH
CYCLES = 2
BAND = 8
CORES = 2
NX = 4
NY = 4
NZ = 8
LANES = 128
GROUP = 32
NFRAMES = 1024
NDEV_FRAME = NX * CORES
OWN_FRAMES = NFRAMES // NDEV_FRAME
NPIX_GROUP = 4096
OWN_PIX = NPIX_GROUP // NDEV_FRAME
CHUNKS = OWN_PIX // LANES
CHIP_PIX = CORES * OWN_PIX
CLASS_ROWS = NFRAMES // 4
SUB_ROWS = CLASS_ROWS // 4
PAD = BAND
TILE = 256
HELD = 640


def remote(src, dst, send_sem, recv_sem, device):
    return pltpu.make_async_remote_copy(
        src_ref=src,
        dst_ref=dst,
        send_sem=send_sem,
        recv_sem=recv_sem,
        device_id=device,
        device_id_type=MESH,
    )


def kernel(
    frames, dead_hbm, band_hbm, label_hbm, valid_hbm,
    out,
    dead, band, label, valid, arrived, rate, smooth, outgoing,
    gram, sums_ref, sums_t, gsend, grecv, gown, hsend, hrecv, hown, tsend, trecv,
    stat1, stat2, stat3, statg2, statg3, spread, spread_t,
    fsend, frecv, m1_out, m1_in, m2_out, m2_in, permuted, ordered,
    par_sem, own_sem, a2a_send, a2a_recv, sib_send, sib_recv,
    s1_send, s1_recv, s2_send, s2_recv, s3_send, s3_recv,
    g_send, g_recv, h_send, h_recv, t_send, t_recv, f_send, f_recv,
    m1_send, m1_recv, m2_send, m2_recv,
):
    f = lax.axis_index("frame")
    p = lax.axis_index("pixel")
    x, c = f // CORES, f % CORES
    y, z = p // NZ, p % NZ
    a1 = c * x + (1 - c) * y
    a2 = c * y + (1 - c) * x

    def peer(a, b):
        return ((c * a + (1 - c) * b) * CORES + c, (c * b + (1 - c) * a) * NZ + z)

    def first_peer(a):
        return peer(a, a2)

    def second_peer(b):
        return peer(a1, b)

    def z_peer(other):
        return (f, y * NZ + other)

    def frame_peer(other):
        return (other, p)

    sibling = (x * CORES + (1 - c), p)

    pending = []

    def launch(copy):
        copy.start()
        pending.append(copy)

    def finish():
        for copy in pending:
            copy.wait_send()

    barrier = pltpu.get_barrier_semaphore()
    for k in range(1, NDEV_FRAME):
        pl.semaphore_signal(barrier, inc=1, device_id=frame_peer((f + k) % NDEV_FRAME), device_id_type=MESH)
    for k in range(1, NY):
        pl.semaphore_signal(barrier, inc=1, device_id=(f, ((y + k) % NY) * NZ + z), device_id_type=MESH)
    for k in range(1, NZ):
        pl.semaphore_signal(barrier, inc=1, device_id=z_peer((z + k) % NZ), device_id_type=MESH)
    pl.semaphore_wait(barrier, NDEV_FRAME - 1 + NY - 1 + NZ - 1)

    def piece(owner, chunk):
        return frames.at[:, pl.ds(pl.multiple_of(owner * OWN_PIX + chunk * LANES, LANES), LANES)]

    def a2a_copy(k, chunk):
        to = (f + k) % NDEV_FRAME
        return remote(
            piece(to, chunk), arrived.at[chunk, f], a2a_send.at[chunk, k], a2a_recv.at[chunk, f], frame_peer(to)
        )

    def own_copy(chunk):
        return pltpu.make_async_copy(piece(f, chunk), arrived.at[chunk, f], own_sem.at[chunk])

    for chunk in range(CHUNKS):
        for k in (4, 3, 5, 2, 6, 7, 1):
            launch(a2a_copy(k, chunk))
        own_copy(chunk).start()
    params = [
        pltpu.make_async_copy(src, dst, par_sem.at[n])
        for n, (src, dst) in enumerate(
            ((dead_hbm, dead), (band_hbm, band), (label_hbm, label), (valid_hbm, valid))
        )
    ]
    for copy in params:
        copy.start()
    rate[0:PAD, :] = jnp.zeros((PAD, LANES), jnp.float32)
    rate[PAD + NFRAMES : PAD + NFRAMES + PAD, :] = jnp.zeros((PAD, LANES), jnp.float32)
    for copy in params:
        copy.wait()

    def sib_copy(chunk):
        return remote(
            outgoing.at[chunk],
            smooth.at[:, pl.ds((2 * chunk + 1) * LANES, LANES)],
            sib_send.at[chunk],
            sib_recv.at[chunk],
            sibling,
        )

    contract_last = (((1,), (1,)), ((), ()))

    def accumulate(chunk):
        lanes = slice(2 * chunk * LANES, 2 * (chunk + 1) * LANES)
        sib_copy(chunk).wait_recv()
        part = lax.dot_general(
            jnp.ones((8, 2 * LANES), jnp.bfloat16), smooth[:, lanes], contract_last, preferred_element_type=jnp.float32
        )
        sums_ref[...] = part if chunk == 0 else sums_ref[...] + part

        for m in range(4):
            for n in (m, (m + 1) % 4, (m + 2) % 4):
                rows, cols = slice(m * TILE, (m + 1) * TILE), slice(n * TILE, (n + 1) * TILE)
                product = lax.dot_general(
                    smooth[rows, lanes], smooth[cols, lanes], contract_last, preferred_element_type=jnp.float32
                )
                gram[rows, cols] = product if chunk == 0 else gram[rows, cols] + product

    for chunk in range(CHUNKS):
        own_copy(chunk).wait()
        for k in range(1, NDEV_FRAME):
            source = (f + k) % NDEV_FRAME
            remote(
                piece(source, chunk), arrived.at[chunk, source], a2a_send.at[chunk, k],
                a2a_recv.at[chunk, source], frame_peer(source),
            ).wait_recv()
        row = f * CHUNKS + chunk
        dead_row = dead[pl.ds(row, 1), :]
        width = band[pl.ds(row, 1), :]
        cycle = label[pl.ds(row, 1), :]
        used = valid[pl.ds(row, 1), :] == 1
        mine = jnp.where(used & (cycle == c), 1.0, 0.0)
        other = jnp.where(used & (cycle == 1 - c), 1.0, 0.0)
        within = [jnp.where(width >= k, 1.0, 0.0) for k in range(1, BAND + 1)]
        full = 1.0 / (2 * width + 1).astype(jnp.float32)

        def correct(block, _):
            for half in range(OWN_FRAMES // GROUP):
                count = 4.0 + arrived[chunk, block, half * GROUP : (half + 1) * GROUP, :].astype(jnp.float32)
                rate[pl.ds(pl.multiple_of(PAD + block * OWN_FRAMES + half * GROUP, 8), GROUP), :] = count / (
                    1.0 - dead_row * count
                )
            return 0

        lax.fori_loop(0, NDEV_FRAME, correct, 0)

        def window(start):
            total = rate[pl.ds(start + PAD, GROUP), :]
            for k in range(1, BAND + 1):
                total = total + within[k - 1] * (
                    rate[pl.ds(start + PAD - k, GROUP), :] + rate[pl.ds(start + PAD + k, GROUP), :]
                )
            return total

        def put(block, value):
            row_x, core, row_y = block // 8, block // 4 % 2, block % 4
            along_x, along_y = row_x * 8 + row_y * 2 + core, row_y * 8 + row_x * 2 + core
            own_rows = pl.ds(pl.multiple_of((c * along_x + (1 - c) * along_y) * GROUP, GROUP), GROUP)
            sib_rows = pl.ds(pl.multiple_of((c * along_y + (1 - c) * along_x) * GROUP, GROUP), GROUP)
            smooth[own_rows, 2 * chunk * LANES : (2 * chunk + 1) * LANES] = (value * mine).astype(jnp.bfloat16)
            outgoing[chunk, sib_rows, :] = (value * other).astype(jnp.bfloat16)

        def inside(block, _):
            put(block, window(pl.multiple_of(block * GROUP, GROUP)) * full)
            return 0

        for start in (0, NFRAMES - GROUP):
            frame = start + lax.broadcasted_iota(jnp.int32, (GROUP, LANES), 0)
            span = jnp.minimum(frame + width, NFRAMES - 1) - jnp.maximum(frame - width, 0) + 1
            put(start // GROUP, window(start) / span.astype(jnp.float32))
        lax.fori_loop(1, NFRAMES // GROUP - 1, inside, 0)
        launch(sib_copy(chunk))
        if chunk:
            accumulate(chunk - 1)

    chip_label = label[pl.ds(pl.multiple_of(x * (CHIP_PIX // LANES), 8), CHIP_PIX // LANES), :]
    chip_valid = valid[pl.ds(pl.multiple_of(x * (CHIP_PIX // LANES), 8), CHIP_PIX // LANES), :]
    held = jnp.sum(jnp.where((chip_label == c) & (chip_valid == 1), 1.0, 0.0), axis=(0, 1), keepdims=True)

    accumulate(CHUNKS - 1)
    sums_t[...] = jnp.transpose(sums_ref[...] / jnp.maximum(held, 1.0))
    stat1[a1, 0:1, :] = sums_ref[0:1, :]
    stat1[a1, 1:2, :] = jnp.broadcast_to(held, (1, NFRAMES))

    def stat1_copy(k):
        to = (a1 + k) % 4
        return remote(stat1.at[a1], stat1.at[a1], s1_send.at[k], s1_recv.at[a1], first_peer(to))

    for k in range(1, 4):
        launch(stat1_copy(k))

    def lane(a, half):
        return pl.ds(pl.multiple_of(((a1 + a) % 4 * 2 + half) * LANES, LANES), LANES)

    def other_half(a, half):
        high = a // 2
        return (1 - half) * high + half * (1 - high)

    def g_copy(k, sub):
        to = (a1 + k) % 4
        rows = pl.ds(pl.multiple_of(sub * SUB_ROWS, SUB_ROWS), SUB_ROWS)
        return remote(
            gsend.at[to, rows, :], grecv.at[a1, rows, :], g_send.at[k, sub], g_recv.at[a1, sub], first_peer(to)
        )

    for k in (1, 2, 3, 0):
        to = (a1 + k) % 4
        for half in range(2):
            start = pl.multiple_of(to * CLASS_ROWS + half * LANES, LANES)
            column = jnp.broadcast_to(sums_t[pl.ds(start, LANES), 0:1], (LANES, LANES))
            rows = slice(half * LANES, (half + 1) * LANES)
            held_lanes = [lane(k, 0), lane(k, 1), lane(k + 1, 0), lane(k + 1, 1), lane(k + 2, other_half(to, half))]
            for n, cols in enumerate(held_lanes):
                centred = gram[pl.ds(start, LANES), cols] - column * sums_ref[0:1, cols]
                if k:
                    gsend[to, rows, n * LANES : (n + 1) * LANES] = centred.astype(jnp.bfloat16)
                else:
                    gown[rows, n * LANES : (n + 1) * LANES] = centred

    for j in (1, 2, 3, 0):
        for k in (2, 1, 3):
            launch(g_copy(k, (a2 + j) % 4))
    for k in range(1, 4):
        source = (a1 + k) % 4
        remote(stat1.at[source], stat1.at[source], s1_send.at[k], s1_recv.at[source], first_peer(source)).wait_recv()
    statg2[...] = stat1[0] + stat1[1] + stat1[2] + stat1[3]
    stat2[a2] = statg2[...]

    def stat2_copy(k):
        return remote(statg2, stat2.at[a2], s2_send.at[k], s2_recv.at[a2], second_peer((a2 + k) % 4))

    for k in range(1, 4):
        launch(stat2_copy(k))
    def stat3_copy(k):
        return remote(statg3, stat3.at[z], s3_send.at[k], s3_recv.at[z], z_peer((z + k) % NZ))

    def between(stat, members):
        group = stat[0]
        for k in range(1, members):
            group = group + stat[k]
        mean = group[0:1, :] / jnp.maximum(group[1:2, :], 1.0)
        for k in range(members):
            spread[k : k + 1, :] = stat[k, 0:1, :] / jnp.maximum(stat[k, 1:2, :], 1.0) - mean
        spread_t[...] = jnp.transpose(spread[...])
        for k in range(members):
            spread[k : k + 1, :] = spread[k : k + 1, :] * stat[k, 1:2, :]
        return group

    def outer(rows, cols):
        return jnp.dot(rows, spread[:, cols], preferred_element_type=jnp.float32, precision=lax.Precision.HIGHEST)

    spread[...] = jnp.zeros_like(spread)
    between(stat1, 4)
    own_start = pl.multiple_of(a1 * CLASS_ROWS, CLASS_ROWS)
    for n in range(4):
        gown[:, n * LANES : (n + 1) * LANES] += outer(spread_t[pl.ds(own_start, CLASS_ROWS), :], lane(n // 2, n % 2))
    for half in range(2):
        gown[half * LANES : (half + 1) * LANES, 4 * LANES :] += outer(
            spread_t[pl.ds(own_start + half * LANES, LANES), :], lane(2, other_half(a1, half))
        )

    def h_copy(k):
        to = (a2 + k) % 4
        return remote(hsend.at[to], hrecv.at[a2], h_send.at[k], h_recv.at[a2], second_peer(to))

    for j in (1, 2, 3, 0):
        sub = (a2 + j) % 4
        rows = pl.ds(pl.multiple_of(sub * SUB_ROWS, SUB_ROWS), SUB_ROWS)
        if j == 0:
            for k in range(1, 4):
                source = (a2 + k) % 4
                remote(statg2, stat2.at[source], s2_send.at[k], s2_recv.at[source], second_peer(source)).wait_recv()
            statg3[...] = stat2[0] + stat2[1] + stat2[2] + stat2[3]
            stat3[z] = statg3[...]
            for k in (4, 3, 5, 2, 6, 1, 7):
                launch(stat3_copy(k))
        for k in range(1, 4):
            source = (a1 + k) % 4
            remote(
                gsend.at[source, rows, :], grecv.at[source, rows, :], g_send.at[k, sub], g_recv.at[source, sub],
                first_peer(source),
            ).wait_recv()
        value = gown[rows, :]
        for k in range(1, 4):
            value = value + grecv[(a1 + k) % 4, rows, :].astype(jnp.float32)
        gown[rows, :] = value
        if j:
            hsend[sub] = value.astype(jnp.bfloat16)
            launch(h_copy(j))

    def mirror_copy(n):
        return remote(
            m1_out.at[n], m1_in.at[a2], m1_send.at[n], m1_recv.at[a2], peer((a1 + 1) % 4, n)
        )

    def half_copy(n):
        return remote(
            m2_out.at[n], m2_in.at[a2], m2_send.at[n], m2_recv.at[a2], peer((a1 + 2) % 4, n)
        )

    for half in range(2):
        mirror = jnp.transpose(gown[half * LANES : (half + 1) * LANES, 4 * LANES :]).astype(jnp.bfloat16)
        for n in range(2):
            m2_out[other_half(a1, half) * 2 + n] = mirror[n * SUB_ROWS : (n + 1) * SUB_ROWS, :]
    for n in range(4):
        launch(half_copy(n))

    mirror = jnp.transpose(gown[:, 2 * LANES : 4 * LANES]).astype(jnp.bfloat16)
    for n in range(4):
        m1_out[n] = mirror[n * SUB_ROWS : (n + 1) * SUB_ROWS, :]
        launch(mirror_copy(n))
    between(stat2, 4)
    row_start = pl.multiple_of(a1 * CLASS_ROWS + a2 * SUB_ROWS, SUB_ROWS)
    column = spread_t[pl.ds(row_start, SUB_ROWS), :]
    value = column[:, 0:1] * spread[0:1, :]
    for k in range(1, 4):
        value = value + column[:, k : k + 1] * spread[k : k + 1, :]
    hown[...] = value
    for k in range(1, 4):
        source = (a2 + k) % 4
        remote(hsend.at[source], hrecv.at[source], h_send.at[k], h_recv.at[source], second_peer(source)).wait_recv()
    value = gown[pl.ds(pl.multiple_of(a2 * SUB_ROWS, SUB_ROWS), SUB_ROWS), :]
    for k in range(1, 4):
        value = value + hrecv[(a2 + k) % 4].astype(jnp.float32)
    own_half = other_half(a1, a2 // 2)
    for n, cols in enumerate((lane(0, 0), lane(0, 1), lane(1, 0), lane(1, 1), lane(2, own_half))):
        hown[:, cols] += value[:, n * LANES : (n + 1) * LANES]
    for n in range(4):
        remote(m1_out.at[n], m1_in.at[n], m1_send.at[n], m1_recv.at[n], peer((a1 + 3) % 4, n)).wait_recv()
    value = m1_in[0].astype(jnp.float32)
    for n in range(1, 4):
        value = value + m1_in[n].astype(jnp.float32)
    hown[:, lane(3, 0)] += value[:, 0:LANES]
    hown[:, lane(3, 1)] += value[:, LANES:]
    for n in range(4):
        remote(m2_out.at[n], m2_in.at[n], m2_send.at[n], m2_recv.at[n], peer((a1 + 2) % 4, n)).wait_recv()
    value = m2_in[0].astype(jnp.float32)
    for n in range(1, 4):
        value = value + m2_in[n].astype(jnp.float32)
    hown[:, lane(2, 1 - own_half)] += value
    own_rows = GROUP // NZ

    for other_z in range(NZ):
        rows = jnp.concatenate(
            [hown[core * GROUP + other_z * own_rows : core * GROUP + (other_z + 1) * own_rows, :] for core in range(CORES)],
            axis=0,
        )
        tsend[other_z] = rows.astype(jnp.bfloat16)

    def t_copy(k):
        to = (z + k) % NZ
        return remote(tsend.at[to], trecv.at[z], t_send.at[k], t_recv.at[z], z_peer(to))

    for k in (4, 3, 5, 2, 6, 1, 7):
        launch(t_copy(k))
    for k in range(1, NZ):
        source = (z + k) % NZ
        remote(statg3, stat3.at[source], s3_send.at[k], s3_recv.at[source], z_peer(source)).wait_recv()
    counts = between(stat3, NZ)[1:2, :]
    halves = [
        spread_t[pl.ds(pl.multiple_of(row_start + core * GROUP + z // 2 * 8, 8), 8), :] for core in range(CORES)
    ]
    even = z % 2 == 0
    value = tsend[z].astype(jnp.float32) + outer(
        jnp.concatenate([jnp.where(even, half[0:own_rows], half[own_rows : 2 * own_rows]) for half in halves], axis=0),
        slice(None),
    )
    for k in range(1, NZ):
        source = (z + k) % NZ
        remote(tsend.at[source], trecv.at[source], t_send.at[k], t_recv.at[source], z_peer(source)).wait_recv()
        value = value + trecv[source].astype(jnp.float32)
    permuted[...] = value / counts
    place = lax.broadcasted_iota(jnp.int32, (CORES * own_rows, LANES), 1) // GROUP
    for row_x in range(4):
        for core in range(CORES):
            piece_of = None
            for row_y in range(4):
                first, second = c * row_x + (1 - c) * row_y, c * row_y + (1 - c) * row_x
                block = pl.ds(pl.multiple_of((first * 2 + second // 2) * LANES, LANES), LANES)
                shift = (row_y * GROUP + LANES - (second % 2 * 2 + core) * GROUP) % LANES
                moved = pltpu.roll(permuted[:, block], shift, 1)
                piece_of = moved if piece_of is None else jnp.where(place == row_y, moved, piece_of)
            block = (row_x * CORES + core) * LANES
            ordered[:, block : block + LANES] = piece_of
    value = ordered[...]

    low, high = value[0:own_rows, :], value[own_rows : 2 * own_rows, :]
    fsend[...] = jnp.where(c == 0, high, low)
    last = remote(fsend, frecv, f_send, f_recv, sibling)
    launch(last)
    out[c] = jnp.where(c == 0, low, high)
    last.wait_recv()
    out[1 - c] = frecv[...]

    finish()


def shards(frames, dead_time, band_width, cycle_label, valid):
    rows = NPIX_GROUP // LANES
    flat = [a.reshape(rows, LANES) for a in (dead_time, band_width, cycle_label, valid)]
    own_rows = GROUP // NZ
    dma = pltpu.SemaphoreType.DMA
    f32, bf16 = jnp.float32, jnp.bfloat16
    any_space = pl.BlockSpec(memory_space=pltpu.HBM)
    vmem = pltpu.VMEM
    out = pl.pallas_call(
        kernel,
        out_shape=jax.ShapeDtypeStruct((CYCLES, own_rows, NFRAMES), f32),
        in_specs=[any_space] * 5,
        out_specs=pl.BlockSpec(memory_space=pltpu.VMEM),
        scratch_shapes=[
            vmem((rows, LANES), f32),
            vmem((rows, LANES), jnp.int32),
            vmem((rows, LANES), jnp.int32),
            vmem((rows, LANES), jnp.int32),
            vmem((CHUNKS, NDEV_FRAME, OWN_FRAMES, LANES), bf16),
            vmem((PAD + NFRAMES + PAD, LANES), f32),
            vmem((NFRAMES, CHIP_PIX), bf16),
            vmem((CHUNKS, NFRAMES, LANES), bf16),
            vmem((NFRAMES, NFRAMES), f32),
            vmem((8, NFRAMES), f32),
            vmem((NFRAMES, 8), f32),
            vmem((4, CLASS_ROWS, HELD), bf16),
            vmem((4, CLASS_ROWS, HELD), bf16),
            vmem((CLASS_ROWS, HELD), f32),
            vmem((4, SUB_ROWS, HELD), bf16),
            vmem((4, SUB_ROWS, HELD), bf16),
            vmem((SUB_ROWS, NFRAMES), f32),
            vmem((NZ, CORES * own_rows, NFRAMES), bf16),
            vmem((NZ, CORES * own_rows, NFRAMES), bf16),
            vmem((4, 2, NFRAMES), f32),
            vmem((4, 2, NFRAMES), f32),
            vmem((NZ, 2, NFRAMES), f32),
            vmem((2, NFRAMES), f32),
            vmem((2, NFRAMES), f32),
            vmem((8, NFRAMES), f32),
            vmem((NFRAMES, 8), f32),
            vmem((own_rows, NFRAMES), f32),
            vmem((own_rows, NFRAMES), f32),
            vmem((4, SUB_ROWS, 2 * LANES), bf16), vmem((4, SUB_ROWS, 2 * LANES), bf16),
            vmem((4, SUB_ROWS, LANES), bf16), vmem((4, SUB_ROWS, LANES), bf16),
            vmem((CORES * own_rows, NFRAMES), f32),
            vmem((CORES * own_rows, NFRAMES), f32),
            dma((4,)),
            dma((CHUNKS,)),
            dma((CHUNKS, NDEV_FRAME)), dma((CHUNKS, NDEV_FRAME)),
            dma((CHUNKS,)), dma((CHUNKS,)),
            dma((4,)), dma((4,)),
            dma((4,)), dma((4,)),
            dma((NZ,)), dma((NZ,)),
            dma((4, 4)), dma((4, 4)),
            dma((4,)), dma((4,)),
            dma((NZ,)), dma((NZ,)),
            dma, dma,
            dma((4,)), dma((4,)),
            dma((4,)), dma((4,)),
        ],
        compiler_params=pltpu.CompilerParams(
            collective_id=0, has_side_effects=True, vmem_limit_bytes=60 * 2**20
        ),
    )(frames, *flat)
    return jnp.transpose(out, (1, 0, 2))


def solution(mesh):
    in_specs = (P("frame", "pixel"), P("pixel"), P("pixel"), P("pixel"), P("pixel"))
    out_specs = P(("frame", "pixel"), None, None)
    return jax.shard_map(shards, mesh=mesh, in_specs=in_specs, out_specs=out_specs, check_vma=False)
```

```python
import functools

import jax
import jax.numpy as jnp
from jax import lax
from jax.experimental import pallas as pl
from jax.experimental.pallas import tpu as pltpu
from jax.sharding import PartitionSpec as P

MESH = pl.DeviceIdType.MESH
CYCLES = 2
BAND = 8
CORES = 2
NX = 4
NY = 4
NZ = 8
LANES = 128
GROUP = 32
NFRAMES = 1024
NDEV_FRAME = NX * CORES
OWN_FRAMES = NFRAMES // NDEV_FRAME
NPIX_GROUP = 4096
OWN_PIX = NPIX_GROUP // NDEV_FRAME
CHUNKS = OWN_PIX // LANES
CHIP_PIX = CORES * OWN_PIX
CLASS_ROWS = NFRAMES // 4
SUB_ROWS = CLASS_ROWS // 4
PAD = BAND
TILE = 256
HELD = 640


def remote(src, dst, send_sem, recv_sem, device):
    return pltpu.make_async_remote_copy(
        src_ref=src,
        dst_ref=dst,
        send_sem=send_sem,
        recv_sem=recv_sem,
        device_id=device,
        device_id_type=MESH,
    )


def kernel(
    frames, dead_hbm, band_hbm, label_hbm, valid_hbm,
    out,
    dead, band, label, valid, arrived, rate, smooth, outgoing,
    gram, sums_ref, sums_t, gsend, grecv, gown, hsend, hrecv, hown, tsend, trecv,
    stat1, stat2, stat3, statg2, statg3, spread, spread_t,
    fsend, frecv, m1_out, m1_in, m2_out, m2_in, permuted,
    par_sem, own_sem, a2a_send, a2a_recv, sib_send, sib_recv,
    s1_send, s1_recv, s2_send, s2_recv, s3_send, s3_recv,
    g_send, g_recv, h_send, h_recv, t_send, t_recv, f_send, f_recv,
    m1_send, m1_recv, m2_send, m2_recv,
):
    f = lax.axis_index("frame")
    p = lax.axis_index("pixel")
    x, c = f // CORES, f % CORES
    y, z = p // NZ, p % NZ
    a1 = c * x + (1 - c) * y
    a2 = c * y + (1 - c) * x

    def peer(a, b):
        return ((c * a + (1 - c) * b) * CORES + c, (c * b + (1 - c) * a) * NZ + z)

    def first_peer(a):
        return peer(a, a2)

    def second_peer(b):
        return peer(a1, b)

    def z_peer(other):
        return (f, y * NZ + other)

    def frame_peer(other):
        return (other, p)

    sibling = (x * CORES + (1 - c), p)

    pending = []

    def launch(copy):
        copy.start()
        pending.append(copy)

    def finish():
        for copy in pending:
            copy.wait_send()

    barrier = pltpu.get_barrier_semaphore()
    for k in range(1, NDEV_FRAME):
        pl.semaphore_signal(barrier, inc=1, device_id=frame_peer((f + k) % NDEV_FRAME), device_id_type=MESH)
    for k in range(1, NY):
        pl.semaphore_signal(barrier, inc=1, device_id=(f, ((y + k) % NY) * NZ + z), device_id_type=MESH)
    for k in range(1, NZ):
        pl.semaphore_signal(barrier, inc=1, device_id=z_peer((z + k) % NZ), device_id_type=MESH)
    pl.semaphore_wait(barrier, NDEV_FRAME - 1 + NY - 1 + NZ - 1)

    def piece(owner, chunk):
        return frames.at[:, pl.ds(pl.multiple_of(owner * OWN_PIX + chunk * LANES, LANES), LANES)]

    def a2a_copy(k, chunk):
        to = (f + k) % NDEV_FRAME
        return remote(
            piece(to, chunk), arrived.at[chunk, f], a2a_send.at[chunk, k], a2a_recv.at[chunk, f], frame_peer(to)
        )

    def own_copy(chunk):
        return pltpu.make_async_copy(piece(f, chunk), arrived.at[chunk, f], own_sem.at[chunk])

    for chunk in range(CHUNKS):
        for k in (4, 3, 5, 2, 6, 7, 1):
            launch(a2a_copy(k, chunk))
        own_copy(chunk).start()
    params = [
        pltpu.make_async_copy(src, dst, par_sem.at[n])
        for n, (src, dst) in enumerate(
            ((dead_hbm, dead), (band_hbm, band), (label_hbm, label), (valid_hbm, valid))
        )
    ]
    for copy in params:
        copy.start()
    rate[0:PAD, :] = jnp.zeros((PAD, LANES), jnp.float32)
    rate[PAD + NFRAMES : PAD + NFRAMES + PAD, :] = jnp.zeros((PAD, LANES), jnp.float32)
    for copy in params:
        copy.wait()

    def sib_copy(chunk):
        return remote(
            outgoing.at[chunk],
            smooth.at[:, pl.ds((2 * chunk + 1) * LANES, LANES)],
            sib_send.at[chunk],
            sib_recv.at[chunk],
            sibling,
        )

    contract_last = (((1,), (1,)), ((), ()))

    def accumulate(chunk):
        lanes = slice(2 * chunk * LANES, 2 * (chunk + 1) * LANES)
        sib_copy(chunk).wait_recv()
        part = lax.dot_general(
            jnp.ones((8, 2 * LANES), jnp.bfloat16), smooth[:, lanes], contract_last, preferred_element_type=jnp.float32
        )
        sums_ref[...] = part if chunk == 0 else sums_ref[...] + part

        for m in range(4):
            for n in (m, (m + 1) % 4, (m + 2) % 4):
                rows, cols = slice(m * TILE, (m + 1) * TILE), slice(n * TILE, (n + 1) * TILE)
                product = lax.dot_general(
                    smooth[rows, lanes], smooth[cols, lanes], contract_last, preferred_element_type=jnp.float32
                )
                gram[rows, cols] = product if chunk == 0 else gram[rows, cols] + product

    for chunk in range(CHUNKS):
        own_copy(chunk).wait()
        for k in range(1, NDEV_FRAME):
            source = (f + k) % NDEV_FRAME
            remote(
                piece(source, chunk), arrived.at[chunk, source], a2a_send.at[chunk, k],
                a2a_recv.at[chunk, source], frame_peer(source),
            ).wait_recv()
        row = f * CHUNKS + chunk
        dead_row = dead[pl.ds(row, 1), :]
        width = band[pl.ds(row, 1), :]
        cycle = label[pl.ds(row, 1), :]
        used = valid[pl.ds(row, 1), :] == 1
        mine = jnp.where(used & (cycle == c), 1.0, 0.0)
        other = jnp.where(used & (cycle == 1 - c), 1.0, 0.0)
        within = [jnp.where(width >= k, 1.0, 0.0) for k in range(1, BAND + 1)]
        full = 1.0 / (2 * width + 1).astype(jnp.float32)

        def correct(block, _):
            for half in range(OWN_FRAMES // GROUP):
                count = 4.0 + arrived[chunk, block, half * GROUP : (half + 1) * GROUP, :].astype(jnp.float32)
                rate[pl.ds(pl.multiple_of(PAD + block * OWN_FRAMES + half * GROUP, 8), GROUP), :] = count / (
                    1.0 - dead_row * count
                )
            return 0

        lax.fori_loop(0, NDEV_FRAME, correct, 0, unroll=2)

        def window(start):
            total = rate[pl.ds(start + PAD, GROUP), :]
            for k in range(1, BAND + 1):
                total = total + within[k - 1] * (
                    rate[pl.ds(start + PAD - k, GROUP), :] + rate[pl.ds(start + PAD + k, GROUP), :]
                )
            return total

        def put(block, value):
            row_x, core, row_y = block // 8, block // 4 % 2, block % 4
            along_x, along_y = row_x * 8 + row_y * 2 + core, row_y * 8 + row_x * 2 + core
            own_rows = pl.ds(pl.multiple_of((c * along_x + (1 - c) * along_y) * GROUP, GROUP), GROUP)
            sib_rows = pl.ds(pl.multiple_of((c * along_y + (1 - c) * along_x) * GROUP, GROUP), GROUP)
            smooth[own_rows, 2 * chunk * LANES : (2 * chunk + 1) * LANES] = (value * mine).astype(jnp.bfloat16)
            outgoing[chunk, sib_rows, :] = (value * other).astype(jnp.bfloat16)

        def inside(block, _):
            put(block, window(pl.multiple_of(block * GROUP, GROUP)) * full)
            return 0

        for start in (0, NFRAMES - GROUP):
            frame = start + lax.broadcasted_iota(jnp.int32, (GROUP, LANES), 0)
            span = jnp.minimum(frame + width, NFRAMES - 1) - jnp.maximum(frame - width, 0) + 1
            put(start // GROUP, window(start) / span.astype(jnp.float32))
        lax.fori_loop(1, NFRAMES // GROUP - 1, inside, 0, unroll=3)
        launch(sib_copy(chunk))
        if chunk:
            accumulate(chunk - 1)

    chip_label = label[pl.ds(pl.multiple_of(x * (CHIP_PIX // LANES), 8), CHIP_PIX // LANES), :]
    chip_valid = valid[pl.ds(pl.multiple_of(x * (CHIP_PIX // LANES), 8), CHIP_PIX // LANES), :]
    held = jnp.sum(jnp.where((chip_label == c) & (chip_valid == 1), 1.0, 0.0), axis=(0, 1), keepdims=True)

    accumulate(CHUNKS - 1)
    sums_t[...] = jnp.transpose(sums_ref[...] / jnp.maximum(held, 1.0))
    stat1[a1, 0:1, :] = sums_ref[0:1, :]
    stat1[a1, 1:2, :] = jnp.broadcast_to(held, (1, NFRAMES))

    def stat1_copy(k):
        to = (a1 + k) % 4
        return remote(stat1.at[a1], stat1.at[a1], s1_send.at[k], s1_recv.at[a1], first_peer(to))

    for k in range(1, 4):
        launch(stat1_copy(k))

    def lane(a, half):
        return pl.ds(pl.multiple_of(((a1 + a) % 4 * 2 + half) * LANES, LANES), LANES)

    def other_half(a, half):
        high = a // 2
        return (1 - half) * high + half * (1 - high)

    def g_copy(k, sub):
        to = (a1 + k) % 4
        rows = pl.ds(pl.multiple_of(sub * SUB_ROWS, SUB_ROWS), SUB_ROWS)
        return remote(
            gsend.at[to, rows, :], grecv.at[a1, rows, :], g_send.at[k, sub], g_recv.at[a1, sub], first_peer(to)
        )

    for k in (1, 2, 3, 0):
        to = (a1 + k) % 4
        for half in range(2):
            start = pl.multiple_of(to * CLASS_ROWS + half * LANES, LANES)
            column = jnp.broadcast_to(sums_t[pl.ds(start, LANES), 0:1], (LANES, LANES))
            rows = slice(half * LANES, (half + 1) * LANES)
            held_lanes = [lane(k, 0), lane(k, 1), lane(k + 1, 0), lane(k + 1, 1), lane(k + 2, other_half(to, half))]
            for n, cols in enumerate(held_lanes):
                centred = gram[pl.ds(start, LANES), cols] - column * sums_ref[0:1, cols]
                if k:
                    gsend[to, rows, n * LANES : (n + 1) * LANES] = centred.astype(jnp.bfloat16)
                else:
                    gown[rows, n * LANES : (n + 1) * LANES] = centred

    for j in (1, 2, 3, 0):
        for k in (2, 1, 3):
            launch(g_copy(k, (a2 + j) % 4))
    for k in range(1, 4):
        source = (a1 + k) % 4
        remote(stat1.at[source], stat1.at[source], s1_send.at[k], s1_recv.at[source], first_peer(source)).wait_recv()
    statg2[...] = stat1[0] + stat1[1] + stat1[2] + stat1[3]
    stat2[a2] = statg2[...]

    def stat2_copy(k):
        return remote(statg2, stat2.at[a2], s2_send.at[k], s2_recv.at[a2], second_peer((a2 + k) % 4))

    for k in range(1, 4):
        launch(stat2_copy(k))
    def stat3_copy(k):
        return remote(statg3, stat3.at[z], s3_send.at[k], s3_recv.at[z], z_peer((z + k) % NZ))

    def between(stat, members):
        group = stat[0]
        for k in range(1, members):
            group = group + stat[k]
        mean = group[0:1, :] / jnp.maximum(group[1:2, :], 1.0)
        for k in range(members):
            spread[k : k + 1, :] = stat[k, 0:1, :] / jnp.maximum(stat[k, 1:2, :], 1.0) - mean
        spread_t[...] = jnp.transpose(spread[...])
        for k in range(members):
            spread[k : k + 1, :] = spread[k : k + 1, :] * stat[k, 1:2, :]
        return group

    def outer(rows, cols):
        return jnp.dot(rows, spread[:, cols], preferred_element_type=jnp.float32, precision=lax.Precision.HIGHEST)

    spread[...] = jnp.zeros_like(spread)
    between(stat1, 4)
    own_start = pl.multiple_of(a1 * CLASS_ROWS, CLASS_ROWS)
    for n in range(4):
        gown[:, n * LANES : (n + 1) * LANES] += outer(spread_t[pl.ds(own_start, CLASS_ROWS), :], lane(n // 2, n % 2))
    for half in range(2):
        gown[half * LANES : (half + 1) * LANES, 4 * LANES :] += outer(
            spread_t[pl.ds(own_start + half * LANES, LANES), :], lane(2, other_half(a1, half))
        )

    def h_copy(k):
        to = (a2 + k) % 4
        return remote(hsend.at[to], hrecv.at[a2], h_send.at[k], h_recv.at[a2], second_peer(to))

    for j in (1, 2, 3, 0):
        sub = (a2 + j) % 4
        rows = pl.ds(pl.multiple_of(sub * SUB_ROWS, SUB_ROWS), SUB_ROWS)
        if j == 0:
            for k in range(1, 4):
                source = (a2 + k) % 4
                remote(statg2, stat2.at[source], s2_send.at[k], s2_recv.at[source], second_peer(source)).wait_recv()
            statg3[...] = stat2[0] + stat2[1] + stat2[2] + stat2[3]
            stat3[z] = statg3[...]
            for k in (4, 3, 5, 2, 6, 1, 7):
                launch(stat3_copy(k))
        for k in range(1, 4):
            source = (a1 + k) % 4
            remote(
                gsend.at[source, rows, :], grecv.at[source, rows, :], g_send.at[k, sub], g_recv.at[source, sub],
                first_peer(source),
            ).wait_recv()
        value = gown[rows, :]
        for k in range(1, 4):
            value = value + grecv[(a1 + k) % 4, rows, :].astype(jnp.float32)
        gown[rows, :] = value
        if j:
            hsend[sub] = value.astype(jnp.bfloat16)
            launch(h_copy(j))

    def mirror_copy(n):
        return remote(
            m1_out.at[n], m1_in.at[a2], m1_send.at[n], m1_recv.at[a2], peer((a1 + 1) % 4, n)
        )

    def half_copy(n):
        return remote(
            m2_out.at[n], m2_in.at[a2], m2_send.at[n], m2_recv.at[a2], peer((a1 + 2) % 4, n)
        )

    for half in range(2):
        mirror = jnp.transpose(gown[half * LANES : (half + 1) * LANES, 4 * LANES :]).astype(jnp.bfloat16)
        for n in range(2):
            m2_out[other_half(a1, half) * 2 + n] = mirror[n * SUB_ROWS : (n + 1) * SUB_ROWS, :]
    for n in range(4):
        launch(half_copy(n))

    mirror = jnp.transpose(gown[:, 2 * LANES : 4 * LANES]).astype(jnp.bfloat16)
    for n in range(4):
        m1_out[n] = mirror[n * SUB_ROWS : (n + 1) * SUB_ROWS, :]
        launch(mirror_copy(n))
    between(stat2, 4)
    row_start = pl.multiple_of(a1 * CLASS_ROWS + a2 * SUB_ROWS, SUB_ROWS)
    column = spread_t[pl.ds(row_start, SUB_ROWS), :]
    value = column[:, 0:1] * spread[0:1, :]
    for k in range(1, 4):
        value = value + column[:, k : k + 1] * spread[k : k + 1, :]
    hown[...] = value
    for k in range(1, 4):
        source = (a2 + k) % 4
        remote(hsend.at[source], hrecv.at[source], h_send.at[k], h_recv.at[source], second_peer(source)).wait_recv()
    value = gown[pl.ds(pl.multiple_of(a2 * SUB_ROWS, SUB_ROWS), SUB_ROWS), :]
    for k in range(1, 4):
        value = value + hrecv[(a2 + k) % 4].astype(jnp.float32)
    own_half = other_half(a1, a2 // 2)
    for n, cols in enumerate((lane(0, 0), lane(0, 1), lane(1, 0), lane(1, 1), lane(2, own_half))):
        hown[:, cols] += value[:, n * LANES : (n + 1) * LANES]
    for n in range(4):
        remote(m1_out.at[n], m1_in.at[n], m1_send.at[n], m1_recv.at[n], peer((a1 + 3) % 4, n)).wait_recv()
    value = m1_in[0].astype(jnp.float32)
    for n in range(1, 4):
        value = value + m1_in[n].astype(jnp.float32)
    hown[:, lane(3, 0)] += value[:, 0:LANES]
    hown[:, lane(3, 1)] += value[:, LANES:]
    for n in range(4):
        remote(m2_out.at[n], m2_in.at[n], m2_send.at[n], m2_recv.at[n], peer((a1 + 2) % 4, n)).wait_recv()
    value = m2_in[0].astype(jnp.float32)
    for n in range(1, 4):
        value = value + m2_in[n].astype(jnp.float32)
    hown[:, lane(2, 1 - own_half)] += value
    own_rows = GROUP // NZ

    for other_z in range(NZ):
        for core in range(CORES):
            start = core * GROUP + other_z * own_rows
            tsend[other_z, core] = hown[start : start + own_rows, :].astype(jnp.bfloat16)

    def t_copy(k, flip):
        to, core = (z + k) % NZ, (c + flip) % CORES
        return remote(
            tsend.at[to, core], trecv.at[c, z], t_send.at[k, flip], t_recv.at[c, z], (x * CORES + core, y * NZ + to)
        )

    for k in (4, 3, 5, 2, 6, 1, 7):
        for flip in range(CORES):
            launch(t_copy(k, flip))
    launch(t_copy(0, 1))
    trecv[c, z] = tsend[z, c]
    for k in range(1, NZ):
        source = (z + k) % NZ
        remote(statg3, stat3.at[source], s3_send.at[k], s3_recv.at[source], z_peer(source)).wait_recv()
    counts = between(stat3, NZ)[1:2, :]
    halves = [
        spread_t[pl.ds(pl.multiple_of(row_start + core * GROUP + z // 2 * 8, 8), 8), :] for core in range(CORES)
    ]
    even = z % 2 == 0
    term = outer(
        jnp.concatenate([jnp.where(even, half[0:own_rows], half[own_rows : 2 * own_rows]) for half in halves], axis=0),
        slice(None),
    )
    low, high = term[0:own_rows, :], term[own_rows : 2 * own_rows, :]
    fsend[...] = jnp.broadcast_to(counts, (2 * own_rows, NFRAMES))
    fsend[0:own_rows, :] = jnp.where(c == 0, high, low)
    last = remote(fsend, frecv, f_send, f_recv, sibling)
    launch(last)

    place = lax.broadcasted_iota(jnp.int32, (own_rows, LANES), 1) // GROUP

    def give(cycle, flip, value, count):
        for k in range(NZ):
            source, core = (z + k) % NZ, (c + flip) % CORES
            if k or flip:
                remote(
                    tsend.at[source, core], trecv.at[cycle, source], t_send.at[k, flip], t_recv.at[cycle, source],
                    (x * CORES + core, y * NZ + source),
                ).wait_recv()
            value = value + trecv[cycle, source].astype(jnp.float32)
        permuted[flip] = value / count
        for row_x in range(4):
            for core in range(CORES):
                piece_of = None
                for row_y in range(4):
                    first = cycle * row_x + (1 - cycle) * row_y
                    second = cycle * row_y + (1 - cycle) * row_x
                    block = pl.ds(pl.multiple_of((first * 2 + second // 2) * LANES, LANES), LANES)
                    shift = (row_y * GROUP + LANES - (second % 2 * 2 + core) * GROUP) % LANES
                    moved = pltpu.roll(permuted[flip, :, block], shift, 1)
                    piece_of = moved if piece_of is None else jnp.where(place == row_y, moved, piece_of)
                block = (row_x * CORES + core) * LANES
                out[cycle, :, block : block + LANES] = piece_of

    give(c, 0, jnp.where(c == 0, low, high), counts)
    last.wait_recv()
    give(1 - c, 1, frecv[0:own_rows, :], frecv[own_rows : own_rows + 1, :])

    finish()


def shards(frames, dead_time, band_width, cycle_label, valid):
    rows = NPIX_GROUP // LANES
    flat = [a.reshape(rows, LANES) for a in (dead_time, band_width, cycle_label, valid)]
    own_rows = GROUP // NZ
    dma = pltpu.SemaphoreType.DMA
    f32, bf16 = jnp.float32, jnp.bfloat16
    any_space = pl.BlockSpec(memory_space=pltpu.HBM)
    vmem = pltpu.VMEM
    out = pl.pallas_call(
        kernel,
        out_shape=jax.ShapeDtypeStruct((CYCLES, own_rows, NFRAMES), f32),
        in_specs=[any_space] * 5,
        out_specs=pl.BlockSpec(memory_space=pltpu.VMEM),
        scratch_shapes=[
            vmem((rows, LANES), f32),
            vmem((rows, LANES), jnp.int32),
            vmem((rows, LANES), jnp.int32),
            vmem((rows, LANES), jnp.int32),
            vmem((CHUNKS, NDEV_FRAME, OWN_FRAMES, LANES), bf16),
            vmem((PAD + NFRAMES + PAD, LANES), f32),
            vmem((NFRAMES, CHIP_PIX), bf16),
            vmem((CHUNKS, NFRAMES, LANES), bf16),
            vmem((NFRAMES, NFRAMES), f32),
            vmem((8, NFRAMES), f32),
            vmem((NFRAMES, 8), f32),
            vmem((4, CLASS_ROWS, HELD), bf16),
            vmem((4, CLASS_ROWS, HELD), bf16),
            vmem((CLASS_ROWS, HELD), f32),
            vmem((4, SUB_ROWS, HELD), bf16),
            vmem((4, SUB_ROWS, HELD), bf16),
            vmem((SUB_ROWS, NFRAMES), f32),
            vmem((NZ, CORES, own_rows, NFRAMES), bf16),
            vmem((CORES, NZ, own_rows, NFRAMES), bf16),
            vmem((4, 2, NFRAMES), f32),
            vmem((4, 2, NFRAMES), f32),
            vmem((NZ, 2, NFRAMES), f32),
            vmem((2, NFRAMES), f32),
            vmem((2, NFRAMES), f32),
            vmem((8, NFRAMES), f32),
            vmem((NFRAMES, 8), f32),
            vmem((2 * own_rows, NFRAMES), f32),
            vmem((2 * own_rows, NFRAMES), f32),
            vmem((4, SUB_ROWS, 2 * LANES), bf16), vmem((4, SUB_ROWS, 2 * LANES), bf16),
            vmem((4, SUB_ROWS, LANES), bf16), vmem((4, SUB_ROWS, LANES), bf16),
            vmem((CORES, own_rows, NFRAMES), f32),
            dma((4,)),
            dma((CHUNKS,)),
            dma((CHUNKS, NDEV_FRAME)), dma((CHUNKS, NDEV_FRAME)),
            dma((CHUNKS,)), dma((CHUNKS,)),
            dma((4,)), dma((4,)),
            dma((4,)), dma((4,)),
            dma((NZ,)), dma((NZ,)),
            dma((4, 4)), dma((4, 4)),
            dma((4,)), dma((4,)),
            dma((NZ, CORES)), dma((CORES, NZ)),
            dma, dma,
            dma((4,)), dma((4,)),
            dma((4,)), dma((4,)),
        ],
        compiler_params=pltpu.CompilerParams(
            collective_id=0, has_side_effects=True, vmem_limit_bytes=60 * 2**20
        ),
    )(frames, *flat)
    return jnp.transpose(out, (1, 0, 2))


def solution(mesh):
    in_specs = (P("frame", "pixel"), P("pixel"), P("pixel"), P("pixel"), P("pixel"))
    out_specs = P(("frame", "pixel"), None, None)
    return jax.shard_map(shards, mesh=mesh, in_specs=in_specs, out_specs=out_specs, check_vma=False)
```

```python
import functools

import jax
import jax.numpy as jnp
from jax import lax
from jax.experimental import pallas as pl
from jax.experimental.pallas import tpu as pltpu
from jax.sharding import PartitionSpec as P

MESH = pl.DeviceIdType.MESH
CYCLES = 2
BAND = 8
CORES = 2
NX = 4
NY = 4
NZ = 8
LANES = 128
GROUP = 32
NFRAMES = 1024
NDEV_FRAME = NX * CORES
OWN_FRAMES = NFRAMES // NDEV_FRAME
NPIX_GROUP = 4096
OWN_PIX = NPIX_GROUP // NDEV_FRAME
CHUNKS = OWN_PIX // LANES
CHIP_PIX = CORES * OWN_PIX
CLASS_ROWS = NFRAMES // 4
SUB_ROWS = CLASS_ROWS // 4
PAD = BAND
TILE = 256
HELD = 640


def remote(src, dst, send_sem, recv_sem, device):
    return pltpu.make_async_remote_copy(
        src_ref=src,
        dst_ref=dst,
        send_sem=send_sem,
        recv_sem=recv_sem,
        device_id=device,
        device_id_type=MESH,
    )


def kernel(
    frames, dead_hbm, band_hbm, label_hbm, valid_hbm,
    out,
    dead, band, label, valid, arrived, rate, smooth, outgoing,
    gram, sums_ref, sums_t, gsend, grecv, gown, hsend, hrecv, hown, tsend, trecv,
    stat1, stat2, stat3, statg2, statg3, spread, spread_t,
    fsend, frecv, m1_out, m1_in, m2_out, m2_in, permuted,
    par_sem, own_sem, a2a_send, a2a_recv, sib_send, sib_recv,
    s1_send, s1_recv, s2_send, s2_recv, s3_send, s3_recv,
    g_send, g_recv, h_send, h_recv, t_send, t_recv, f_send, f_recv,
    m1_send, m1_recv, m2_send, m2_recv,
):
    f = lax.axis_index("frame")
    p = lax.axis_index("pixel")
    x, c = f // CORES, f % CORES
    y, z = p // NZ, p % NZ
    a1 = c * x + (1 - c) * y
    a2 = c * y + (1 - c) * x

    def peer(a, b):
        return ((c * a + (1 - c) * b) * CORES + c, (c * b + (1 - c) * a) * NZ + z)

    def first_peer(a):
        return peer(a, a2)

    def second_peer(b):
        return peer(a1, b)

    def z_peer(other):
        return (f, y * NZ + other)

    def frame_peer(other):
        return (other, p)

    sibling = (x * CORES + (1 - c), p)

    pending = []

    def launch(copy):
        copy.start()
        pending.append(copy)

    def finish():
        for copy in pending:
            copy.wait_send()

    barrier = pltpu.get_barrier_semaphore()
    for k in range(1, NDEV_FRAME):
        pl.semaphore_signal(barrier, inc=1, device_id=frame_peer((f + k) % NDEV_FRAME), device_id_type=MESH)
    for k in range(1, NY):
        pl.semaphore_signal(barrier, inc=1, device_id=(f, ((y + k) % NY) * NZ + z), device_id_type=MESH)
    for k in range(1, NZ):
        pl.semaphore_signal(barrier, inc=1, device_id=z_peer((z + k) % NZ), device_id_type=MESH)
    pl.semaphore_wait(barrier, NDEV_FRAME - 1 + NY - 1 + NZ - 1)

    def piece(owner, chunk):
        return frames.at[:, pl.ds(pl.multiple_of(owner * OWN_PIX + chunk * LANES, LANES), LANES)]

    def a2a_copy(k, chunk):
        to = (f + k) % NDEV_FRAME
        return remote(
            piece(to, chunk), arrived.at[chunk, f], a2a_send.at[chunk, k], a2a_recv.at[chunk, f], frame_peer(to)
        )

    def own_copy(chunk):
        return pltpu.make_async_copy(piece(f, chunk), arrived.at[chunk, f], own_sem.at[chunk])

    for chunk in range(CHUNKS):
        for k in (4, 3, 5, 2, 6, 7, 1):
            launch(a2a_copy(k, chunk))
        own_copy(chunk).start()
    params = [
        pltpu.make_async_copy(src, dst, par_sem.at[n])
        for n, (src, dst) in enumerate(
            ((dead_hbm, dead), (band_hbm, band), (label_hbm, label), (valid_hbm, valid))
        )
    ]
    for copy in params:
        copy.start()
    rate[0:PAD, :] = jnp.zeros((PAD, LANES), jnp.float32)
    rate[PAD + NFRAMES : PAD + NFRAMES + PAD, :] = jnp.zeros((PAD, LANES), jnp.float32)
    for copy in params:
        copy.wait()

    def sib_copy(chunk):
        return remote(
            outgoing.at[chunk],
            smooth.at[:, pl.ds((2 * chunk + 1) * LANES, LANES)],
            sib_send.at[chunk],
            sib_recv.at[chunk],
            sibling,
        )

    contract_last = (((1,), (1,)), ((), ()))

    def accumulate(chunk):
        lanes = slice(2 * chunk * LANES, 2 * (chunk + 1) * LANES)
        sib_copy(chunk).wait_recv()
        part = lax.dot_general(
            jnp.ones((8, 2 * LANES), jnp.bfloat16), smooth[:, lanes], contract_last, preferred_element_type=jnp.float32
        )
        sums_ref[...] = part if chunk == 0 else sums_ref[...] + part

        for m in range(4):
            for n in (m, (m + 1) % 4, (m + 2) % 4):
                rows, cols = slice(m * TILE, (m + 1) * TILE), slice(n * TILE, (n + 1) * TILE)
                product = lax.dot_general(
                    smooth[rows, lanes], smooth[cols, lanes], contract_last, preferred_element_type=jnp.float32
                )
                gram[rows, cols] = product if chunk == 0 else gram[rows, cols] + product

    for chunk in range(CHUNKS):
        own_copy(chunk).wait()
        for k in range(1, NDEV_FRAME):
            source = (f + k) % NDEV_FRAME
            remote(
                piece(source, chunk), arrived.at[chunk, source], a2a_send.at[chunk, k],
                a2a_recv.at[chunk, source], frame_peer(source),
            ).wait_recv()
        row = f * CHUNKS + chunk
        dead_row = dead[pl.ds(row, 1), :]
        width = band[pl.ds(row, 1), :]
        cycle = label[pl.ds(row, 1), :]
        used = valid[pl.ds(row, 1), :] == 1
        mine = jnp.where(used & (cycle == c), 1.0, 0.0)
        other = jnp.where(used & (cycle == 1 - c), 1.0, 0.0)
        within = [jnp.where(width >= k, 1.0, 0.0) for k in range(1, BAND + 1)]
        full = 1.0 / (2 * width + 1).astype(jnp.float32)

        def correct(block, _):
            for half in range(OWN_FRAMES // GROUP):
                count = 4.0 + arrived[chunk, block, half * GROUP : (half + 1) * GROUP, :].astype(jnp.float32)
                rate[pl.ds(pl.multiple_of(PAD + block * OWN_FRAMES + half * GROUP, 8), GROUP), :] = count / (
                    1.0 - dead_row * count
                )
            return 0

        lax.fori_loop(0, NDEV_FRAME, correct, 0, unroll=4)

        def window(start):
            total = rate[pl.ds(start + PAD, GROUP), :]
            for k in range(1, BAND + 1):
                total = total + within[k - 1] * (
                    rate[pl.ds(start + PAD - k, GROUP), :] + rate[pl.ds(start + PAD + k, GROUP), :]
                )
            return total

        def put(block, value):
            row_x, core, row_y = block // 8, block // 4 % 2, block % 4
            along_x, along_y = row_x * 8 + row_y * 2 + core, row_y * 8 + row_x * 2 + core
            own_rows = pl.ds(pl.multiple_of((c * along_x + (1 - c) * along_y) * GROUP, GROUP), GROUP)
            sib_rows = pl.ds(pl.multiple_of((c * along_y + (1 - c) * along_x) * GROUP, GROUP), GROUP)
            smooth[own_rows, 2 * chunk * LANES : (2 * chunk + 1) * LANES] = (value * mine).astype(jnp.bfloat16)
            outgoing[chunk, sib_rows, :] = (value * other).astype(jnp.bfloat16)

        def inside(block, _):
            put(block, window(pl.multiple_of(block * GROUP, GROUP)) * full)
            return 0

        for start in (0, NFRAMES - GROUP):
            frame = start + lax.broadcasted_iota(jnp.int32, (GROUP, LANES), 0)
            span = jnp.minimum(frame + width, NFRAMES - 1) - jnp.maximum(frame - width, 0) + 1
            put(start // GROUP, window(start) / span.astype(jnp.float32))
        lax.fori_loop(1, NFRAMES // GROUP - 1, inside, 0, unroll=5)
        launch(sib_copy(chunk))
        if chunk:
            accumulate(chunk - 1)

    chip_label = label[pl.ds(pl.multiple_of(x * (CHIP_PIX // LANES), 8), CHIP_PIX // LANES), :]
    chip_valid = valid[pl.ds(pl.multiple_of(x * (CHIP_PIX // LANES), 8), CHIP_PIX // LANES), :]
    held = jnp.sum(jnp.where((chip_label == c) & (chip_valid == 1), 1.0, 0.0), axis=(0, 1), keepdims=True)

    accumulate(CHUNKS - 1)
    sums_t[...] = jnp.transpose(sums_ref[...] / jnp.maximum(held, 1.0))
    stat1[a1, 0:1, :] = sums_ref[0:1, :]
    stat1[a1, 1:2, :] = jnp.broadcast_to(held, (1, NFRAMES))

    def stat1_copy(k):
        to = (a1 + k) % 4
        return remote(stat1.at[a1], stat1.at[a1], s1_send.at[k], s1_recv.at[a1], first_peer(to))

    for k in range(1, 4):
        launch(stat1_copy(k))

    def lane(a, half):
        return pl.ds(pl.multiple_of(((a1 + a) % 4 * 2 + half) * LANES, LANES), LANES)

    def other_half(a, half):
        high = a // 2
        return (1 - half) * high + half * (1 - high)

    def g_copy(k, sub):
        to = (a1 + k) % 4
        rows = pl.ds(pl.multiple_of(sub * SUB_ROWS, SUB_ROWS), SUB_ROWS)
        return remote(
            gsend.at[to, rows, :], grecv.at[a1, rows, :], g_send.at[k, sub], g_recv.at[a1, sub], first_peer(to)
        )

    for k in (1, 2, 3, 0):
        to = (a1 + k) % 4
        for half in range(2):
            start = pl.multiple_of(to * CLASS_ROWS + half * LANES, LANES)
            column = jnp.broadcast_to(sums_t[pl.ds(start, LANES), 0:1], (LANES, LANES))
            rows = slice(half * LANES, (half + 1) * LANES)
            held_lanes = [lane(k, 0), lane(k, 1), lane(k + 1, 0), lane(k + 1, 1), lane(k + 2, other_half(to, half))]
            for n, cols in enumerate(held_lanes):
                centred = gram[pl.ds(start, LANES), cols] - column * sums_ref[0:1, cols]
                if k:
                    gsend[to, rows, n * LANES : (n + 1) * LANES] = centred.astype(jnp.bfloat16)
                else:
                    gown[rows, n * LANES : (n + 1) * LANES] = centred

    for j in (1, 2, 3, 0):
        for k in (2, 1, 3):
            launch(g_copy(k, (a2 + j) % 4))
    for k in range(1, 4):
        source = (a1 + k) % 4
        remote(stat1.at[source], stat1.at[source], s1_send.at[k], s1_recv.at[source], first_peer(source)).wait_recv()
    statg2[...] = stat1[0] + stat1[1] + stat1[2] + stat1[3]
    stat2[a2] = statg2[...]

    def stat2_copy(k):
        return remote(statg2, stat2.at[a2], s2_send.at[k], s2_recv.at[a2], second_peer((a2 + k) % 4))

    for k in range(1, 4):
        launch(stat2_copy(k))
    def stat3_copy(k):
        return remote(statg3, stat3.at[z], s3_send.at[k], s3_recv.at[z], z_peer((z + k) % NZ))

    def between(stat, members):
        group = stat[0]
        for k in range(1, members):
            group = group + stat[k]
        mean = group[0:1, :] / jnp.maximum(group[1:2, :], 1.0)
        for k in range(members):
            spread[k : k + 1, :] = stat[k, 0:1, :] / jnp.maximum(stat[k, 1:2, :], 1.0) - mean
        spread_t[...] = jnp.transpose(spread[...])
        for k in range(members):
            spread[k : k + 1, :] = spread[k : k + 1, :] * stat[k, 1:2, :]
        return group

    def outer(rows, cols):
        return jnp.dot(rows, spread[:, cols], preferred_element_type=jnp.float32, precision=lax.Precision.HIGHEST)

    spread[...] = jnp.zeros_like(spread)
    between(stat1, 4)
    own_start = pl.multiple_of(a1 * CLASS_ROWS, CLASS_ROWS)
    for n in range(4):
        gown[:, n * LANES : (n + 1) * LANES] += outer(spread_t[pl.ds(own_start, CLASS_ROWS), :], lane(n // 2, n % 2))
    for half in range(2):
        gown[half * LANES : (half + 1) * LANES, 4 * LANES :] += outer(
            spread_t[pl.ds(own_start + half * LANES, LANES), :], lane(2, other_half(a1, half))
        )

    def h_copy(k):
        to = (a2 + k) % 4
        return remote(hsend.at[to], hrecv.at[a2], h_send.at[k], h_recv.at[a2], second_peer(to))

    for j in (1, 2, 3, 0):
        sub = (a2 + j) % 4
        rows = pl.ds(pl.multiple_of(sub * SUB_ROWS, SUB_ROWS), SUB_ROWS)
        if j == 0:
            for k in range(1, 4):
                source = (a2 + k) % 4
                remote(statg2, stat2.at[source], s2_send.at[k], s2_recv.at[source], second_peer(source)).wait_recv()
            statg3[...] = stat2[0] + stat2[1] + stat2[2] + stat2[3]
            stat3[z] = statg3[...]
            for k in (4, 3, 5, 2, 6, 1, 7):
                launch(stat3_copy(k))
        for k in range(1, 4):
            source = (a1 + k) % 4
            remote(
                gsend.at[source, rows, :], grecv.at[source, rows, :], g_send.at[k, sub], g_recv.at[source, sub],
                first_peer(source),
            ).wait_recv()
        value = gown[rows, :]
        for k in range(1, 4):
            value = value + grecv[(a1 + k) % 4, rows, :].astype(jnp.float32)
        gown[rows, :] = value
        if j:
            hsend[sub] = value.astype(jnp.bfloat16)
            launch(h_copy(j))

    def mirror_copy(n):
        return remote(
            m1_out.at[n], m1_in.at[a2], m1_send.at[n], m1_recv.at[a2], peer((a1 + 1) % 4, n)
        )

    def half_copy(n):
        return remote(
            m2_out.at[n], m2_in.at[a2], m2_send.at[n], m2_recv.at[a2], peer((a1 + 2) % 4, n)
        )

    for half in range(2):
        mirror = jnp.transpose(gown[half * LANES : (half + 1) * LANES, 4 * LANES :]).astype(jnp.bfloat16)
        for n in range(2):
            m2_out[other_half(a1, half) * 2 + n] = mirror[n * SUB_ROWS : (n + 1) * SUB_ROWS, :]
    for n in range(4):
        launch(half_copy(n))

    mirror = jnp.transpose(gown[:, 2 * LANES : 4 * LANES]).astype(jnp.bfloat16)
    for n in range(4):
        m1_out[n] = mirror[n * SUB_ROWS : (n + 1) * SUB_ROWS, :]
        launch(mirror_copy(n))
    between(stat2, 4)
    row_start = pl.multiple_of(a1 * CLASS_ROWS + a2 * SUB_ROWS, SUB_ROWS)
    column = spread_t[pl.ds(row_start, SUB_ROWS), :]
    value = column[:, 0:1] * spread[0:1, :]
    for k in range(1, 4):
        value = value + column[:, k : k + 1] * spread[k : k + 1, :]
    hown[...] = value
    for k in range(1, 4):
        source = (a2 + k) % 4
        remote(hsend.at[source], hrecv.at[source], h_send.at[k], h_recv.at[source], second_peer(source)).wait_recv()
    value = gown[pl.ds(pl.multiple_of(a2 * SUB_ROWS, SUB_ROWS), SUB_ROWS), :]
    for k in range(1, 4):
        value = value + hrecv[(a2 + k) % 4].astype(jnp.float32)
    own_half = other_half(a1, a2 // 2)
    for n, cols in enumerate((lane(0, 0), lane(0, 1), lane(1, 0), lane(1, 1), lane(2, own_half))):
        hown[:, cols] += value[:, n * LANES : (n + 1) * LANES]
    own_rows = GROUP // NZ
    for k in range(1, NZ):
        source = (z + k) % NZ
        remote(statg3, stat3.at[source], s3_send.at[k], s3_recv.at[source], z_peer(source)).wait_recv()
    counts = between(stat3, NZ)[1:2, :]
    halves = [
        spread_t[pl.ds(pl.multiple_of(row_start + core * GROUP + z // 2 * 8, 8), 8), :] for core in range(CORES)
    ]
    even = z % 2 == 0
    term = outer(
        jnp.concatenate([jnp.where(even, half[0:own_rows], half[own_rows : 2 * own_rows]) for half in halves], axis=0),
        slice(None),
    )
    low, high = term[0:own_rows, :], term[own_rows : 2 * own_rows, :]
    fsend[...] = jnp.broadcast_to(counts, (2 * own_rows, NFRAMES))
    fsend[0:own_rows, :] = jnp.where(c == 0, high, low)
    last = remote(fsend, frecv, f_send, f_recv, sibling)
    launch(last)

    for n in range(4):
        remote(m1_out.at[n], m1_in.at[n], m1_send.at[n], m1_recv.at[n], peer((a1 + 3) % 4, n)).wait_recv()
    value = m1_in[0].astype(jnp.float32)
    for n in range(1, 4):
        value = value + m1_in[n].astype(jnp.float32)
    hown[:, lane(3, 0)] += value[:, 0:LANES]
    hown[:, lane(3, 1)] += value[:, LANES:]
    for n in range(4):
        remote(m2_out.at[n], m2_in.at[n], m2_send.at[n], m2_recv.at[n], peer((a1 + 2) % 4, n)).wait_recv()
    value = m2_in[0].astype(jnp.float32)
    for n in range(1, 4):
        value = value + m2_in[n].astype(jnp.float32)
    hown[:, lane(2, 1 - own_half)] += value
    for other_z in range(NZ):
        for core in range(CORES):
            start = core * GROUP + other_z * own_rows
            tsend[other_z, core] = hown[start : start + own_rows, :].astype(jnp.bfloat16)

    def t_copy(k, flip):
        to, core = (z + k) % NZ, (c + flip) % CORES
        return remote(
            tsend.at[to, core], trecv.at[c, z], t_send.at[k, flip], t_recv.at[c, z], (x * CORES + core, y * NZ + to)
        )

    for flip in (1, 0):
        for k in (4, 3, 5, 2, 6, 1, 7):
            launch(t_copy(k, flip))
    launch(t_copy(0, 1))
    trecv[c, z] = tsend[z, c]
    place = lax.broadcasted_iota(jnp.int32, (own_rows, LANES), 1) // GROUP

    def give(cycle, flip, value, count):
        for k in range(NZ):
            source, core = (z + k) % NZ, (c + flip) % CORES
            if k or flip:
                remote(
                    tsend.at[source, core], trecv.at[cycle, source], t_send.at[k, flip], t_recv.at[cycle, source],
                    (x * CORES + core, y * NZ + source),
                ).wait_recv()
            value = value + trecv[cycle, source].astype(jnp.float32)
        permuted[flip] = value / count
        for row_x in range(4):
            for core in range(CORES):
                piece_of = None
                for row_y in range(4):
                    first = cycle * row_x + (1 - cycle) * row_y
                    second = cycle * row_y + (1 - cycle) * row_x
                    block = pl.ds(pl.multiple_of((first * 2 + second // 2) * LANES, LANES), LANES)
                    shift = (row_y * GROUP + LANES - (second % 2 * 2 + core) * GROUP) % LANES
                    moved = pltpu.roll(permuted[flip, :, block], shift, 1)
                    piece_of = moved if piece_of is None else jnp.where(place == row_y, moved, piece_of)
                block = (row_x * CORES + core) * LANES
                out[cycle, :, block : block + LANES] = piece_of

    give(c, 0, jnp.where(c == 0, low, high), counts)
    last.wait_recv()
    give(1 - c, 1, frecv[0:own_rows, :], frecv[own_rows : own_rows + 1, :])

    finish()


def shards(frames, dead_time, band_width, cycle_label, valid):
    rows = NPIX_GROUP // LANES
    flat = [a.reshape(rows, LANES) for a in (dead_time, band_width, cycle_label, valid)]
    own_rows = GROUP // NZ
    dma = pltpu.SemaphoreType.DMA
    f32, bf16 = jnp.float32, jnp.bfloat16
    any_space = pl.BlockSpec(memory_space=pltpu.HBM)
    vmem = pltpu.VMEM
    out = pl.pallas_call(
        kernel,
        out_shape=jax.ShapeDtypeStruct((CYCLES, own_rows, NFRAMES), f32),
        in_specs=[any_space] * 5,
        out_specs=pl.BlockSpec(memory_space=pltpu.VMEM),
        scratch_shapes=[
            vmem((rows, LANES), f32),
            vmem((rows, LANES), jnp.int32),
            vmem((rows, LANES), jnp.int32),
            vmem((rows, LANES), jnp.int32),
            vmem((CHUNKS, NDEV_FRAME, OWN_FRAMES, LANES), bf16),
            vmem((PAD + NFRAMES + PAD, LANES), f32),
            vmem((NFRAMES, CHIP_PIX), bf16),
            vmem((CHUNKS, NFRAMES, LANES), bf16),
            vmem((NFRAMES, NFRAMES), f32),
            vmem((8, NFRAMES), f32),
            vmem((NFRAMES, 8), f32),
            vmem((4, CLASS_ROWS, HELD), bf16),
            vmem((4, CLASS_ROWS, HELD), bf16),
            vmem((CLASS_ROWS, HELD), f32),
            vmem((4, SUB_ROWS, HELD), bf16),
            vmem((4, SUB_ROWS, HELD), bf16),
            vmem((SUB_ROWS, NFRAMES), f32),
            vmem((NZ, CORES, own_rows, NFRAMES), bf16),
            vmem((CORES, NZ, own_rows, NFRAMES), bf16),
            vmem((4, 2, NFRAMES), f32),
            vmem((4, 2, NFRAMES), f32),
            vmem((NZ, 2, NFRAMES), f32),
            vmem((2, NFRAMES), f32),
            vmem((2, NFRAMES), f32),
            vmem((8, NFRAMES), f32),
            vmem((NFRAMES, 8), f32),
            vmem((2 * own_rows, NFRAMES), f32),
            vmem((2 * own_rows, NFRAMES), f32),
            vmem((4, SUB_ROWS, 2 * LANES), bf16), vmem((4, SUB_ROWS, 2 * LANES), bf16),
            vmem((4, SUB_ROWS, LANES), bf16), vmem((4, SUB_ROWS, LANES), bf16),
            vmem((CORES, own_rows, NFRAMES), f32),
            dma((4,)),
            dma((CHUNKS,)),
            dma((CHUNKS, NDEV_FRAME)), dma((CHUNKS, NDEV_FRAME)),
            dma((CHUNKS,)), dma((CHUNKS,)),
            dma((4,)), dma((4,)),
            dma((4,)), dma((4,)),
            dma((NZ,)), dma((NZ,)),
            dma((4, 4)), dma((4, 4)),
            dma((4,)), dma((4,)),
            dma((NZ, CORES)), dma((CORES, NZ)),
            dma, dma,
            dma((4,)), dma((4,)),
            dma((4,)), dma((4,)),
        ],
        compiler_params=pltpu.CompilerParams(
            collective_id=0, has_side_effects=True, vmem_limit_bytes=60 * 2**20
        ),
    )(frames, *flat)
    return jnp.transpose(out, (1, 0, 2))


def solution(mesh):
    in_specs = (P("frame", "pixel"), P("pixel"), P("pixel"), P("pixel"), P("pixel"))
    out_specs = P(("frame", "pixel"), None, None)
    return jax.shard_map(shards, mesh=mesh, in_specs=in_specs, out_specs=out_specs, check_vma=False)
```

```python
import functools

import jax
import jax.numpy as jnp
from jax import lax
from jax.experimental import pallas as pl
from jax.experimental.pallas import tpu as pltpu
from jax.sharding import PartitionSpec as P

MESH = pl.DeviceIdType.MESH
CYCLES = 2
BAND = 8
CORES = 2
NX = 4
NY = 4
NZ = 8
LANES = 128
GROUP = 32
NFRAMES = 1024
NDEV_FRAME = NX * CORES
OWN_FRAMES = NFRAMES // NDEV_FRAME
NPIX_GROUP = 4096
OWN_PIX = NPIX_GROUP // NDEV_FRAME
CHUNKS = OWN_PIX // LANES
CHIP_PIX = CORES * OWN_PIX
CLASS_ROWS = NFRAMES // 4
SUB_ROWS = CLASS_ROWS // 4
PAD = BAND
TILE = 256
HELD = 640


def remote(src, dst, send_sem, recv_sem, device):
    return pltpu.make_async_remote_copy(
        src_ref=src,
        dst_ref=dst,
        send_sem=send_sem,
        recv_sem=recv_sem,
        device_id=device,
        device_id_type=MESH,
    )


def kernel(
    frames, dead_hbm, band_hbm, label_hbm, valid_hbm,
    out,
    dead, band, label, valid, arrived, rate, smooth, outgoing,
    gram, sums_ref, sums_t, gsend, grecv, gown, hsend, hrecv, hown, tsend, trecv,
    stat1, stat2, stat3, statg2, statg3, spread, spread_t,
    fsend, frecv, m1_out, m1_in, m2_out, m2_in, permuted,
    par_sem, own_sem, a2a_send, a2a_recv, sib_send, sib_recv,
    s1_send, s1_recv, s2_send, s2_recv, s3_send, s3_recv,
    g_send, g_recv, h_send, h_recv, t_send, t_recv, f_send, f_recv,
    m1_send, m1_recv, m2_send, m2_recv,
):
    f = lax.axis_index("frame")
    p = lax.axis_index("pixel")
    x, c = f // CORES, f % CORES
    y, z = p // NZ, p % NZ
    a1 = c * x + (1 - c) * y
    a2 = c * y + (1 - c) * x

    def peer(a, b):
        return ((c * a + (1 - c) * b) * CORES + c, (c * b + (1 - c) * a) * NZ + z)

    def first_peer(a):
        return peer(a, a2)

    def second_peer(b):
        return peer(a1, b)

    def z_peer(other):
        return (f, y * NZ + other)

    def frame_peer(other):
        return (other, p)

    sibling = (x * CORES + (1 - c), p)

    pending = []

    def launch(copy):
        copy.start()
        pending.append(copy)

    def finish():
        for copy in pending:
            copy.wait_send()

    barrier = pltpu.get_barrier_semaphore()
    for k in range(1, NDEV_FRAME):
        pl.semaphore_signal(barrier, inc=1, device_id=frame_peer((f + k) % NDEV_FRAME), device_id_type=MESH)
    for k in range(1, NY):
        pl.semaphore_signal(barrier, inc=1, device_id=(f, ((y + k) % NY) * NZ + z), device_id_type=MESH)
    for k in range(1, NZ):
        pl.semaphore_signal(barrier, inc=1, device_id=z_peer((z + k) % NZ), device_id_type=MESH)
    pl.semaphore_wait(barrier, NDEV_FRAME - 1 + NY - 1 + NZ - 1)

    def piece(owner, chunk):
        return frames.at[:, pl.ds(pl.multiple_of(owner * OWN_PIX + chunk * LANES, LANES), LANES)]

    def a2a_copy(k, chunk):
        to = (f + k) % NDEV_FRAME
        return remote(
            piece(to, chunk), arrived.at[chunk, f], a2a_send.at[chunk, k], a2a_recv.at[chunk, f], frame_peer(to)
        )

    def own_copy(chunk):
        return pltpu.make_async_copy(piece(f, chunk), arrived.at[chunk, f], own_sem.at[chunk])

    for chunk in range(CHUNKS):
        for k in (4, 3, 5, 2, 6, 7, 1):
            launch(a2a_copy(k, chunk))
        own_copy(chunk).start()
    params = [
        pltpu.make_async_copy(src, dst, par_sem.at[n])
        for n, (src, dst) in enumerate(
            ((dead_hbm, dead), (band_hbm, band), (label_hbm, label), (valid_hbm, valid))
        )
    ]
    for copy in params:
        copy.start()
    rate[0:PAD, :] = jnp.zeros((PAD, LANES), jnp.float32)
    rate[PAD + NFRAMES : PAD + NFRAMES + PAD, :] = jnp.zeros((PAD, LANES), jnp.float32)
    for copy in params:
        copy.wait()

    def sib_copy(chunk):
        return remote(
            outgoing.at[chunk],
            smooth.at[:, pl.ds((2 * chunk + 1) * LANES, LANES)],
            sib_send.at[chunk],
            sib_recv.at[chunk],
            sibling,
        )

    contract_last = (((1,), (1,)), ((), ()))

    def accumulate(chunk):
        lanes = slice(2 * chunk * LANES, 2 * (chunk + 1) * LANES)
        sib_copy(chunk).wait_recv()
        part = lax.dot_general(
            jnp.ones((8, 2 * LANES), jnp.bfloat16), smooth[:, lanes], contract_last, preferred_element_type=jnp.float32
        )
        sums_ref[...] = part if chunk == 0 else sums_ref[...] + part

        for m in range(4):
            for n in (m, (m + 1) % 4, (m + 2) % 4):
                rows, cols = slice(m * TILE, (m + 1) * TILE), slice(n * TILE, (n + 1) * TILE)
                product = lax.dot_general(
                    smooth[rows, lanes], smooth[cols, lanes], contract_last, preferred_element_type=jnp.float32
                )
                gram[rows, cols] = product if chunk == 0 else gram[rows, cols] + product

    for chunk in range(CHUNKS):
        own_copy(chunk).wait()
        for k in range(1, NDEV_FRAME):
            source = (f + k) % NDEV_FRAME
            remote(
                piece(source, chunk), arrived.at[chunk, source], a2a_send.at[chunk, k],
                a2a_recv.at[chunk, source], frame_peer(source),
            ).wait_recv()
        row = f * CHUNKS + chunk
        dead_row = dead[pl.ds(row, 1), :]
        width = band[pl.ds(row, 1), :]
        cycle = label[pl.ds(row, 1), :]
        used = valid[pl.ds(row, 1), :] == 1
        mine = jnp.where(used & (cycle == c), 1.0, 0.0)
        other = jnp.where(used & (cycle == 1 - c), 1.0, 0.0)
        within = [jnp.where(width >= k, 1.0, 0.0) for k in range(1, BAND + 1)]
        full = 1.0 / (2 * width + 1).astype(jnp.float32)

        def correct(block, _):
            for half in range(OWN_FRAMES // GROUP):
                count = 4.0 + arrived[chunk, block, half * GROUP : (half + 1) * GROUP, :].astype(jnp.float32)
                rate[pl.ds(pl.multiple_of(PAD + block * OWN_FRAMES + half * GROUP, 8), GROUP), :] = count / (
                    1.0 - dead_row * count
                )
            return 0

        lax.fori_loop(0, NDEV_FRAME, correct, 0, unroll=4)

        def window(start):
            total = rate[pl.ds(start + PAD, GROUP), :]
            for k in range(1, BAND + 1):
                total = total + within[k - 1] * (
                    rate[pl.ds(start + PAD - k, GROUP), :] + rate[pl.ds(start + PAD + k, GROUP), :]
                )
            return total

        def put(block, value):
            row_x, core, row_y = block // 8, block // 4 % 2, block % 4
            along_x, along_y = row_x * 8 + row_y * 2 + core, row_y * 8 + row_x * 2 + core
            own_rows = pl.ds(pl.multiple_of((c * along_x + (1 - c) * along_y) * GROUP, GROUP), GROUP)
            sib_rows = pl.ds(pl.multiple_of((c * along_y + (1 - c) * along_x) * GROUP, GROUP), GROUP)
            smooth[own_rows, 2 * chunk * LANES : (2 * chunk + 1) * LANES] = (value * mine).astype(jnp.bfloat16)
            outgoing[chunk, sib_rows, :] = (value * other).astype(jnp.bfloat16)

        def inside(block, _):
            put(block, window(pl.multiple_of(block * GROUP, GROUP)) * full)
            return 0

        for start in (0, NFRAMES - GROUP):
            frame = start + lax.broadcasted_iota(jnp.int32, (GROUP, LANES), 0)
            span = jnp.minimum(frame + width, NFRAMES - 1) - jnp.maximum(frame - width, 0) + 1
            put(start // GROUP, window(start) / span.astype(jnp.float32))
        lax.fori_loop(1, NFRAMES // GROUP - 1, inside, 0, unroll=5)
        launch(sib_copy(chunk))
        if chunk:
            accumulate(chunk - 1)

    chip_label = label[pl.ds(pl.multiple_of(x * (CHIP_PIX // LANES), 8), CHIP_PIX // LANES), :]
    chip_valid = valid[pl.ds(pl.multiple_of(x * (CHIP_PIX // LANES), 8), CHIP_PIX // LANES), :]
    held = jnp.sum(jnp.where((chip_label == c) & (chip_valid == 1), 1.0, 0.0), axis=(0, 1), keepdims=True)

    accumulate(CHUNKS - 1)
    sums_t[...] = jnp.transpose(sums_ref[...] / jnp.maximum(held, 1.0))
    stat1[a1, 0:1, :] = sums_ref[0:1, :]
    stat1[a1, 1:2, :] = jnp.broadcast_to(held, (1, NFRAMES))

    def stat1_copy(k):
        to = (a1 + k) % 4
        return remote(stat1.at[a1], stat1.at[a1], s1_send.at[k], s1_recv.at[a1], first_peer(to))

    for k in range(1, 4):
        launch(stat1_copy(k))

    def lane(a, half):
        return pl.ds(pl.multiple_of(((a1 + a) % 4 * 2 + half) * LANES, LANES), LANES)

    def other_half(a, half):
        high = a // 2
        return (1 - half) * high + half * (1 - high)

    def g_copy(k, sub):
        to = (a1 + k) % 4
        rows = pl.ds(pl.multiple_of(sub * SUB_ROWS, SUB_ROWS), SUB_ROWS)
        return remote(
            gsend.at[to, rows, :], grecv.at[a1, rows, :], g_send.at[k, sub], g_recv.at[a1, sub], first_peer(to)
        )

    for k in (1, 2, 3, 0):
        to = (a1 + k) % 4
        for half in range(2):
            start = pl.multiple_of(to * CLASS_ROWS + half * LANES, LANES)
            column = jnp.broadcast_to(sums_t[pl.ds(start, LANES), 0:1], (LANES, LANES))
            rows = slice(half * LANES, (half + 1) * LANES)
            held_lanes = [lane(k, 0), lane(k, 1), lane(k + 1, 0), lane(k + 1, 1), lane(k + 2, other_half(to, half))]
            for n, cols in enumerate(held_lanes):
                centred = gram[pl.ds(start, LANES), cols] - column * sums_ref[0:1, cols]
                if k:
                    gsend[to, rows, n * LANES : (n + 1) * LANES] = centred.astype(jnp.bfloat16)
                else:
                    gown[rows, n * LANES : (n + 1) * LANES] = centred

    for j in (1, 2, 3, 0):
        for k in (2, 1, 3):
            launch(g_copy(k, (a2 + j) % 4))
    for k in range(1, 4):
        source = (a1 + k) % 4
        remote(stat1.at[source], stat1.at[source], s1_send.at[k], s1_recv.at[source], first_peer(source)).wait_recv()
    statg2[...] = stat1[0] + stat1[1] + stat1[2] + stat1[3]
    stat2[a2] = statg2[...]

    def stat2_copy(k):
        return remote(statg2, stat2.at[a2], s2_send.at[k], s2_recv.at[a2], second_peer((a2 + k) % 4))

    for k in range(1, 4):
        launch(stat2_copy(k))
    def stat3_copy(k):
        return remote(statg3, stat3.at[z], s3_send.at[k], s3_recv.at[z], z_peer((z + k) % NZ))

    def between(stat, members):
        group = stat[0]
        for k in range(1, members):
            group = group + stat[k]
        mean = group[0:1, :] / jnp.maximum(group[1:2, :], 1.0)
        for k in range(members):
            spread[k : k + 1, :] = stat[k, 0:1, :] / jnp.maximum(stat[k, 1:2, :], 1.0) - mean
        spread_t[...] = jnp.transpose(spread[...])
        for k in range(members):
            spread[k : k + 1, :] = spread[k : k + 1, :] * stat[k, 1:2, :]
        return group

    def outer(rows, cols):
        return jnp.dot(rows, spread[:, cols], preferred_element_type=jnp.float32, precision=lax.Precision.HIGHEST)

    spread[...] = jnp.zeros_like(spread)
    between(stat1, 4)
    own_start = pl.multiple_of(a1 * CLASS_ROWS, CLASS_ROWS)
    for n in range(4):
        gown[:, n * LANES : (n + 1) * LANES] += outer(spread_t[pl.ds(own_start, CLASS_ROWS), :], lane(n // 2, n % 2))
    for half in range(2):
        gown[half * LANES : (half + 1) * LANES, 4 * LANES :] += outer(
            spread_t[pl.ds(own_start + half * LANES, LANES), :], lane(2, other_half(a1, half))
        )

    def h_copy(k):
        to = (a2 + k) % 4
        return remote(hsend.at[to], hrecv.at[a2], h_send.at[k], h_recv.at[a2], second_peer(to))

    for j in (1, 2, 3, 0):
        sub = (a2 + j) % 4
        rows = pl.ds(pl.multiple_of(sub * SUB_ROWS, SUB_ROWS), SUB_ROWS)
        if j == 0:
            for k in range(1, 4):
                source = (a2 + k) % 4
                remote(statg2, stat2.at[source], s2_send.at[k], s2_recv.at[source], second_peer(source)).wait_recv()
            statg3[...] = stat2[0] + stat2[1] + stat2[2] + stat2[3]
            stat3[z] = statg3[...]
            for k in (4, 3, 5, 2, 6, 1, 7):
                launch(stat3_copy(k))
        for k in range(1, 4):
            source = (a1 + k) % 4
            remote(
                gsend.at[source, rows, :], grecv.at[source, rows, :], g_send.at[k, sub], g_recv.at[source, sub],
                first_peer(source),
            ).wait_recv()
        value = gown[rows, :]
        for k in range(1, 4):
            value = value + grecv[(a1 + k) % 4, rows, :].astype(jnp.float32)
        gown[rows, :] = value
        if j:
            hsend[sub] = value.astype(jnp.bfloat16)
            launch(h_copy(j))

    def mirror_copy(n):
        return remote(
            m1_out.at[n], m1_in.at[a2], m1_send.at[n], m1_recv.at[a2], peer((a1 + 1) % 4, n)
        )

    def half_copy(n):
        return remote(
            m2_out.at[n], m2_in.at[a2], m2_send.at[n], m2_recv.at[a2], peer((a1 + 2) % 4, n)
        )

    for half in range(2):
        mirror = jnp.transpose(gown[half * LANES : (half + 1) * LANES, 4 * LANES :]).astype(jnp.bfloat16)
        for n in range(2):
            to = other_half(a1, half) * 2 + n
            m2_out[to] = mirror[n * SUB_ROWS : (n + 1) * SUB_ROWS, :]
            launch(half_copy(to))

    mirror = jnp.transpose(gown[:, 2 * LANES : 4 * LANES]).astype(jnp.bfloat16)
    for n in range(4):
        m1_out[n] = mirror[n * SUB_ROWS : (n + 1) * SUB_ROWS, :]
        launch(mirror_copy(n))
    between(stat2, 4)
    row_start = pl.multiple_of(a1 * CLASS_ROWS + a2 * SUB_ROWS, SUB_ROWS)
    column = spread_t[pl.ds(row_start, SUB_ROWS), :]
    value = column[:, 0:1] * spread[0:1, :]
    for k in range(1, 4):
        value = value + column[:, k : k + 1] * spread[k : k + 1, :]
    hown[...] = value
    for k in range(1, 4):
        source = (a2 + k) % 4
        remote(hsend.at[source], hrecv.at[source], h_send.at[k], h_recv.at[source], second_peer(source)).wait_recv()
    value = gown[pl.ds(pl.multiple_of(a2 * SUB_ROWS, SUB_ROWS), SUB_ROWS), :]
    for k in range(1, 4):
        value = value + hrecv[(a2 + k) % 4].astype(jnp.float32)
    own_half = other_half(a1, a2 // 2)
    for n, cols in enumerate((lane(0, 0), lane(0, 1), lane(1, 0), lane(1, 1), lane(2, own_half))):
        hown[:, cols] += value[:, n * LANES : (n + 1) * LANES]
    own_rows = GROUP // NZ
    for k in range(1, NZ):
        source = (z + k) % NZ
        remote(statg3, stat3.at[source], s3_send.at[k], s3_recv.at[source], z_peer(source)).wait_recv()
    counts = between(stat3, NZ)[1:2, :]
    halves = [
        spread_t[pl.ds(pl.multiple_of(row_start + core * GROUP + z // 2 * 8, 8), 8), :] for core in range(CORES)
    ]
    even = z % 2 == 0
    term = outer(
        jnp.concatenate([jnp.where(even, half[0:own_rows], half[own_rows : 2 * own_rows]) for half in halves], axis=0),
        slice(None),
    )
    low, high = term[0:own_rows, :], term[own_rows : 2 * own_rows, :]
    fsend[...] = jnp.broadcast_to(counts, (2 * own_rows, NFRAMES))
    fsend[0:own_rows, :] = jnp.where(c == 0, high, low)
    last = remote(fsend, frecv, f_send, f_recv, sibling)
    launch(last)

    for n in range(4):
        remote(m1_out.at[n], m1_in.at[n], m1_send.at[n], m1_recv.at[n], peer((a1 + 3) % 4, n)).wait_recv()
    value = m1_in[0].astype(jnp.float32)
    for n in range(1, 4):
        value = value + m1_in[n].astype(jnp.float32)
    hown[:, lane(3, 0)] += value[:, 0:LANES]
    hown[:, lane(3, 1)] += value[:, LANES:]
    for n in range(4):
        remote(m2_out.at[n], m2_in.at[n], m2_send.at[n], m2_recv.at[n], peer((a1 + 2) % 4, n)).wait_recv()
    value = m2_in[0].astype(jnp.float32)
    for n in range(1, 4):
        value = value + m2_in[n].astype(jnp.float32)
    hown[:, lane(2, 1 - own_half)] += value
    for other_z in range(NZ):
        for core in range(CORES):
            start = core * GROUP + other_z * own_rows
            tsend[other_z, core] = hown[start : start + own_rows, :].astype(jnp.bfloat16)

    def t_copy(k, flip):
        to, core = (z + k) % NZ, (c + flip) % CORES
        return remote(
            tsend.at[to, core], trecv.at[c, z], t_send.at[k, flip], t_recv.at[c, z], (x * CORES + core, y * NZ + to)
        )

    for flip in (1, 0):
        for k in (4, 3, 5, 2, 6, 1, 7):
            launch(t_copy(k, flip))
    launch(t_copy(0, 1))
    trecv[c, z] = tsend[z, c]
    place = lax.broadcasted_iota(jnp.int32, (own_rows, LANES), 1) // GROUP

    def give(cycle, flip, value, count):
        for k in range(NZ):
            source, core = (z + k) % NZ, (c + flip) % CORES
            if k or flip:
                remote(
                    tsend.at[source, core], trecv.at[cycle, source], t_send.at[k, flip], t_recv.at[cycle, source],
                    (x * CORES + core, y * NZ + source),
                ).wait_recv()
            value = value + trecv[cycle, source].astype(jnp.float32)
        permuted[flip] = value / count
        for row_x in range(4):
            for core in range(CORES):
                piece_of = None
                for row_y in range(4):
                    first = cycle * row_x + (1 - cycle) * row_y
                    second = cycle * row_y + (1 - cycle) * row_x
                    block = pl.ds(pl.multiple_of((first * 2 + second // 2) * LANES, LANES), LANES)
                    shift = (row_y * GROUP + LANES - (second % 2 * 2 + core) * GROUP) % LANES
                    moved = pltpu.roll(permuted[flip, :, block], shift, 1)
                    piece_of = moved if piece_of is None else jnp.where(place == row_y, moved, piece_of)
                block = (row_x * CORES + core) * LANES
                out[cycle, :, block : block + LANES] = piece_of

    give(c, 0, jnp.where(c == 0, low, high), counts)
    last.wait_recv()
    give(1 - c, 1, frecv[0:own_rows, :], frecv[own_rows : own_rows + 1, :])

    finish()


def shards(frames, dead_time, band_width, cycle_label, valid):
    rows = NPIX_GROUP // LANES
    flat = [a.reshape(rows, LANES) for a in (dead_time, band_width, cycle_label, valid)]
    own_rows = GROUP // NZ
    dma = pltpu.SemaphoreType.DMA
    f32, bf16 = jnp.float32, jnp.bfloat16
    any_space = pl.BlockSpec(memory_space=pltpu.HBM)
    vmem = pltpu.VMEM
    out = pl.pallas_call(
        kernel,
        out_shape=jax.ShapeDtypeStruct((CYCLES, own_rows, NFRAMES), f32),
        in_specs=[any_space] * 5,
        out_specs=pl.BlockSpec(memory_space=pltpu.VMEM),
        scratch_shapes=[
            vmem((rows, LANES), f32),
            vmem((rows, LANES), jnp.int32),
            vmem((rows, LANES), jnp.int32),
            vmem((rows, LANES), jnp.int32),
            vmem((CHUNKS, NDEV_FRAME, OWN_FRAMES, LANES), bf16),
            vmem((PAD + NFRAMES + PAD, LANES), f32),
            vmem((NFRAMES, CHIP_PIX), bf16),
            vmem((CHUNKS, NFRAMES, LANES), bf16),
            vmem((NFRAMES, NFRAMES), f32),
            vmem((8, NFRAMES), f32),
            vmem((NFRAMES, 8), f32),
            vmem((4, CLASS_ROWS, HELD), bf16),
            vmem((4, CLASS_ROWS, HELD), bf16),
            vmem((CLASS_ROWS, HELD), f32),
            vmem((4, SUB_ROWS, HELD), bf16),
            vmem((4, SUB_ROWS, HELD), bf16),
            vmem((SUB_ROWS, NFRAMES), f32),
            vmem((NZ, CORES, own_rows, NFRAMES), bf16),
            vmem((CORES, NZ, own_rows, NFRAMES), bf16),
            vmem((4, 2, NFRAMES), f32),
            vmem((4, 2, NFRAMES), f32),
            vmem((NZ, 2, NFRAMES), f32),
            vmem((2, NFRAMES), f32),
            vmem((2, NFRAMES), f32),
            vmem((8, NFRAMES), f32),
            vmem((NFRAMES, 8), f32),
            vmem((2 * own_rows, NFRAMES), f32),
            vmem((2 * own_rows, NFRAMES), f32),
            vmem((4, SUB_ROWS, 2 * LANES), bf16), vmem((4, SUB_ROWS, 2 * LANES), bf16),
            vmem((4, SUB_ROWS, LANES), bf16), vmem((4, SUB_ROWS, LANES), bf16),
            vmem((CORES, own_rows, NFRAMES), f32),
            dma((4,)),
            dma((CHUNKS,)),
            dma((CHUNKS, NDEV_FRAME)), dma((CHUNKS, NDEV_FRAME)),
            dma((CHUNKS,)), dma((CHUNKS,)),
            dma((4,)), dma((4,)),
            dma((4,)), dma((4,)),
            dma((NZ,)), dma((NZ,)),
            dma((4, 4)), dma((4, 4)),
            dma((4,)), dma((4,)),
            dma((NZ, CORES)), dma((CORES, NZ)),
            dma, dma,
            dma((4,)), dma((4,)),
            dma((4,)), dma((4,)),
        ],
        compiler_params=pltpu.CompilerParams(
            collective_id=0, has_side_effects=True, vmem_limit_bytes=60 * 2**20
        ),
    )(frames, *flat)
    return jnp.transpose(out, (1, 0, 2))


def solution(mesh):
    in_specs = (P("frame", "pixel"), P("pixel"), P("pixel"), P("pixel"), P("pixel"))
    out_specs = P(("frame", "pixel"), None, None)
    return jax.shard_map(shards, mesh=mesh, in_specs=in_specs, out_specs=out_specs, check_vma=False)
```

```python
import functools

import jax
import jax.numpy as jnp
from jax import lax
from jax.experimental import pallas as pl
from jax.experimental.pallas import tpu as pltpu
from jax.sharding import PartitionSpec as P

MESH = pl.DeviceIdType.MESH
CYCLES = 2
BAND = 8
CORES = 2
NX = 4
NY = 4
NZ = 8
LANES = 128
GROUP = 32
NFRAMES = 1024
NDEV_FRAME = NX * CORES
OWN_FRAMES = NFRAMES // NDEV_FRAME
NPIX_GROUP = 4096
OWN_PIX = NPIX_GROUP // NDEV_FRAME
CHUNKS = OWN_PIX // LANES
CHIP_PIX = CORES * OWN_PIX
CLASS_ROWS = NFRAMES // 4
SUB_ROWS = CLASS_ROWS // 4
PAD = BAND
TILE = 256
HELD = 640


def remote(src, dst, send_sem, recv_sem, device):
    return pltpu.make_async_remote_copy(
        src_ref=src,
        dst_ref=dst,
        send_sem=send_sem,
        recv_sem=recv_sem,
        device_id=device,
        device_id_type=MESH,
    )


def kernel(
    frames, dead_hbm, band_hbm, label_hbm, valid_hbm,
    out,
    dead, band, label, valid, arrived, rate, smooth, outgoing,
    gram, sums_ref, sums_t, gsend, grecv, gown, hsend, hrecv, hown, tsend, trecv,
    stat1, stat2, stat3, statg2, statg3, spread, spread_t,
    fsend, frecv, m1_out, m1_in, m2_out, m2_in, permuted,
    par_sem, own_sem, a2a_send, a2a_recv, sib_send, sib_recv,
    s1_send, s1_recv, s2_send, s2_recv, s3_send, s3_recv,
    g_send, g_recv, h_send, h_recv, t_send, t_recv, f_send, f_recv,
    m1_send, m1_recv, m2_send, m2_recv,
):
    f = lax.axis_index("frame")
    p = lax.axis_index("pixel")
    x, c = f // CORES, f % CORES
    y, z = p // NZ, p % NZ
    a1 = c * x + (1 - c) * y
    a2 = c * y + (1 - c) * x

    def peer(a, b):
        return ((c * a + (1 - c) * b) * CORES + c, (c * b + (1 - c) * a) * NZ + z)

    def first_peer(a):
        return peer(a, a2)

    def second_peer(b):
        return peer(a1, b)

    def z_peer(other):
        return (f, y * NZ + other)

    def frame_peer(other):
        return (other, p)

    sibling = (x * CORES + (1 - c), p)

    pending = []

    def launch(copy):
        copy.start()
        pending.append(copy)

    def finish():
        for copy in pending:
            copy.wait_send()

    barrier = pltpu.get_barrier_semaphore()
    for k in range(1, NDEV_FRAME):
        pl.semaphore_signal(barrier, inc=1, device_id=frame_peer((f + k) % NDEV_FRAME), device_id_type=MESH)
    for k in range(1, NY):
        pl.semaphore_signal(barrier, inc=1, device_id=(f, ((y + k) % NY) * NZ + z), device_id_type=MESH)
    for k in range(1, NZ):
        pl.semaphore_signal(barrier, inc=1, device_id=z_peer((z + k) % NZ), device_id_type=MESH)
    pl.semaphore_wait(barrier, NDEV_FRAME - 1 + NY - 1 + NZ - 1)

    def piece(owner, chunk):
        return frames.at[:, pl.ds(pl.multiple_of(owner * OWN_PIX + chunk * LANES, LANES), LANES)]

    def a2a_copy(k, chunk):
        to = (f + k) % NDEV_FRAME
        return remote(
            piece(to, chunk), arrived.at[chunk, f], a2a_send.at[chunk, k], a2a_recv.at[chunk, f], frame_peer(to)
        )

    def own_copy(chunk):
        return pltpu.make_async_copy(piece(f, chunk), arrived.at[chunk, f], own_sem.at[chunk])

    for chunk in range(CHUNKS):
        for k in (4, 3, 5, 2, 6, 7, 1):
            launch(a2a_copy(k, chunk))
        own_copy(chunk).start()
    params = [
        pltpu.make_async_copy(src, dst, par_sem.at[n])
        for n, (src, dst) in enumerate(
            ((dead_hbm, dead), (band_hbm, band), (label_hbm, label), (valid_hbm, valid))
        )
    ]
    for copy in params:
        copy.start()
    rate[0:PAD, :] = jnp.zeros((PAD, LANES), jnp.float32)
    rate[PAD + NFRAMES : PAD + NFRAMES + PAD, :] = jnp.zeros((PAD, LANES), jnp.float32)
    for copy in params:
        copy.wait()

    def sib_copy(chunk):
        return remote(
            outgoing.at[chunk],
            smooth.at[:, pl.ds((2 * chunk + 1) * LANES, LANES)],
            sib_send.at[chunk],
            sib_recv.at[chunk],
            sibling,
        )

    contract_last = (((1,), (1,)), ((), ()))

    def accumulate(chunk):
        lanes = slice(2 * chunk * LANES, 2 * (chunk + 1) * LANES)
        sib_copy(chunk).wait_recv()
        part = lax.dot_general(
            jnp.ones((8, 2 * LANES), jnp.bfloat16), smooth[:, lanes], contract_last, preferred_element_type=jnp.float32
        )
        sums_ref[...] = part if chunk == 0 else sums_ref[...] + part

        for m in range(4):
            for n in (m, (m + 1) % 4, (m + 2) % 4):
                rows, cols = slice(m * TILE, (m + 1) * TILE), slice(n * TILE, (n + 1) * TILE)
                product = lax.dot_general(
                    smooth[rows, lanes], smooth[cols, lanes], contract_last, preferred_element_type=jnp.float32
                )
                gram[rows, cols] = product if chunk == 0 else gram[rows, cols] + product

    for chunk in range(CHUNKS):
        own_copy(chunk).wait()
        for k in range(1, NDEV_FRAME):
            source = (f + k) % NDEV_FRAME
            remote(
                piece(source, chunk), arrived.at[chunk, source], a2a_send.at[chunk, k],
                a2a_recv.at[chunk, source], frame_peer(source),
            ).wait_recv()
        row = f * CHUNKS + chunk
        dead_row = dead[pl.ds(row, 1), :]
        width = band[pl.ds(row, 1), :]
        cycle = label[pl.ds(row, 1), :]
        used = valid[pl.ds(row, 1), :] == 1
        mine = jnp.where(used & (cycle == c), 1.0, 0.0)
        other = jnp.where(used & (cycle == 1 - c), 1.0, 0.0)
        within = [jnp.where(width >= k, 1.0, 0.0) for k in range(1, BAND + 1)]
        full = 1.0 / (2 * width + 1).astype(jnp.float32)

        def correct(block, _):
            for half in range(OWN_FRAMES // GROUP):
                count = 4.0 + arrived[chunk, block, half * GROUP : (half + 1) * GROUP, :].astype(jnp.float32)
                rate[pl.ds(pl.multiple_of(PAD + block * OWN_FRAMES + half * GROUP, 8), GROUP), :] = count / (
                    1.0 - dead_row * count
                )
            return 0

        lax.fori_loop(0, NDEV_FRAME, correct, 0, unroll=2)

        def window(start):
            total = rate[pl.ds(start + PAD, GROUP), :]
            for k in range(1, BAND + 1):
                total = total + within[k - 1] * (
                    rate[pl.ds(start + PAD - k, GROUP), :] + rate[pl.ds(start + PAD + k, GROUP), :]
                )
            return total

        def put(block, value):
            row_x, core, row_y = block // 8, block // 4 % 2, block % 4
            along_x, along_y = row_x * 8 + row_y * 2 + core, row_y * 8 + row_x * 2 + core
            own_rows = pl.ds(pl.multiple_of((c * along_x + (1 - c) * along_y) * GROUP, GROUP), GROUP)
            sib_rows = pl.ds(pl.multiple_of((c * along_y + (1 - c) * along_x) * GROUP, GROUP), GROUP)
            smooth[own_rows, 2 * chunk * LANES : (2 * chunk + 1) * LANES] = (value * mine).astype(jnp.bfloat16)
            outgoing[chunk, sib_rows, :] = (value * other).astype(jnp.bfloat16)

        def inside(block, _):
            put(block, window(pl.multiple_of(block * GROUP, GROUP)) * full)
            return 0

        for start in (0, NFRAMES - GROUP):
            frame = start + lax.broadcasted_iota(jnp.int32, (GROUP, LANES), 0)
            span = jnp.minimum(frame + width, NFRAMES - 1) - jnp.maximum(frame - width, 0) + 1
            put(start // GROUP, window(start) / span.astype(jnp.float32))
        lax.fori_loop(1, NFRAMES // GROUP - 1, inside, 0, unroll=3)
        launch(sib_copy(chunk))
        if chunk:
            accumulate(chunk - 1)

    chip_label = label[pl.ds(pl.multiple_of(x * (CHIP_PIX // LANES), 8), CHIP_PIX // LANES), :]
    chip_valid = valid[pl.ds(pl.multiple_of(x * (CHIP_PIX // LANES), 8), CHIP_PIX // LANES), :]
    held = jnp.sum(jnp.where((chip_label == c) & (chip_valid == 1), 1.0, 0.0), axis=(0, 1), keepdims=True)

    accumulate(CHUNKS - 1)
    sums_t[...] = jnp.transpose(sums_ref[...] / jnp.maximum(held, 1.0))
    stat1[a1, 0:1, :] = sums_ref[0:1, :]
    stat1[a1, 1:2, :] = jnp.broadcast_to(held, (1, NFRAMES))

    def stat1_copy(k):
        to = (a1 + k) % 4
        return remote(stat1.at[a1], stat1.at[a1], s1_send.at[k], s1_recv.at[a1], first_peer(to))

    for k in range(1, 4):
        launch(stat1_copy(k))

    def lane(a, half):
        return pl.ds(pl.multiple_of(((a1 + a) % 4 * 2 + half) * LANES, LANES), LANES)

    def other_half(a, half):
        high = a // 2
        return (1 - half) * high + half * (1 - high)

    def g_copy(k, sub):
        to = (a1 + k) % 4
        rows = pl.ds(pl.multiple_of(sub * SUB_ROWS, SUB_ROWS), SUB_ROWS)
        return remote(
            gsend.at[to, rows, :], grecv.at[a1, rows, :], g_send.at[k, sub], g_recv.at[a1, sub], first_peer(to)
        )

    for k in (1, 2, 3, 0):
        to = (a1 + k) % 4
        for half in range(2):
            start = pl.multiple_of(to * CLASS_ROWS + half * LANES, LANES)
            column = jnp.broadcast_to(sums_t[pl.ds(start, LANES), 0:1], (LANES, LANES))
            rows = slice(half * LANES, (half + 1) * LANES)
            held_lanes = [lane(k, 0), lane(k, 1), lane(k + 1, 0), lane(k + 1, 1), lane(k + 2, other_half(to, half))]
            for n, cols in enumerate(held_lanes):
                centred = gram[pl.ds(start, LANES), cols] - column * sums_ref[0:1, cols]
                if k:
                    gsend[to, rows, n * LANES : (n + 1) * LANES] = centred.astype(jnp.bfloat16)
                else:
                    gown[rows, n * LANES : (n + 1) * LANES] = centred

    for j in (1, 2, 3, 0):
        for k in (2, 1, 3):
            launch(g_copy(k, (a2 + j) % 4))
    for k in range(1, 4):
        source = (a1 + k) % 4
        remote(stat1.at[source], stat1.at[source], s1_send.at[k], s1_recv.at[source], first_peer(source)).wait_recv()
    statg2[...] = stat1[0] + stat1[1] + stat1[2] + stat1[3]
    stat2[a2] = statg2[...]

    def stat2_copy(k):
        return remote(statg2, stat2.at[a2], s2_send.at[k], s2_recv.at[a2], second_peer((a2 + k) % 4))

    for k in range(1, 4):
        launch(stat2_copy(k))
    def stat3_copy(k):
        return remote(statg3, stat3.at[z], s3_send.at[k], s3_recv.at[z], z_peer((z + k) % NZ))

    def between(stat, members):
        group = stat[0]
        for k in range(1, members):
            group = group + stat[k]
        mean = group[0:1, :] / jnp.maximum(group[1:2, :], 1.0)
        for k in range(members):
            spread[k : k + 1, :] = stat[k, 0:1, :] / jnp.maximum(stat[k, 1:2, :], 1.0) - mean
        spread_t[...] = jnp.transpose(spread[...])
        for k in range(members):
            spread[k : k + 1, :] = spread[k : k + 1, :] * stat[k, 1:2, :]
        return group

    def outer(rows, cols):
        return jnp.dot(rows, spread[:, cols], preferred_element_type=jnp.float32, precision=lax.Precision.HIGHEST)

    spread[...] = jnp.zeros_like(spread)
    between(stat1, 4)
    own_start = pl.multiple_of(a1 * CLASS_ROWS, CLASS_ROWS)
    for n in range(4):
        gown[:, n * LANES : (n + 1) * LANES] += outer(spread_t[pl.ds(own_start, CLASS_ROWS), :], lane(n // 2, n % 2))
    for half in range(2):
        gown[half * LANES : (half + 1) * LANES, 4 * LANES :] += outer(
            spread_t[pl.ds(own_start + half * LANES, LANES), :], lane(2, other_half(a1, half))
        )

    def h_copy(k):
        to = (a2 + k) % 4
        return remote(hsend.at[to], hrecv.at[a2], h_send.at[k], h_recv.at[a2], second_peer(to))

    for j in (1, 2, 3, 0):
        sub = (a2 + j) % 4
        rows = pl.ds(pl.multiple_of(sub * SUB_ROWS, SUB_ROWS), SUB_ROWS)
        if j == 0:
            for k in range(1, 4):
                source = (a2 + k) % 4
                remote(statg2, stat2.at[source], s2_send.at[k], s2_recv.at[source], second_peer(source)).wait_recv()
            statg3[...] = stat2[0] + stat2[1] + stat2[2] + stat2[3]
            stat3[z] = statg3[...]
            for k in (4, 3, 5, 2, 6, 1, 7):
                launch(stat3_copy(k))
        for k in range(1, 4):
            source = (a1 + k) % 4
            remote(
                gsend.at[source, rows, :], grecv.at[source, rows, :], g_send.at[k, sub], g_recv.at[source, sub],
                first_peer(source),
            ).wait_recv()
        value = gown[rows, :]
        for k in range(1, 4):
            value = value + grecv[(a1 + k) % 4, rows, :].astype(jnp.float32)
        gown[rows, :] = value
        if j:
            hsend[sub] = value.astype(jnp.bfloat16)
            launch(h_copy(j))

    def mirror_copy(n):
        return remote(
            m1_out.at[n], m1_in.at[a2], m1_send.at[n], m1_recv.at[a2], peer((a1 + 1) % 4, n)
        )

    def half_copy(n):
        return remote(
            m2_out.at[n], m2_in.at[a2], m2_send.at[n], m2_recv.at[a2], peer((a1 + 2) % 4, n)
        )

    for half in range(2):
        mirror = jnp.transpose(gown[half * LANES : (half + 1) * LANES, 4 * LANES :]).astype(jnp.bfloat16)
        for n in range(2):
            m2_out[other_half(a1, half) * 2 + n] = mirror[n * SUB_ROWS : (n + 1) * SUB_ROWS, :]
    for n in range(4):
        launch(half_copy(n))

    mirror = jnp.transpose(gown[:, 2 * LANES : 4 * LANES]).astype(jnp.bfloat16)
    for n in range(4):
        m1_out[n] = mirror[n * SUB_ROWS : (n + 1) * SUB_ROWS, :]
        launch(mirror_copy(n))
    between(stat2, 4)
    row_start = pl.multiple_of(a1 * CLASS_ROWS + a2 * SUB_ROWS, SUB_ROWS)
    column = spread_t[pl.ds(row_start, SUB_ROWS), :]
    value = column[:, 0:1] * spread[0:1, :]
    for k in range(1, 4):
        value = value + column[:, k : k + 1] * spread[k : k + 1, :]
    hown[...] = value
    for k in range(1, 4):
        source = (a2 + k) % 4
        remote(hsend.at[source], hrecv.at[source], h_send.at[k], h_recv.at[source], second_peer(source)).wait_recv()
    value = gown[pl.ds(pl.multiple_of(a2 * SUB_ROWS, SUB_ROWS), SUB_ROWS), :]
    for k in range(1, 4):
        value = value + hrecv[(a2 + k) % 4].astype(jnp.float32)
    own_half = other_half(a1, a2 // 2)
    for n, cols in enumerate((lane(0, 0), lane(0, 1), lane(1, 0), lane(1, 1), lane(2, own_half))):
        hown[:, cols] += value[:, n * LANES : (n + 1) * LANES]
    for n in range(4):
        remote(m1_out.at[n], m1_in.at[n], m1_send.at[n], m1_recv.at[n], peer((a1 + 3) % 4, n)).wait_recv()
    value = m1_in[0].astype(jnp.float32)
    for n in range(1, 4):
        value = value + m1_in[n].astype(jnp.float32)
    hown[:, lane(3, 0)] += value[:, 0:LANES]
    hown[:, lane(3, 1)] += value[:, LANES:]
    for n in range(4):
        remote(m2_out.at[n], m2_in.at[n], m2_send.at[n], m2_recv.at[n], peer((a1 + 2) % 4, n)).wait_recv()
    value = m2_in[0].astype(jnp.float32)
    for n in range(1, 4):
        value = value + m2_in[n].astype(jnp.float32)
    hown[:, lane(2, 1 - own_half)] += value
    own_rows = GROUP // NZ

    for other_z in range(NZ):
        for core in range(CORES):
            start = core * GROUP + other_z * own_rows
            tsend[other_z, core] = hown[start : start + own_rows, :].astype(jnp.bfloat16)

    def t_copy(k, flip):
        to, core = (z + k) % NZ, (c + flip) % CORES
        return remote(
            tsend.at[to, core], trecv.at[c, z], t_send.at[k, flip], t_recv.at[c, z], (x * CORES + core, y * NZ + to)
        )

    for flip in (1, 0):
        for k in (4, 3, 5, 2, 6, 1, 7):
            launch(t_copy(k, flip))
    launch(t_copy(0, 1))
    trecv[c, z] = tsend[z, c]
    for k in range(1, NZ):
        source = (z + k) % NZ
        remote(statg3, stat3.at[source], s3_send.at[k], s3_recv.at[source], z_peer(source)).wait_recv()
    counts = between(stat3, NZ)[1:2, :]
    halves = [
        spread_t[pl.ds(pl.multiple_of(row_start + core * GROUP + z // 2 * 8, 8), 8), :] for core in range(CORES)
    ]
    even = z % 2 == 0
    term = outer(
        jnp.concatenate([jnp.where(even, half[0:own_rows], half[own_rows : 2 * own_rows]) for half in halves], axis=0),
        slice(None),
    )
    low, high = term[0:own_rows, :], term[own_rows : 2 * own_rows, :]
    fsend[...] = jnp.broadcast_to(counts, (2 * own_rows, NFRAMES))
    fsend[0:own_rows, :] = jnp.where(c == 0, high, low)
    last = remote(fsend, frecv, f_send, f_recv, sibling)
    launch(last)

    place = lax.broadcasted_iota(jnp.int32, (own_rows, LANES), 1) // GROUP

    def give(cycle, flip, value, count):
        for k in range(NZ):
            source, core = (z + k) % NZ, (c + flip) % CORES
            if k or flip:
                remote(
                    tsend.at[source, core], trecv.at[cycle, source], t_send.at[k, flip], t_recv.at[cycle, source],
                    (x * CORES + core, y * NZ + source),
                ).wait_recv()
            value = value + trecv[cycle, source].astype(jnp.float32)
        permuted[flip] = value / count
        for row_x in range(4):
            for core in range(CORES):
                piece_of = None
                for row_y in range(4):
                    first = cycle * row_x + (1 - cycle) * row_y
                    second = cycle * row_y + (1 - cycle) * row_x
                    block = pl.ds(pl.multiple_of((first * 2 + second // 2) * LANES, LANES), LANES)
                    shift = (row_y * GROUP + LANES - (second % 2 * 2 + core) * GROUP) % LANES
                    moved = pltpu.roll(permuted[flip, :, block], shift, 1)
                    piece_of = moved if piece_of is None else jnp.where(place == row_y, moved, piece_of)
                block = (row_x * CORES + core) * LANES
                out[cycle, :, block : block + LANES] = piece_of

    give(c, 0, jnp.where(c == 0, low, high), counts)
    last.wait_recv()
    give(1 - c, 1, frecv[0:own_rows, :], frecv[own_rows : own_rows + 1, :])

    finish()


def shards(frames, dead_time, band_width, cycle_label, valid):
    rows = NPIX_GROUP // LANES
    flat = [a.reshape(rows, LANES) for a in (dead_time, band_width, cycle_label, valid)]
    own_rows = GROUP // NZ
    dma = pltpu.SemaphoreType.DMA
    f32, bf16 = jnp.float32, jnp.bfloat16
    any_space = pl.BlockSpec(memory_space=pltpu.HBM)
    vmem = pltpu.VMEM
    out = pl.pallas_call(
        kernel,
        out_shape=jax.ShapeDtypeStruct((CYCLES, own_rows, NFRAMES), f32),
        in_specs=[any_space] * 5,
        out_specs=pl.BlockSpec(memory_space=pltpu.VMEM),
        scratch_shapes=[
            vmem((rows, LANES), f32),
            vmem((rows, LANES), jnp.int32),
            vmem((rows, LANES), jnp.int32),
            vmem((rows, LANES), jnp.int32),
            vmem((CHUNKS, NDEV_FRAME, OWN_FRAMES, LANES), bf16),
            vmem((PAD + NFRAMES + PAD, LANES), f32),
            vmem((NFRAMES, CHIP_PIX), bf16),
            vmem((CHUNKS, NFRAMES, LANES), bf16),
            vmem((NFRAMES, NFRAMES), f32),
            vmem((8, NFRAMES), f32),
            vmem((NFRAMES, 8), f32),
            vmem((4, CLASS_ROWS, HELD), bf16),
            vmem((4, CLASS_ROWS, HELD), bf16),
            vmem((CLASS_ROWS, HELD), f32),
            vmem((4, SUB_ROWS, HELD), bf16),
            vmem((4, SUB_ROWS, HELD), bf16),
            vmem((SUB_ROWS, NFRAMES), f32),
            vmem((NZ, CORES, own_rows, NFRAMES), bf16),
            vmem((CORES, NZ, own_rows, NFRAMES), bf16),
            vmem((4, 2, NFRAMES), f32),
            vmem((4, 2, NFRAMES), f32),
            vmem((NZ, 2, NFRAMES), f32),
            vmem((2, NFRAMES), f32),
            vmem((2, NFRAMES), f32),
            vmem((8, NFRAMES), f32),
            vmem((NFRAMES, 8), f32),
            vmem((2 * own_rows, NFRAMES), f32),
            vmem((2 * own_rows, NFRAMES), f32),
            vmem((4, SUB_ROWS, 2 * LANES), bf16), vmem((4, SUB_ROWS, 2 * LANES), bf16),
            vmem((4, SUB_ROWS, LANES), bf16), vmem((4, SUB_ROWS, LANES), bf16),
            vmem((CORES, own_rows, NFRAMES), f32),
            dma((4,)),
            dma((CHUNKS,)),
            dma((CHUNKS, NDEV_FRAME)), dma((CHUNKS, NDEV_FRAME)),
            dma((CHUNKS,)), dma((CHUNKS,)),
            dma((4,)), dma((4,)),
            dma((4,)), dma((4,)),
            dma((NZ,)), dma((NZ,)),
            dma((4, 4)), dma((4, 4)),
            dma((4,)), dma((4,)),
            dma((NZ, CORES)), dma((CORES, NZ)),
            dma, dma,
            dma((4,)), dma((4,)),
            dma((4,)), dma((4,)),
        ],
        compiler_params=pltpu.CompilerParams(
            collective_id=0, has_side_effects=True, vmem_limit_bytes=60 * 2**20
        ),
    )(frames, *flat)
    return jnp.transpose(out, (1, 0, 2))


def solution(mesh):
    in_specs = (P("frame", "pixel"), P("pixel"), P("pixel"), P("pixel"), P("pixel"))
    out_specs = P(("frame", "pixel"), None, None)
    return jax.shard_map(shards, mesh=mesh, in_specs=in_specs, out_specs=out_specs, check_vma=False)
```
